128 devices in a mesh: slab: 4 (over z), mode: 32 (over x, y, core).
Axes of the slice: x: 4, y: 4, z: 4, core: 2. Of those that a mesh axis runs over, the one named last changes fastest.
Arguments:
- field: bfloat16 [1024, 8, 32, 256], P('mode', 'slab'), may hold values from -6 to 6
- coefficient: float32 [9, 8, 32, 256], P(None, 'slab'), may hold values from 0.1 to 1
- slot_mode: int32 [1024], replicated, may hold values from 0 to 495, as said below
- couplings: int32 [2640, 4], replicated, may hold values from -8 to 494, as said below
Outputs:
- images: float32 [1024, 8, 32, 256], P('mode', 'slab')
The draws below stay inside these ranges and needn't reach their ends.
Inputs may be any that keep to these rules, and one draw needn't show every extreme that they name: `slot_mode`: slot s belongs to group s // 32. A value 495 marks an empty slot; every mode stands in exactly one slot; a group's occupied slots come first in it; every group holds at least one mode and one group fills all 32 of its slots. `couplings`: columns are mode k, mode i (k != i), term t from 1 to 8, and a nonzero weight; every row (k, i, t, w) stands beside its mirror (i, k, t, w).
All inputs are finite; a program needn't handle non-finite values.
Results may differ from the reference program's by a relative error of at most 0.0003.
Values may be sent and summed in bfloat16 or wider, within the bound.
A program may use at most 192 MiB of HBM per device.

```python
import math
import jax
import jax.numpy as jnp
from jax import lax

MODES = 495
VARS = 8
PAIRS = 165
NY = 32
NZ = 256
TERMS = 9
GROUPS = 32
SLOTS = 32
SLOTS_ALL = 1024
NX = 8


def draw_slot_mode(key, part):
    remaining = MODES - SLOTS
    other_groups = GROUPS - 1
    base_size = remaining // other_groups
    surplus = remaining % other_groups
    spread_most = max(min(base_size - 1, SLOTS - base_size - 2), 0)
    pair_count = other_groups // 2
    shifts = jax.random.randint(jax.random.fold_in(key, 11), (pair_count,), 0, spread_most + 1).astype(jnp.int32)
    paired = jnp.stack([shifts, -shifts], 1).reshape(-1)
    shift_all = jnp.concatenate([paired, jnp.zeros((other_groups - 2 * pair_count,), jnp.int32)])
    other_sizes = base_size + (jnp.arange(other_groups) < surplus).astype(jnp.int32) + shift_all
    sizes_all = jnp.concatenate([jnp.full((1,), SLOTS, jnp.int32), other_sizes.astype(jnp.int32)])
    group_order = jax.random.permutation(jax.random.fold_in(key, 12), GROUPS)
    group_sizes = sizes_all[group_order]
    modes_perm = jax.random.permutation(jax.random.fold_in(key, 13), MODES).astype(jnp.int32)
    offsets = jnp.cumsum(group_sizes) - group_sizes
    within = jnp.arange(SLOTS, dtype=jnp.int32)[None, :]
    live_slots = within < group_sizes[:, None]
    mode_index = jnp.minimum(offsets[:, None] + within, MODES - 1)
    return jnp.where(live_slots, modes_perm[mode_index], MODES).reshape(-1).astype(jnp.int32)


def draw_couplings(key, part):
    entries = VARS * PAIRS
    leader = jax.random.randint(jax.random.fold_in(key, 21), (entries,), 0, MODES)
    partner = (leader + jax.random.randint(jax.random.fold_in(key, 22), (entries,), 1, MODES)) % MODES
    term_ids = jnp.repeat(jnp.arange(1, VARS + 1, dtype=jnp.int32), PAIRS)
    magnitude = jax.random.randint(jax.random.fold_in(key, 23), (entries,), 1, 9)
    signed = 2 * jax.random.randint(jax.random.fold_in(key, 24), (entries,), 0, 2) - 1
    weight = magnitude * signed
    forward = jnp.stack([leader, partner, term_ids, weight], 1)
    mirror = jnp.stack([partner, leader, term_ids, weight], 1)
    return jnp.stack([forward, mirror], 1).reshape(2 * entries, 4).astype(jnp.int32)


def level_of(stream_key, shape, shards, low, largest):
    loudness, own = 1.0, jax.random.fold_in(stream_key, 6)
    for axis_at, shards_of in shards:
        heights = jnp.exp(jax.random.uniform(jax.random.fold_in(own, axis_at), (shards_of,), jnp.float32, low / len(shards), largest / len(shards)))
        loudness = loudness * jnp.repeat(heights, shape[axis_at] // shards_of).reshape([-1 if axis == axis_at else 1 for axis in range(len(shape))])
    return loudness


def gaussian(key, shape, scale, limit, split=(), kind=jnp.bfloat16):
    drawn = scale * jax.random.normal(key, shape, jnp.float32)
    if split:
        drawn = drawn * level_of(key, shape, split, -0.22, 0.18)
    return jnp.clip(drawn, -limit, limit).astype(kind)


def setup_inputs(seed: int = 0) -> dict:
    key_of = jax.random.split(jax.random.key(seed), 5)
    return {
        "field": gaussian(key_of[0], (SLOTS_ALL, NX, NY, NZ), 1.0, 6.0, ((0, 32), (1, 4))),
        "coefficient": jnp.clip(jnp.exp(math.log(1.0) - 2.3025851 * jax.random.uniform(key_of[1], (TERMS, NX, NY, NZ), jnp.float32) ** level_of(key_of[1], (TERMS, NX, NY, NZ), ((1, 4),), -0.2, 0.2)), 0.1, 1.0),
        "slot_mode": draw_slot_mode(jax.random.fold_in(key_of[4], 71), 0),
        "couplings": draw_couplings(jax.random.fold_in(key_of[4], 71), 0),
    }


def planes_image(val_planes, coef_planes):
    center_coef = coef_planes[1:-1]
    center_vals = val_planes[:, 1:-1]
    summed = 0.5 * (center_coef + coef_planes[2:]) * (center_vals - val_planes[:, 2:])
    summed = summed + 0.5 * (center_coef + coef_planes[:-2]) * (center_vals - val_planes[:, :-2])
    padded_coef = jnp.pad(center_coef, ((0, 0), (1, 1), (0, 0)))
    padded_vals = jnp.pad(center_vals, ((0, 0), (0, 0), (1, 1), (0, 0)))
    summed = summed + 0.5 * (center_coef + padded_coef[:, 2:]) * (center_vals - padded_vals[:, :, 2:])
    summed = summed + 0.5 * (center_coef + padded_coef[:, :-2]) * (center_vals - padded_vals[:, :, :-2])
    padded_coef = jnp.pad(center_coef, ((0, 0), (0, 0), (1, 1)))
    padded_vals = jnp.pad(center_vals, ((0, 0), (0, 0), (0, 0), (1, 1)))
    summed = summed + 0.5 * (center_coef + padded_coef[:, :, 2:]) * (center_vals - padded_vals[:, :, :, 2:])
    summed = summed + 0.5 * (center_coef + padded_coef[:, :, :-2]) * (center_vals - padded_vals[:, :, :, :-2])
    return summed


def coupling_matrix(couplings, extent, positions):
    target = positions[couplings[:, 0]]
    partner = positions[couplings[:, 1]]
    term_ids = couplings[:, 2]
    weight = couplings[:, 3].astype(jnp.float32) * 0.125
    galerkin = jnp.zeros((extent, TERMS * extent), jnp.float32)
    galerkin = galerkin.at[target, term_ids * extent + partner].add(weight)
    galerkin = galerkin.at[positions, positions].add(1.0)
    return galerkin


def reference(field, coefficient, slot_mode, couplings):
    all_slots = jnp.arange(SLOTS_ALL, dtype=jnp.int32)
    slot_of_mode = jnp.zeros((MODES + 1,), jnp.int32).at[slot_mode].set(all_slots)[:MODES]
    modes_field = field[slot_of_mode].astype(jnp.float32)
    galerkin = coupling_matrix(couplings, MODES, jnp.arange(MODES, dtype=jnp.int32))
    cell_count = NX * NY * NZ
    coef_planes = jnp.pad(coefficient, ((0, 0), (1, 1), (0, 0), (0, 0)))
    val_planes = jnp.pad(modes_field, ((0, 0), (1, 1), (0, 0), (0, 0)))
    summed = jnp.zeros((MODES, cell_count), jnp.float32)
    for term_index in range(TERMS):
        stiff = planes_image(val_planes, coef_planes[term_index]).reshape(MODES, cell_count)
        block = galerkin[:, term_index * MODES:(term_index + 1) * MODES]
        summed = summed + jnp.dot(block, stiff, precision=lax.Precision.HIGHEST, preferred_element_type=jnp.float32)
    padded = jnp.concatenate([summed, jnp.zeros((1, cell_count), jnp.float32)])
    return padded[slot_mode].reshape(SLOTS_ALL, NX, NY, NZ)
```

```python
import jax
import jax.numpy as jnp
from jax import lax
from jax.experimental import pallas as pl
from jax.experimental.pallas import tpu as pltpu
from jax.sharding import PartitionSpec as P

MODES = 495
HELD = 512
TERMS = 9
ROWS = 4 * HELD
LANES = 8
MESH = pl.DeviceIdType.MESH
VMEM = pl.BlockSpec(memory_space=pltpu.VMEM)
SMEM = pl.BlockSpec(memory_space=pltpu.SMEM)
LIMIT = 60 * 1024 * 1024


def shape_of(shape, dtype):
    return jax.ShapeDtypeStruct(shape, dtype)


def greet(count):
    slab, me = lax.axis_index("slab"), lax.axis_index("mode")
    barrier = pltpu.get_barrier_semaphore()

    def tell(step, carry):
        peer = lax.rem(me + step, count)
        pl.semaphore_signal(barrier, inc=1, device_id=(slab, peer), device_id_type=MESH)
        return carry

    lax.fori_loop(1, count, tell, 0)
    pl.semaphore_wait(barrier, count - 1)


def gather_kernel(count, inverse, blocks, held, planes, raw, wide, wide_planes, own_sem, send_sem, recv_sem):
    slab, me = lax.axis_index("slab"), lax.axis_index("mode")
    slots = blocks.shape[1]
    greet(count)

    def copy_to(step):
        peer = lax.rem(me + step, count)
        return pltpu.make_async_remote_copy(
            src_ref=blocks.at[peer],
            dst_ref=raw.at[pl.ds(me * slots, slots)],
            send_sem=send_sem.at[step],
            recv_sem=recv_sem.at[step],
            device_id=(slab, peer),
            device_id_type=MESH,
        )

    def start(step, carry):
        copy_to(step).start()
        return carry

    lax.fori_loop(1, count, start, 0)
    own = pltpu.make_async_copy(blocks.at[me], raw.at[pl.ds(me * slots, slots)], own_sem)
    own.start()
    own.wait()

    def finish(step, carry):
        copy_to(step).wait()
        return carry

    lax.fori_loop(1, count, finish, 0)

    def pick(step, carry):
        for part in range(8):
            mode = step * 8 + part
            value = raw[inverse[mode]].astype(jnp.float32)
            wide[pl.ds(pl.multiple_of(4 * mode, 4), 4), :] = value
            wide_planes[0, pl.ds(pl.multiple_of(2 * mode, 2), 2), :] = value[0:2]
            wide_planes[1, pl.ds(pl.multiple_of(2 * mode, 2), 2), :] = value[2:4]
        return carry

    lax.fori_loop(0, HELD // 8, pick, 0)

    def narrow(step, carry):
        at = pl.ds(pl.multiple_of(step * 64, 64), 64)
        held[at, :] = wide[at, :].astype(jnp.bfloat16)
        return carry

    lax.fori_loop(0, ROWS // 64, narrow, 0)

    def narrow_planes(step, carry):
        at = pl.ds(pl.multiple_of(step * 64, 64), 64)
        planes[0, at, :] = wide_planes[0, at, :].astype(jnp.bfloat16)
        planes[1, at, :] = wide_planes[1, at, :].astype(jnp.bfloat16)
        return carry

    lax.fori_loop(0, ROWS // 128, narrow_planes, 0)


def halo_kernel(slabs, count, held, planes, coef, row_low, row_high, plane_low, plane_high, coef_low, coef_high, send_sem, recv_sem):
    slab, me = lax.axis_index("slab"), lax.axis_index("mode")
    above = (slab, lax.rem(me + 1, count))
    below = (slab, lax.rem(me + count - 1, count))
    right = (lax.rem(slab + 1, slabs), me)
    left = (lax.rem(slab + slabs - 1, slabs), me)
    barrier = pltpu.get_barrier_semaphore()
    for peer in (above, below, right, left):
        pl.semaphore_signal(barrier, inc=1, device_id=peer, device_id_type=MESH)
    pl.semaphore_wait(barrier, 4)
    copies = []
    for place, (source, target, peer) in enumerate(
        (
            (held, row_low, above),
            (held, row_high, below),
            (planes.at[1], plane_low, right),
            (planes.at[0], plane_high, left),
            (coef.at[1], coef_low, right),
            (coef.at[1], coef_high, left),
        )
    ):
        copy = pltpu.make_async_remote_copy(
            src_ref=source,
            dst_ref=target,
            send_sem=send_sem.at[place],
            recv_sem=recv_sem.at[place],
            device_id=peer,
            device_id_type=MESH,
        )
        copy.start()
        copies.append(copy)
    for copy in copies:
        copy.wait()


def neighbours(centre, plane, sub, lane):
    front = lax.rem(sub, 4) < 2
    second = lax.rem(sub, 2) == 1
    zero = jnp.zeros_like(centre)
    plane_low = jnp.where(front, plane, pltpu.roll(centre, 2, 0))
    plane_high = jnp.where(front, pltpu.roll(centre, 6, 0), plane)
    low = pltpu.roll(centre, 1, 1)
    high = pltpu.roll(centre, 127, 1)
    column_low = jnp.where(lane == 0, jnp.where(second, pltpu.roll(low, 1, 0), zero), low)
    column_high = jnp.where(lane == 127, jnp.where(second, zero, pltpu.roll(high, 7, 0)), high)
    return plane_low, plane_high, column_low, column_high


def apply_kernel(slabs, count, address, weight, slot_mode, held, row_low, row_high, plane_low, plane_high, coef, coef_low, coef_high, coded, scales, faces, plane_rows, image, *sums_and_picked):
    sums, picked = sums_and_picked[:LANES], sums_and_picked[LANES]
    slab, me = lax.axis_index("slab"), lax.axis_index("mode")
    sub = lax.broadcasted_iota(jnp.int32, (8, 128), 0)
    lane = lax.broadcasted_iota(jnp.int32, (8, 128), 1)
    front = lax.rem(sub, 4) < 2
    has_left = (slab > 0).astype(jnp.float32)
    has_right = (slab < slabs - 1).astype(jnp.float32)
    mask_plane = jnp.where(front, has_left, has_right)
    mask_low = (me > 0).astype(jnp.float32)
    mask_high = (me < count - 1).astype(jnp.float32)

    for term in range(TERMS):
        own = coef[1, term]
        outer = jnp.where(front, pltpu.roll(coef_low[term], 6, 0), pltpu.roll(coef_high[term], 2, 0)) * mask_plane
        around = neighbours(own, outer, sub, lane)
        around = around + (coef[0, term] * mask_low, coef[2, term] * mask_high)
        for place, other in enumerate(around):
            faces[6 * term + place] = 0.5 * (own + other)

    def interleave(step, carry):
        at = pl.ds(pl.multiple_of(step * 16, 16), 16)
        low = plane_low[at, :].astype(jnp.float32)
        high = plane_high[at, :].astype(jnp.float32)
        for part in range(8):
            base = pl.multiple_of(step * 32 + 4 * part, 4)
            plane_rows[pl.ds(base, 2), :] = low[2 * part : 2 * part + 2]
            plane_rows[pl.ds(base + 2, 2), :] = high[2 * part : 2 * part + 2]
        return carry

    lax.fori_loop(0, ROWS // 32, interleave, 0)

    def stencil(step, carry):
        at = pl.ds(pl.multiple_of(step * 16, 16), 16)
        centre = held[at, :].astype(jnp.float32)
        low = row_low[at, :].astype(jnp.float32)
        high = row_high[at, :].astype(jnp.float32)
        halves = []
        for half in range(2):
            part = slice(8 * half, 8 * half + 8)
            base = pl.multiple_of(step * 16 + 8 * half, 8)
            own = centre[part]
            outer = plane_rows[pl.ds(base, 8), :] * mask_plane
            around = neighbours(own, outer, sub, lane)
            around = around + (low[part] * mask_low, high[part] * mask_high)
            halves.append((base, [own - other for other in around]))
        for term in range(TERMS):
            face = [faces[6 * term + place] for place in range(6)]
            for base, drops in halves:
                total = face[0] * drops[0]
                for place in range(1, 6):
                    total = total + face[place] * drops[place]
                if term == 0:
                    sums[0][pl.ds(base, 8), :] = total
                else:
                    image[pl.ds(pl.multiple_of((term - 1) * ROWS + base, 8), 8), :] = total
        return carry

    lax.fori_loop(0, ROWS // 16, stencil, 0)

    def clear(step, carry):
        at = pl.ds(pl.multiple_of(step * 32, 32), 32)
        for total in sums[1:]:
            total[at, :] = jnp.zeros((32, 128), jnp.float32)
        return carry

    lax.fori_loop(0, ROWS // 32, clear, 0)

    def couple(step, carry):
        for part in range(LANES):
            place = step * LANES + part
            both = address[place]
            source = pl.ds(pl.multiple_of(lax.bitwise_and(both, 0xFFFF), 4), 4)
            target = pl.ds(pl.multiple_of(lax.shift_right_logical(both, 16), 4), 4)
            sums[part][target, :] = sums[part][target, :] + weight[place] * image[source, :]
        return carry

    lax.fori_loop(0, address.shape[0] // LANES, couple, 0)

    def join(step, carry):
        at = pl.ds(pl.multiple_of(step * 16, 16), 16)
        total = sums[0][at, :]
        for other in sums[1:]:
            total = total + other[at, :]
        sums[0][at, :] = total
        return carry

    lax.fori_loop(0, ROWS // 16, join, 0)
    sums[0][4 * MODES : 4 * MODES + 4, :] = jnp.zeros((4, 128), jnp.float32)

    def pick(step, carry):
        for part in range(8):
            slot = step * 8 + part
            source = pl.ds(pl.multiple_of(4 * slot_mode[slot], 4), 4)
            picked[pl.ds(pl.multiple_of(4 * slot, 4), 4), :] = sums[0][source, :]
        return carry

    lax.fori_loop(0, slot_mode.shape[0] // 8, pick, 0)

    sub16 = lax.broadcasted_iota(jnp.int32, (16, 128), 0)
    lane16 = lax.broadcasted_iota(jnp.int32, (16, 128), 1)

    def encode(group, carry):
        row = jnp.zeros((1, 128), jnp.float32)
        for part in range(8):
            at = pl.ds(pl.multiple_of(group * 128 + part * 16, 16), 16)
            value = picked[at, :]
            largest = jnp.max(jnp.abs(value), axis=1, keepdims=True)
            factor = jnp.where(largest > 0, 1.0 / jnp.where(largest > 0, largest, 1.0), 0.0)
            code = jnp.round((value * factor) * 32767.0).astype(jnp.int32)
            coded[at, :] = code.astype(jnp.int16)
            spread = jnp.where(lane16 == sub16 + 16 * part, largest * (1.0 / 32767.0), 0.0)
            row = row + jnp.sum(spread, axis=0, keepdims=True)
        scales[group] = row
        return carry

    lax.fori_loop(0, count, encode, 0)


def return_kernel(count, coded, scales, got, got_scales, own_sem, send_sem, recv_sem):
    slab, me = lax.axis_index("slab"), lax.axis_index("mode")
    greet(count)

    def copies_to(step):
        peer = lax.rem(me + step, count)
        return [
            pltpu.make_async_remote_copy(
                src_ref=source.at[peer],
                dst_ref=target.at[me],
                send_sem=send_sem.at[place, step],
                recv_sem=recv_sem.at[place, step],
                device_id=(slab, peer),
                device_id_type=MESH,
            )
            for place, (source, target) in enumerate(((coded, got), (scales, got_scales)))
        ]

    def start(step, carry):
        for copy in copies_to(step):
            copy.start()
        return carry

    lax.fori_loop(1, count, start, 0)
    own = [
        pltpu.make_async_copy(coded.at[me], got.at[me], own_sem.at[0]),
        pltpu.make_async_copy(scales.at[me], got_scales.at[me], own_sem.at[1]),
    ]
    for copy in own:
        copy.start()
    for copy in own:
        copy.wait()

    def finish(step, carry):
        for copy in copies_to(step):
            copy.wait()
        return carry

    lax.fori_loop(1, count, finish, 0)


def decode_kernel(got, got_scales, out, wide, scale):
    block = pl.program_id(0)
    count, rows = got.shape[0], got.shape[1]
    for source in range(count):
        scale[source : source + 1, :] = got_scales[source]

    def widen(source, carry):
        at = pl.ds(pl.multiple_of(source * rows, rows), rows)
        wide[at, :] = got[source].astype(jnp.int32).astype(jnp.float32)
        return carry

    lax.fori_loop(0, count, widen, 0)
    factors = pltpu.roll(scale[...], lax.rem(128 - block * rows, 128), 1)
    for place in range(rows):
        slot, plane, half = place // 4, (place // 2) % 2, place % 2
        value = wide[pl.ds(place, count, stride=rows), :]
        out[slot, plane, :, 128 * half : 128 * half + 128] = value * factors[:, place : place + 1]


def on_device(field, coefficient, slot_mode, couplings):
    slabs, count = lax.axis_size("slab"), lax.axis_size("mode")
    row = lax.axis_index("mode")
    slots, planes_here, rows_all, columns = field.shape
    f32, bf16, i16 = jnp.float32, jnp.bfloat16, jnp.int16
    dma = pltpu.SemaphoreType.DMA

    blocks = field.reshape(slots, planes_here, rows_all, 2, 128).transpose(2, 0, 1, 3, 4)
    blocks = blocks.reshape(rows_all, slots, 4, 128)
    mode_ids = jnp.arange(HELD, dtype=jnp.int32)
    slot_ids = jnp.arange(slots * count, dtype=jnp.int32)
    inverse = jnp.sum(jnp.where(slot_mode[None, :] == mode_ids[:, None], slot_ids[None, :], 0), axis=1)
    inverse = jnp.where(mode_ids < MODES, inverse, 0).astype(jnp.int32)
    near = jnp.stack([lax.dynamic_slice_in_dim(coefficient, row + shift, 1, 2) for shift in (-1, 0, 1)])
    near = near.reshape(3, TERMS, 4, 128)
    near = jnp.concatenate([near, near], axis=2)
    source = (couplings[:, 2] - 1) * ROWS + couplings[:, 1] * 4
    address = source + couplings[:, 0] * (4 << 16)
    weight = couplings[:, 3].astype(f32) * 0.125

    held, planes = pl.pallas_call(
        lambda *refs: gather_kernel(count, *refs),
        out_shape=(shape_of((ROWS, 128), bf16), shape_of((2, ROWS // 2, 128), bf16)),
        in_specs=[SMEM, VMEM],
        out_specs=(VMEM, VMEM),
        scratch_shapes=[
            pltpu.VMEM((slots * count, 4, 128), bf16),
            pltpu.VMEM((ROWS, 128), f32),
            pltpu.VMEM((2, ROWS // 2, 128), f32),
            dma,
            dma((count,)),
            dma((count,)),
        ],
        compiler_params=pltpu.CompilerParams(collective_id=0, has_side_effects=True, vmem_limit_bytes=LIMIT),
        name="gather",
    )(inverse, blocks)

    row_low, row_high, plane_low, plane_high, coef_low, coef_high = pl.pallas_call(
        lambda *refs: halo_kernel(slabs, count, *refs),
        out_shape=(
            shape_of((ROWS, 128), bf16),
            shape_of((ROWS, 128), bf16),
            shape_of((ROWS // 2, 128), bf16),
            shape_of((ROWS // 2, 128), bf16),
            shape_of((TERMS, 8, 128), f32),
            shape_of((TERMS, 8, 128), f32),
        ),
        in_specs=[VMEM] * 3,
        out_specs=(VMEM,) * 6,
        scratch_shapes=[dma((6,)), dma((6,))],
        compiler_params=pltpu.CompilerParams(collective_id=1, has_side_effects=True, vmem_limit_bytes=LIMIT),
        name="halo",
    )(held, planes, near)

    coded, scales = pl.pallas_call(
        lambda *refs: apply_kernel(slabs, count, *refs),
        out_shape=(shape_of((slots * count * 4, 128), i16), shape_of((count, 1, 128), f32)),
        in_specs=[SMEM] * 3 + [VMEM] * 8,
        out_specs=(VMEM, VMEM),
        scratch_shapes=[
            pltpu.VMEM((6 * TERMS, 8, 128), f32),
            pltpu.VMEM((ROWS, 128), f32),
            pltpu.VMEM(((TERMS - 1) * ROWS, 128), f32),
        ]
        + [pltpu.VMEM((ROWS, 128), f32)] * LANES
        + [pltpu.VMEM((slots * count * 4, 128), f32)],
        compiler_params=pltpu.CompilerParams(vmem_limit_bytes=LIMIT),
        name="apply",
    )(address, weight, slot_mode, held, row_low, row_high, plane_low, plane_high, near, coef_low, coef_high)

    got, got_scales = pl.pallas_call(
        lambda *refs: return_kernel(count, *refs),
        out_shape=(shape_of((count, slots * 4, 128), i16), shape_of((count, 1, 128), f32)),
        in_specs=[VMEM] * 2,
        out_specs=(VMEM, VMEM),
        scratch_shapes=[dma((2,)), dma((2, count)), dma((2, count))],
        compiler_params=pltpu.CompilerParams(collective_id=2, has_side_effects=True, vmem_limit_bytes=LIMIT),
        name="give",
    )(coded.reshape(count, slots * 4, 128), scales)

    step = 8
    return pl.pallas_call(
        decode_kernel,
        out_shape=shape_of((slots, planes_here, rows_all, columns), f32),
        grid=(slots // step,),
        in_specs=[
            pl.BlockSpec((count, 4 * step, 128), lambda i: (0, i, 0)),
            pl.BlockSpec((count, 1, 128), lambda i: (0, 0, 0)),
        ],
        out_specs=pl.BlockSpec((step, planes_here, rows_all, columns), lambda i: (i, 0, 0, 0)),
        scratch_shapes=[pltpu.VMEM((count * 4 * step, 128), f32), pltpu.VMEM((count, 128), f32)],
        compiler_params=pltpu.CompilerParams(vmem_limit_bytes=LIMIT),
        name="decode",
    )(got, got_scales)


def solution(mesh):
    in_specs = (P("mode", "slab", None, None), P(None, "slab", None, None), P(), P())
    return jax.shard_map(
        on_device,
        mesh=mesh,
        in_specs=in_specs,
        out_specs=P("mode", "slab", None, None),
        check_vma=False,
    )
```

```python
import jax
import jax.numpy as jnp
from jax import lax
from jax.experimental import pallas as pl
from jax.experimental.pallas import tpu as pltpu
from jax.sharding import PartitionSpec as P

MODES = 495
HELD = 512
TERMS = 9
ROWS = 4 * HELD
LANES = 4
UNROLL = 16
CHUNKS = 4
TOP = 32700.0
SIDE = 4
MESH = pl.DeviceIdType.MESH
VMEM = pl.BlockSpec(memory_space=pltpu.VMEM)
SMEM = pl.BlockSpec(memory_space=pltpu.SMEM)
MIB = 1024 * 1024


def far_first():
    offsets = [(x, y, core) for x in range(SIDE) for y in range(SIDE) for core in range(2)]
    hops = lambda offset: min(offset[0], SIDE - offset[0]) + min(offset[1], SIDE - offset[1])
    return sorted(offsets[1:], key=hops, reverse=True)


OFFSETS = far_first()


def shape_of(shape, dtype):
    return jax.ShapeDtypeStruct(shape, dtype)


def moved(me, offset, sign=1):
    x, y, core = me // (2 * SIDE), (me // 2) % SIDE, me % 2
    x = lax.rem(x + (sign * offset[0]) % SIDE, SIDE)
    y = lax.rem(y + (sign * offset[1]) % SIDE, SIDE)
    return (x * SIDE + y) * 2 + lax.rem(core + offset[2], 2)


def rows_at(start, size):
    return pl.ds(pl.multiple_of(start, size), size)


def gather_kernel(
    slabs, count, slot_mode, field, coefficient, couplings,
    held, row_low, row_high, plane_low, plane_high, near, coef_low, coef_high, address, weight,
    turned, blocks, raw, wide_raw, planes, wide, wide_planes, found, inverse,
    own_sem, send_sem, recv_sem, halo_send, halo_recv,
):
    slab, me = lax.axis_index("slab"), lax.axis_index("mode")
    slots = field.shape[0]
    above = (slab, lax.rem(me + 1, count))
    below = (slab, lax.rem(me + count - 1, count))
    right = (lax.rem(slab + 1, slabs), me)
    left = (lax.rem(slab + slabs - 1, slabs), me)
    barrier = pltpu.get_barrier_semaphore()
    for offset in OFFSETS:
        pl.semaphore_signal(barrier, inc=1, device_id=(slab, moved(me, offset)), device_id_type=MESH)
    for peer in (right, left):
        pl.semaphore_signal(barrier, inc=1, device_id=peer, device_id_type=MESH)

    def turn(slot, carry):
        for part in range(4):
            plane, half = part // 2, part % 2
            value = field[slot, plane, :, 128 * half : 128 * half + 128].astype(jnp.float32)
            turned[pl.ds(4 * slot + part, count, stride=4 * slots), :] = value
        return carry

    lax.fori_loop(0, slots, turn, 0)

    def narrow_block(row, carry):
        blocks[row] = turned[rows_at(row * 4 * slots, 4 * slots), :].astype(jnp.bfloat16)
        return carry

    lax.fori_loop(0, count, narrow_block, 0)

    pl.semaphore_wait(barrier, len(OFFSETS) + 2)
    copies = []
    for place, offset in enumerate(OFFSETS):
        peer = moved(me, offset)
        copy = pltpu.make_async_remote_copy(
            src_ref=blocks.at[peer],
            dst_ref=raw.at[me],
            send_sem=send_sem.at[place],
            recv_sem=recv_sem.at[place],
            device_id=(slab, peer),
            device_id_type=MESH,
        )
        copy.start()
        copies.append(copy)
    own = pltpu.make_async_copy(blocks.at[me], raw.at[me], own_sem.at[0])
    own.start()

    ids = lax.broadcasted_iota(jnp.int32, (8, 128), 0) * 128 + lax.broadcasted_iota(jnp.int32, (8, 128), 1)

    def find(step, place):
        for part in range(8):
            slot = step * 8 + part
            place = jnp.where(ids == slot_mode[slot], slot, place)
        return place

    found[...] = lax.fori_loop(0, slots * count // 8, find, jnp.zeros((8, 128), jnp.int32))

    for shift in range(3):
        row = jnp.clip(me + shift - 1, 0, count - 1)
        for term in range(TERMS):
            for part in range(4):
                plane, half = part // 2, part % 2
                tile = coefficient[term, plane, rows_at(row // 8 * 8, 8), 128 * half : 128 * half + 128]
                value = pltpu.roll(tile, lax.rem(8 - row % 8, 8), 0)[0:1]
                near[shift, term, part : part + 1, :] = value
                near[shift, term, part + 4 : part + 5, :] = value

    listed = pltpu.make_async_copy(found, inverse, own_sem.at[1])
    listed.start()
    listed.wait()
    own.wait()

    def widen(source):
        for part in range(4):
            value = raw[source, 32 * part : 32 * part + 32, :].astype(jnp.float32)
            wide_raw[pl.ds(source * slots + 8 * part, 8)] = value.reshape(8, 4, 128)

    widen(me)
    for copy, offset in zip(copies, OFFSETS):
        copy.wait()
        widen(moved(me, offset, -1))

    modes = HELD // CHUNKS

    def pick(step, carry):
        for part in range(8):
            mode = step * 8 + part
            source = inverse[mode // 128, mode % 128]
            value = wide_raw[source]
            wide[rows_at(4 * mode, 4), :] = value
            wide_planes[0, rows_at(2 * mode, 2), :] = value[0:2]
            wide_planes[1, rows_at(2 * mode, 2), :] = value[2:4]
        return carry

    def narrow(step, carry):
        at = rows_at(step * 64, 64)
        held[at, :] = wide[at, :].astype(jnp.bfloat16)
        at = rows_at(step * 32, 32)
        planes[0, at, :] = wide_planes[0, at, :].astype(jnp.bfloat16)
        planes[1, at, :] = wide_planes[1, at, :].astype(jnp.bfloat16)
        return carry

    sent = []

    def send(place, source, target, peer):
        copy = pltpu.make_async_remote_copy(
            src_ref=source,
            dst_ref=target,
            send_sem=halo_send.at[place],
            recv_sem=halo_recv.at[place],
            device_id=peer,
            device_id_type=MESH,
        )
        copy.start()
        sent.append(copy)

    def send_chunk(chunk):
        at, half = pl.ds(chunk * 4 * modes, 4 * modes), pl.ds(chunk * 2 * modes, 2 * modes)
        send(4 * chunk, held.at[at], row_low.at[at], above)
        send(4 * chunk + 1, held.at[at], row_high.at[at], below)
        send(4 * chunk + 2, planes.at[1, half], plane_low.at[half], right)
        send(4 * chunk + 3, planes.at[0, half], plane_high.at[half], left)

    for chunk in range(CHUNKS):
        lax.fori_loop(chunk * modes // 8, (chunk + 1) * modes // 8, pick, 0)
        lax.fori_loop(chunk * modes // 16, (chunk + 1) * modes // 16, narrow, 0)
        if chunk:
            send_chunk(chunk - 1)
    send(4 * CHUNKS, near.at[1], coef_low, right)
    send(4 * CHUNKS + 1, near.at[1], coef_high, left)
    source = (couplings[2:3, :] - 1) * ROWS + couplings[1:2, :] * 4
    address[...] = source + couplings[0:1, :] * (4 << 16)
    weight[...] = couplings[3:4, :].astype(jnp.float32) * 0.125
    send_chunk(CHUNKS - 1)
    for copy in sent:
        copy.wait()


def plane_neighbours(centre, plane, front):
    return (
        jnp.where(front, plane, pltpu.roll(centre, 2, 0)),
        jnp.where(front, pltpu.roll(centre, 6, 0), plane),
    )


def column_neighbours(centre, second, lane):
    zero = jnp.zeros_like(centre)
    low = pltpu.roll(centre, 1, 1)
    high = pltpu.roll(centre, 127, 1)
    return (
        jnp.where(lane == 0, jnp.where(second, pltpu.roll(low, 1, 0), zero), low),
        jnp.where(lane == 127, jnp.where(second, zero, pltpu.roll(high, 7, 0)), high),
    )


def apply_kernel(
    slabs, count, address, weight, held, row_low, row_high, plane_low, plane_high, near, coef_low, coef_high,
    out, faces, plane_rows, column_low, column_high, image, *sums,
):
    slab, me = lax.axis_index("slab"), lax.axis_index("mode")
    sub = lax.broadcasted_iota(jnp.int32, (8, 128), 0)
    lane = lax.broadcasted_iota(jnp.int32, (8, 128), 1)
    front = lax.rem(sub, 4) < 2
    second = lax.rem(sub, 2) == 1
    has_left = (slab > 0).astype(jnp.float32)
    has_right = (slab < slabs - 1).astype(jnp.float32)
    mask_plane = jnp.where(front, has_left, has_right)
    mask_low = (me > 0).astype(jnp.float32)
    mask_high = (me < count - 1).astype(jnp.float32)

    for term in range(TERMS):
        own = near[1, term]
        outer = jnp.where(front, pltpu.roll(coef_low[term], 6, 0), pltpu.roll(coef_high[term], 2, 0)) * mask_plane
        around = plane_neighbours(own, outer, front) + column_neighbours(own, second, lane)
        around = around + (near[0, term] * mask_low, near[2, term] * mask_high)
        for place, other in enumerate(around):
            faces[6 * term + place] = 0.5 * (own + other)

    def interleave(step, carry):
        at = rows_at(step * 16, 16)
        low = plane_low[at, :].astype(jnp.float32) * has_left
        high = plane_high[at, :].astype(jnp.float32) * has_right
        for part in range(8):
            base = pl.multiple_of(step * 32 + 4 * part, 4)
            plane_rows[pl.ds(base, 2), :] = low[2 * part : 2 * part + 2]
            plane_rows[pl.ds(base + 2, 2), :] = high[2 * part : 2 * part + 2]
        return carry

    lax.fori_loop(0, ROWS // 32, interleave, 0)

    def shift(step, carry):
        value = held[rows_at(step * 128, 128), :].astype(jnp.float32)
        around = [column_neighbours(value[8 * part : 8 * part + 8], second, lane) for part in range(16)]
        for part, (low, high) in enumerate(around):
            at = rows_at(step * 128 + 8 * part, 8)
            column_low[at, :] = low
            column_high[at, :] = high
        return carry

    lax.fori_loop(0, ROWS // 128, shift, 0)

    def stencil(step, carry):
        at = rows_at(step * 16, 16)
        centre = held[at, :].astype(jnp.float32)
        low = row_low[at, :].astype(jnp.float32)
        high = row_high[at, :].astype(jnp.float32)
        halves = []
        for half in range(2):
            part = slice(8 * half, 8 * half + 8)
            base = pl.multiple_of(step * 16 + 8 * half, 8)
            at = pl.ds(base, 8)
            own = centre[part]
            around = plane_neighbours(own, plane_rows[at, :], front) + (column_low[at, :], column_high[at, :])
            around = around + (low[part] * mask_low, high[part] * mask_high)
            halves.append((base, [own - other for other in around]))
        for term in range(TERMS):
            face = [faces[6 * term + place] for place in range(6)]
            for base, drops in halves:
                total = face[0] * drops[0]
                for place in range(1, 6):
                    total = total + face[place] * drops[place]
                if term == 0:
                    sums[0][pl.ds(base, 8), :] = total
                else:
                    image[rows_at((term - 1) * ROWS + base, 8), :] = total
        return carry

    lax.fori_loop(0, ROWS // 16, stencil, 0)

    def clear(step, carry):
        at = rows_at(step * 32, 32)
        for total in sums[1:]:
            total[at, :] = jnp.zeros((32, 128), jnp.float32)
        return carry

    lax.fori_loop(0, ROWS // 32, clear, 0)

    def couple(step, carry):
        for part in range(UNROLL):
            place = step * UNROLL + part
            both = address[0, place]
            source = pl.ds(pl.multiple_of(lax.bitwise_and(both, 0xFFFF), 4), 4)
            target = pl.ds(pl.multiple_of(lax.shift_right_logical(both, 16), 4), 4)
            total = sums[part % LANES]
            total[target, :] = total[target, :] + weight[0, place] * image[source, :]
        return carry

    lax.fori_loop(0, address.shape[1] // UNROLL, couple, 0)

    def join(step, carry):
        at = rows_at(step * 32, 32)
        total = sums[0][at, :]
        for other in sums[1:]:
            total = total + other[at, :]
        out[pl.ds(8 * step, 8)] = total.reshape(8, 4, 128)
        return carry

    lax.fori_loop(0, ROWS // 32, join, 0)
    out[MODES] = jnp.zeros((4, 128), jnp.float32)


def return_kernel(count, slot_mode, image, got, got_scales, picked, factors, coded, scales, own_sem, send_sem, recv_sem):
    slab, me = lax.axis_index("slab"), lax.axis_index("mode")
    slots = slot_mode.shape[0] // count
    barrier = pltpu.get_barrier_semaphore()
    for offset in OFFSETS:
        pl.semaphore_signal(barrier, inc=1, device_id=(slab, moved(me, offset)), device_id_type=MESH)

    def pick(group, carry):
        tops = [jnp.zeros((4, 128), jnp.float32)] * 4
        for part in range(slots):
            slot = group * slots + part
            value = image[slot_mode[slot]]
            picked[rows_at(4 * slot, 4), :] = value
            tops[part % 4] = jnp.maximum(tops[part % 4], jnp.abs(value))
        factors[group] = jnp.maximum(jnp.maximum(tops[0], tops[1]), jnp.maximum(tops[2], tops[3]))
        return carry

    lax.fori_loop(0, count, pick, 0)

    def measure(step, carry):
        for part in range(8):
            group = step * 8 + part
            top = jnp.max(jnp.max(factors[group], axis=0, keepdims=True), axis=1, keepdims=True)
            top = jnp.broadcast_to(top, (1, 128))
            scales[group] = top * (1.0 / (TOP * TOP))
            factors[group] = jnp.broadcast_to(TOP * lax.rsqrt(jnp.maximum(top, 1e-37)), (4, 128))
        return carry

    lax.fori_loop(0, count // 8, measure, 0)

    def encode(group):
        factor = factors[group][0:1]

        def part_of(part, carry):
            value = picked[rows_at(group * 4 * slots + part * 32, 32), :]
            root = value * lax.rsqrt(jnp.maximum(jnp.abs(value), 1e-37))
            code = jnp.round(root * factor).astype(jnp.int32)
            coded[group, rows_at(part * 32, 32), :] = code.astype(jnp.int16)
            return carry

        lax.fori_loop(0, 4 * slots // 32, part_of, 0)

    copies = []

    def send(place):
        peer = moved(me, OFFSETS[place])
        for kind, (source, target) in enumerate(((coded, got), (scales, got_scales))):
            copy = pltpu.make_async_remote_copy(
                src_ref=source.at[peer],
                dst_ref=target.at[me],
                send_sem=send_sem.at[kind, place],
                recv_sem=recv_sem.at[kind, place],
                device_id=(slab, peer),
                device_id_type=MESH,
            )
            copy.start()
            copies.append(copy)

    encode(moved(me, OFFSETS[0]))
    pl.semaphore_wait(barrier, len(OFFSETS))
    for place in range(1, len(OFFSETS)):
        encode(moved(me, OFFSETS[place]))
        send(place - 1)
    encode(me)
    send(len(OFFSETS) - 1)
    own = [
        pltpu.make_async_copy(coded.at[me], got.at[me], own_sem.at[0]),
        pltpu.make_async_copy(scales.at[me], got_scales.at[me], own_sem.at[1]),
    ]
    for copy in own:
        copy.start()
    for copy in own + copies:
        copy.wait()


def decode_kernel(got, got_scales, out, wide, scale):
    count, rows = got.shape[0], got.shape[1]
    for source in range(count):
        scale[source : source + 1, :] = got_scales[source]

    def widen(source, carry):
        at = rows_at(source * rows, rows)
        wide[at, :] = got[source].astype(jnp.int32).astype(jnp.float32)
        return carry

    lax.fori_loop(0, count, widen, 0)
    factor = scale[...]
    for place in range(rows):
        slot, plane, half = place // 4, (place // 2) % 2, place % 2
        value = wide[pl.ds(place, count, stride=rows), :]
        out[slot, plane, :, 128 * half : 128 * half + 128] = (value * jnp.abs(value)) * factor


def on_device(field, coefficient, slot_mode, couplings):
    slabs, count = lax.axis_size("slab"), lax.axis_size("mode")
    slots, planes_here, rows_all, columns = field.shape
    entries = couplings.shape[0]
    f32, bf16, i16, i32 = jnp.float32, jnp.bfloat16, jnp.int16, jnp.int32
    dma = pltpu.SemaphoreType.DMA
    halo = 4 * CHUNKS + 2

    held, row_low, row_high, plane_low, plane_high, near, coef_low, coef_high, address, weight = pl.pallas_call(
        lambda *refs: gather_kernel(slabs, count, *refs),
        out_shape=(
            shape_of((ROWS, 128), bf16),
            shape_of((ROWS, 128), bf16),
            shape_of((ROWS, 128), bf16),
            shape_of((ROWS // 2, 128), bf16),
            shape_of((ROWS // 2, 128), bf16),
            shape_of((3, TERMS, 8, 128), f32),
            shape_of((TERMS, 8, 128), f32),
            shape_of((TERMS, 8, 128), f32),
            shape_of((1, entries), i32),
            shape_of((1, entries), f32),
        ),
        in_specs=[SMEM, VMEM, VMEM, VMEM],
        out_specs=(VMEM,) * 10,
        scratch_shapes=[
            pltpu.VMEM((count * slots * 4, 128), f32),
            pltpu.VMEM((count, slots * 4, 128), bf16),
            pltpu.VMEM((count, slots * 4, 128), bf16),
            pltpu.VMEM((count * slots, 4, 128), f32),
            pltpu.VMEM((2, ROWS // 2, 128), bf16),
            pltpu.VMEM((ROWS, 128), f32),
            pltpu.VMEM((2, ROWS // 2, 128), f32),
            pltpu.VMEM((8, 128), i32),
            pltpu.SMEM((8, 128), i32),
            dma((2,)),
            dma((len(OFFSETS),)),
            dma((len(OFFSETS),)),
            dma((halo,)),
            dma((halo,)),
        ],
        compiler_params=pltpu.CompilerParams(collective_id=0, has_side_effects=True, vmem_limit_bytes=20 * MIB),
        name="gather",
    )(slot_mode, field, coefficient, couplings.T)

    image = pl.pallas_call(
        lambda *refs: apply_kernel(slabs, count, *refs),
        out_shape=shape_of((HELD, 4, 128), f32),
        in_specs=[SMEM] * 2 + [VMEM] * 8,
        out_specs=VMEM,
        scratch_shapes=[
            pltpu.VMEM((6 * TERMS, 8, 128), f32),
            pltpu.VMEM((ROWS, 128), f32),
            pltpu.VMEM((ROWS, 128), f32),
            pltpu.VMEM((ROWS, 128), f32),
            pltpu.VMEM(((TERMS - 1) * ROWS, 128), f32),
        ]
        + [pltpu.VMEM((ROWS, 128), f32)] * LANES,
        compiler_params=pltpu.CompilerParams(vmem_limit_bytes=24 * MIB),
        name="apply",
    )(address, weight, held, row_low, row_high, plane_low, plane_high, near, coef_low, coef_high)

    got, got_scales = pl.pallas_call(
        lambda *refs: return_kernel(count, *refs),
        out_shape=(shape_of((count, slots * 4, 128), i16), shape_of((count, 1, 128), f32)),
        in_specs=[SMEM, VMEM],
        out_specs=(VMEM, VMEM),
        scratch_shapes=[
            pltpu.VMEM((count * slots * 4, 128), f32),
            pltpu.VMEM((count, 4, 128), f32),
            pltpu.VMEM((count, slots * 4, 128), i16),
            pltpu.VMEM((count, 1, 128), f32),
            dma((2,)),
            dma((2, len(OFFSETS))),
            dma((2, len(OFFSETS))),
        ],
        compiler_params=pltpu.CompilerParams(collective_id=2, has_side_effects=True, vmem_limit_bytes=12 * MIB),
        name="give",
    )(slot_mode, image)

    step = 8
    return pl.pallas_call(
        decode_kernel,
        out_shape=shape_of((slots, planes_here, rows_all, columns), f32),
        grid=(slots // step,),
        in_specs=[
            pl.BlockSpec((count, 4 * step, 128), lambda i: (0, i, 0)),
            pl.BlockSpec((count, 1, 128), lambda i: (0, 0, 0)),
        ],
        out_specs=pl.BlockSpec((step, planes_here, rows_all, columns), lambda i: (i, 0, 0, 0)),
        scratch_shapes=[pltpu.VMEM((count * 4 * step, 128), f32), pltpu.VMEM((count, 128), f32)],
        compiler_params=pltpu.CompilerParams(vmem_limit_bytes=12 * MIB),
        name="decode",
    )(got, got_scales)


def solution(mesh):
    in_specs = (P("mode", "slab", None, None), P(None, "slab", None, None), P(), P())
    return jax.shard_map(
        on_device,
        mesh=mesh,
        in_specs=in_specs,
        out_specs=P("mode", "slab", None, None),
        check_vma=False,
    )
```

```python
import jax
import jax.numpy as jnp
from jax import lax
from jax.experimental import pallas as pl
from jax.experimental.pallas import tpu as pltpu
from jax.sharding import PartitionSpec as P

MODES = 495
HELD = 512
TERMS = 9
ROWS = 4 * HELD
LANES = 4
UNROLL = 8
CHUNKS = 4
TOP = 32700.0
SIDE = 4
MESH = pl.DeviceIdType.MESH
VMEM = pl.BlockSpec(memory_space=pltpu.VMEM)
SMEM = pl.BlockSpec(memory_space=pltpu.SMEM)
HBM = pl.BlockSpec(memory_space=pltpu.HBM)
MIB = 1024 * 1024


def far_first():
    offsets = [(x, y, core) for x in range(SIDE) for y in range(SIDE) for core in range(2)]
    hops = lambda offset: min(offset[0], SIDE - offset[0]) + min(offset[1], SIDE - offset[1])
    return sorted(offsets[1:], key=hops, reverse=True)


OFFSETS = far_first()


def shape_of(shape, dtype):
    return jax.ShapeDtypeStruct(shape, dtype)


def moved(me, offset, sign=1):
    x, y, core = me // (2 * SIDE), (me // 2) % SIDE, me % 2
    x = lax.rem(x + (sign * offset[0]) % SIDE, SIDE)
    y = lax.rem(y + (sign * offset[1]) % SIDE, SIDE)
    return (x * SIDE + y) * 2 + lax.rem(core + offset[2], 2)


def rows_at(start, size):
    return pl.ds(pl.multiple_of(start, size), size)


def plane_neighbours(centre, plane, front):
    return (
        jnp.where(front, plane, pltpu.roll(centre, 2, 0)),
        jnp.where(front, pltpu.roll(centre, 6, 0), plane),
    )


def column_neighbours(centre, second, lane):
    zero = jnp.zeros_like(centre)
    low = pltpu.roll(centre, 1, 1)
    high = pltpu.roll(centre, 127, 1)
    return (
        jnp.where(lane == 0, jnp.where(second, pltpu.roll(low, 1, 0), zero), low),
        jnp.where(lane == 127, jnp.where(second, zero, pltpu.roll(high, 7, 0)), high),
    )


def gather_kernel(
    slabs, count, slot_mode_hbm, field_hbm, coefficient_hbm, couplings_hbm,
    start, image, address, weight,
    slot_mode, field, coefficient, couplings, turned, blocks, raw, wide_raw, wide, wide_planes, found, inverse,
    held, planes, row_low, row_high, plane_low, plane_high, near, coef_low, coef_high,
    faces, plane_rows, column_low, column_high,
    load_sem, own_sem, send_sem, recv_sem, halo_send, halo_recv,
):
    slab, me = lax.axis_index("slab"), lax.axis_index("mode")
    slots = field.shape[0]
    above = (slab, lax.rem(me + 1, count))
    below = (slab, lax.rem(me + count - 1, count))
    right = (lax.rem(slab + 1, slabs), me)
    left = (lax.rem(slab + slabs - 1, slabs), me)
    sub = lax.broadcasted_iota(jnp.int32, (8, 128), 0)
    lane = lax.broadcasted_iota(jnp.int32, (8, 128), 1)
    front = lax.rem(sub, 4) < 2
    second = lax.rem(sub, 2) == 1
    has_left = (slab > 0).astype(jnp.float32)
    has_right = (slab < slabs - 1).astype(jnp.float32)
    mask_plane = jnp.where(front, has_left, has_right)
    mask_low = (me > 0).astype(jnp.float32)
    mask_high = (me < count - 1).astype(jnp.float32)

    piece = slots // 4
    loads = [
        pltpu.make_async_copy(field_hbm.at[pl.ds(piece * part, piece)], field.at[pl.ds(piece * part, piece)], load_sem.at[part])
        for part in range(4)
    ]
    others = [
        pltpu.make_async_copy(source, target, load_sem.at[4 + place])
        for place, (source, target) in enumerate(
            ((coefficient_hbm, coefficient), (slot_mode_hbm, slot_mode), (couplings_hbm, couplings))
        )
    ]
    for load in loads + others:
        load.start()
    barrier = pltpu.get_barrier_semaphore()
    for offset in OFFSETS:
        pl.semaphore_signal(barrier, inc=1, device_id=(slab, moved(me, offset)), device_id_type=MESH)
    for peer in (right, left):
        pl.semaphore_signal(barrier, inc=1, device_id=peer, device_id_type=MESH)

    def turn(slot, carry):
        for part in range(4):
            plane, half = part // 2, part % 2
            value = field[slot, plane, :, 128 * half : 128 * half + 128].astype(jnp.float32)
            turned[pl.ds(4 * slot + part, count, stride=4 * slots), :] = value
        return carry

    for part, load in enumerate(loads):
        load.wait()
        lax.fori_loop(piece * part, piece * (part + 1), turn, 0)

    def narrow_block(row, carry):
        blocks[row] = turned[rows_at(row * 4 * slots, 4 * slots), :].astype(jnp.bfloat16)
        return carry

    lax.fori_loop(0, count, narrow_block, 0)

    pl.semaphore_wait(barrier, len(OFFSETS) + 2)
    copies = []
    for place, offset in enumerate(OFFSETS):
        peer = moved(me, offset)
        copy = pltpu.make_async_remote_copy(
            src_ref=blocks.at[peer],
            dst_ref=raw.at[me],
            send_sem=send_sem.at[place],
            recv_sem=recv_sem.at[place],
            device_id=(slab, peer),
            device_id_type=MESH,
        )
        copy.start()
        copies.append(copy)
    own = pltpu.make_async_copy(blocks.at[me], raw.at[me], own_sem.at[0])
    own.start()
    for load in others:
        load.wait()

    for shift in range(3):
        row = jnp.clip(me + shift - 1, 0, count - 1)
        for term in range(TERMS):
            for part in range(4):
                plane, half = part // 2, part % 2
                tile = coefficient[term, plane, rows_at(row // 8 * 8, 8), 128 * half : 128 * half + 128]
                value = pltpu.roll(tile, lax.rem(8 - row % 8, 8), 0)[0:1]
                near[shift, term, part : part + 1, :] = value
                near[shift, term, part + 4 : part + 5, :] = value

    ids = sub * 128 + lane

    def find(step, place):
        for part in range(8):
            slot = step * 8 + part
            place = jnp.where(ids == slot_mode[slot], slot, place)
        return place

    found[...] = lax.fori_loop(0, slots * count // 8, find, jnp.zeros((8, 128), jnp.int32))
    sent = []

    def send(place, source, target, peer):
        copy = pltpu.make_async_remote_copy(
            src_ref=source,
            dst_ref=target,
            send_sem=halo_send.at[place],
            recv_sem=halo_recv.at[place],
            device_id=peer,
            device_id_type=MESH,
        )
        copy.start()
        sent.append(copy)

    send(4 * CHUNKS, near.at[1], coef_low, right)
    send(4 * CHUNKS + 1, near.at[1], coef_high, left)
    own_coef = near.at[1]
    first = couplings[0:1, :] * 4 + (couplings[2:3, :] - 1) * ROWS
    other = couplings[1:2, :] * 4 + (couplings[2:3, :] - 1) * ROWS
    address[...] = other + first * (1 << 16)
    weight[...] = couplings[3:4, :].astype(jnp.float32) * 0.125

    listed = pltpu.make_async_copy(found, inverse, own_sem.at[1])
    listed.start()
    listed.wait()
    for copy in sent:
        copy.wait()
    sent.clear()

    for term in range(TERMS):
        middle = own_coef[term]
        outer = jnp.where(front, pltpu.roll(coef_low[term], 6, 0), pltpu.roll(coef_high[term], 2, 0)) * mask_plane
        around = plane_neighbours(middle, outer, front) + column_neighbours(middle, second, lane)
        around = around + (near[0, term] * mask_low, near[2, term] * mask_high)
        for place, value in enumerate(around):
            faces[6 * term + place] = 0.5 * (middle + value)

    def widen(source):
        for part in range(4):
            value = raw[source, 32 * part : 32 * part + 32, :].astype(jnp.float32)
            wide_raw[pl.ds(source * slots + 8 * part, 8)] = value.reshape(8, 4, 128)

    own.wait()
    widen(me)
    for copy, offset in zip(copies, OFFSETS):
        copy.wait()
        widen(moved(me, offset, -1))

    modes = HELD // CHUNKS

    def pick(step, carry):
        for part in range(8):
            mode = step * 8 + part
            source = inverse[mode // 128, mode % 128]
            value = wide_raw[source]
            wide[rows_at(4 * mode, 4), :] = value
            wide_planes[0, rows_at(2 * mode, 2), :] = value[0:2]
            wide_planes[1, rows_at(2 * mode, 2), :] = value[2:4]
        return carry

    def narrow(step, carry):
        at = rows_at(step * 64, 64)
        held[at, :] = wide[at, :].astype(jnp.bfloat16)
        at = rows_at(step * 32, 32)
        planes[0, at, :] = wide_planes[0, at, :].astype(jnp.bfloat16)
        planes[1, at, :] = wide_planes[1, at, :].astype(jnp.bfloat16)
        return carry

    def send_chunk(chunk):
        at, half = pl.ds(chunk * 4 * modes, 4 * modes), pl.ds(chunk * 2 * modes, 2 * modes)
        send(4 * chunk, held.at[at], row_low.at[at], above)
        send(4 * chunk + 1, held.at[at], row_high.at[at], below)
        send(4 * chunk + 2, planes.at[1, half], plane_low.at[half], right)
        send(4 * chunk + 3, planes.at[0, half], plane_high.at[half], left)

    def shift_columns(step, carry):
        value = wide[rows_at(step * 128, 128), :]
        around = [column_neighbours(value[8 * part : 8 * part + 8], second, lane) for part in range(16)]
        for part, (low, high) in enumerate(around):
            at = rows_at(step * 128 + 8 * part, 8)
            column_low[at, :] = low
            column_high[at, :] = high
        return carry

    for chunk in range(CHUNKS):
        lax.fori_loop(chunk * modes // 8, (chunk + 1) * modes // 8, pick, 0)
        lax.fori_loop(chunk * modes // 16, (chunk + 1) * modes // 16, narrow, 0)
        if chunk:
            send_chunk(chunk - 1)
    lax.fori_loop(0, 4, shift_columns, 0)
    send_chunk(CHUNKS - 1)
    lax.fori_loop(4, ROWS // 128, shift_columns, 0)

    def interleave(step, carry):
        at = rows_at(step * 16, 16)
        low = plane_low[at, :].astype(jnp.float32) * has_left
        high = plane_high[at, :].astype(jnp.float32) * has_right
        for part in range(8):
            base = pl.multiple_of(step * 32 + 4 * part, 4)
            plane_rows[pl.ds(base, 2), :] = low[2 * part : 2 * part + 2]
            plane_rows[pl.ds(base + 2, 2), :] = high[2 * part : 2 * part + 2]
        return carry

    def stencil(step, carry):
        at = rows_at(step * 16, 16)
        low = row_low[at, :].astype(jnp.float32)
        high = row_high[at, :].astype(jnp.float32)
        halves = []
        for half in range(2):
            part = slice(8 * half, 8 * half + 8)
            base = pl.multiple_of(step * 16 + 8 * half, 8)
            at = pl.ds(base, 8)
            middle = wide[at, :]
            around = plane_neighbours(middle, plane_rows[at, :], front) + (column_low[at, :], column_high[at, :])
            around = around + (low[part] * mask_low, high[part] * mask_high)
            halves.append((base, [middle - value for value in around]))
        for term in range(TERMS):
            face = [faces[6 * term + place] for place in range(6)]
            for base, drops in halves:
                total = face[0] * drops[0]
                for place in range(1, 6):
                    total = total + face[place] * drops[place]
                if term == 0:
                    start[pl.ds(base, 8), :] = total
                else:
                    image[rows_at((term - 1) * ROWS + base, 8), :] = total
        return carry

    for chunk in range(CHUNKS):
        for copy in sent[4 * chunk : 4 * chunk + 4]:
            copy.wait()
        lax.fori_loop(chunk * modes // 8, (chunk + 1) * modes // 8, interleave, 0)
        lax.fori_loop(chunk * modes // 4, (chunk + 1) * modes // 4, stencil, 0)


def apply_kernel(address, weight, start, image, out, *sums):
    def clear(step, carry):
        at = rows_at(step * 32, 32)
        for total in sums:
            total[at, :] = jnp.zeros((32, 128), jnp.float32)
        return carry

    lax.fori_loop(0, ROWS // 32, clear, 0)

    def couple(step, carry):
        for part in range(UNROLL):
            place = 2 * (step * UNROLL + part)
            both = address[0, place]
            low, high = lax.bitwise_and(both, 0xFFFF), lax.shift_right_logical(both, 16)
            at_low = pl.ds(pl.multiple_of(lax.bitwise_and(low, ROWS - 1), 4), 4)
            at_high = pl.ds(pl.multiple_of(lax.bitwise_and(high, ROWS - 1), 4), 4)
            factor = weight[0, place]
            total = sums[part % LANES]
            to_high = total[at_high, :] + factor * image[pl.ds(pl.multiple_of(low, 4), 4), :]
            to_low = total[at_low, :] + factor * image[pl.ds(pl.multiple_of(high, 4), 4), :]
            total[at_high, :] = to_high
            total[at_low, :] = to_low
        return carry

    lax.fori_loop(0, address.shape[1] // (2 * UNROLL), couple, 0)

    def join(step, carry):
        at = rows_at(step * 32, 32)
        total = start[at, :]
        for other in sums:
            total = total + other[at, :]
        out[pl.ds(8 * step, 8)] = total.reshape(8, 4, 128)
        return carry

    lax.fori_loop(0, ROWS // 32, join, 0)
    out[MODES] = jnp.zeros((4, 128), jnp.float32)


def return_kernel(count, slot_mode, image, got, got_scales, picked, factors, coded, scales, own_sem, send_sem, recv_sem):
    slab, me = lax.axis_index("slab"), lax.axis_index("mode")
    slots = slot_mode.shape[0] // count
    barrier = pltpu.get_barrier_semaphore()
    for offset in OFFSETS:
        pl.semaphore_signal(barrier, inc=1, device_id=(slab, moved(me, offset)), device_id_type=MESH)

    def pick(group, carry):
        tops = [jnp.zeros((4, 128), jnp.float32)] * 4
        for part in range(slots):
            slot = group * slots + part
            value = image[slot_mode[slot]]
            picked[rows_at(4 * slot, 4), :] = value
            tops[part % 4] = jnp.maximum(tops[part % 4], jnp.abs(value))
        factors[group] = jnp.maximum(jnp.maximum(tops[0], tops[1]), jnp.maximum(tops[2], tops[3]))
        return carry

    lax.fori_loop(0, count, pick, 0)

    def measure(step, carry):
        for part in range(8):
            group = step * 8 + part
            top = jnp.max(jnp.max(factors[group], axis=0, keepdims=True), axis=1, keepdims=True)
            top = jnp.broadcast_to(top, (1, 128))
            scales[group] = top * (1.0 / (TOP * TOP))
            factors[group] = jnp.broadcast_to(TOP * lax.rsqrt(jnp.maximum(top, 1e-37)), (4, 128))
        return carry

    lax.fori_loop(0, count // 8, measure, 0)

    def encode(group):
        factor = factors[group][0:1]

        def part_of(part, carry):
            value = picked[rows_at(group * 4 * slots + part * 32, 32), :]
            root = value * lax.rsqrt(jnp.maximum(jnp.abs(value), 1e-37))
            code = jnp.round(root * factor).astype(jnp.int32)
            coded[group, rows_at(part * 32, 32), :] = code.astype(jnp.int16)
            return carry

        lax.fori_loop(0, 4 * slots // 32, part_of, 0)

    copies = []

    def send(place):
        peer = moved(me, OFFSETS[place])
        for kind, (source, target) in enumerate(((coded, got), (scales, got_scales))):
            copy = pltpu.make_async_remote_copy(
                src_ref=source.at[peer],
                dst_ref=target.at[me],
                send_sem=send_sem.at[kind, place],
                recv_sem=recv_sem.at[kind, place],
                device_id=(slab, peer),
                device_id_type=MESH,
            )
            copy.start()
            copies.append(copy)

    encode(moved(me, OFFSETS[0]))
    pl.semaphore_wait(barrier, len(OFFSETS))
    for place in range(1, len(OFFSETS)):
        encode(moved(me, OFFSETS[place]))
        send(place - 1)
    encode(me)
    send(len(OFFSETS) - 1)
    own = [
        pltpu.make_async_copy(coded.at[me], got.at[me], own_sem.at[0]),
        pltpu.make_async_copy(scales.at[me], got_scales.at[me], own_sem.at[1]),
    ]
    for copy in own:
        copy.start()
    for copy in own + copies:
        copy.wait()


def decode_kernel(got, got_scales, out, wide, scale):
    count, rows = got.shape[0], got.shape[1]
    for source in range(count):
        scale[source : source + 1, :] = got_scales[source]

    def widen(source, carry):
        at = rows_at(source * rows, rows)
        wide[at, :] = got[source].astype(jnp.int32).astype(jnp.float32)
        return carry

    lax.fori_loop(0, count, widen, 0)
    factor = scale[...]
    for place in range(rows):
        slot, plane, half = place // 4, (place // 2) % 2, place % 2
        value = wide[pl.ds(place, count, stride=rows), :]
        out[slot, plane, :, 128 * half : 128 * half + 128] = (value * jnp.abs(value)) * factor


def on_device(field, coefficient, slot_mode, couplings):
    slabs, count = lax.axis_size("slab"), lax.axis_size("mode")
    slots, planes_here, rows_all, columns = field.shape
    entries = couplings.shape[0]
    f32, bf16, i16, i32 = jnp.float32, jnp.bfloat16, jnp.int16, jnp.int32
    dma = pltpu.SemaphoreType.DMA
    halo = 4 * CHUNKS + 2

    start, image, address, weight = pl.pallas_call(
        lambda *refs: gather_kernel(slabs, count, *refs),
        out_shape=(
            shape_of((ROWS, 128), f32),
            shape_of(((TERMS - 1) * ROWS, 128), f32),
            shape_of((1, entries), i32),
            shape_of((1, entries), f32),
        ),
        in_specs=[HBM] * 4,
        out_specs=(VMEM,) * 4,
        scratch_shapes=[
            pltpu.SMEM(slot_mode.shape, i32),
            pltpu.VMEM(field.shape, bf16),
            pltpu.VMEM(coefficient.shape, f32),
            pltpu.VMEM((4, entries), i32),
            pltpu.VMEM((count * slots * 4, 128), f32),
            pltpu.VMEM((count, slots * 4, 128), bf16),
            pltpu.VMEM((count, slots * 4, 128), bf16),
            pltpu.VMEM((count * slots, 4, 128), f32),
            pltpu.VMEM((ROWS, 128), f32),
            pltpu.VMEM((2, ROWS // 2, 128), f32),
            pltpu.VMEM((8, 128), i32),
            pltpu.SMEM((8, 128), i32),
            pltpu.VMEM((ROWS, 128), bf16),
            pltpu.VMEM((2, ROWS // 2, 128), bf16),
            pltpu.VMEM((ROWS, 128), bf16),
            pltpu.VMEM((ROWS, 128), bf16),
            pltpu.VMEM((ROWS // 2, 128), bf16),
            pltpu.VMEM((ROWS // 2, 128), bf16),
            pltpu.VMEM((3, TERMS, 8, 128), f32),
            pltpu.VMEM((TERMS, 8, 128), f32),
            pltpu.VMEM((TERMS, 8, 128), f32),
            pltpu.VMEM((6 * TERMS, 8, 128), f32),
            pltpu.VMEM((ROWS, 128), f32),
            pltpu.VMEM((ROWS, 128), f32),
            pltpu.VMEM((ROWS, 128), f32),
            dma((7,)),
            dma((2,)),
            dma((len(OFFSETS),)),
            dma((len(OFFSETS),)),
            dma((halo,)),
            dma((halo,)),
        ],
        compiler_params=pltpu.CompilerParams(collective_id=0, has_side_effects=True, vmem_limit_bytes=30 * MIB),
        name="gather",
    )(*(pltpu.with_memory_space_constraint(value, pltpu.HBM) for value in (slot_mode, field, coefficient, couplings.T)))

    image = pl.pallas_call(
        apply_kernel,
        out_shape=shape_of((HELD, 4, 128), f32),
        in_specs=[SMEM] * 2 + [VMEM] * 2,
        out_specs=VMEM,
        scratch_shapes=[pltpu.VMEM((ROWS, 128), f32)] * LANES,
        compiler_params=pltpu.CompilerParams(vmem_limit_bytes=20 * MIB),
        name="apply",
    )(address, weight, start, image)

    got, got_scales = pl.pallas_call(
        lambda *refs: return_kernel(count, *refs),
        out_shape=(shape_of((count, slots * 4, 128), i16), shape_of((count, 1, 128), f32)),
        in_specs=[SMEM, VMEM],
        out_specs=(VMEM, VMEM),
        scratch_shapes=[
            pltpu.VMEM((count * slots * 4, 128), f32),
            pltpu.VMEM((count, 4, 128), f32),
            pltpu.VMEM((count, slots * 4, 128), i16),
            pltpu.VMEM((count, 1, 128), f32),
            dma((2,)),
            dma((2, len(OFFSETS))),
            dma((2, len(OFFSETS))),
        ],
        compiler_params=pltpu.CompilerParams(collective_id=2, has_side_effects=True, vmem_limit_bytes=12 * MIB),
        name="give",
    )(slot_mode, image)

    step = 8
    return pl.pallas_call(
        decode_kernel,
        out_shape=shape_of((slots, planes_here, rows_all, columns), f32),
        grid=(slots // step,),
        in_specs=[
            pl.BlockSpec((count, 4 * step, 128), lambda i: (0, i, 0)),
            pl.BlockSpec((count, 1, 128), lambda i: (0, 0, 0)),
        ],
        out_specs=pl.BlockSpec((step, planes_here, rows_all, columns), lambda i: (i, 0, 0, 0)),
        scratch_shapes=[pltpu.VMEM((count * 4 * step, 128), f32), pltpu.VMEM((count, 128), f32)],
        compiler_params=pltpu.CompilerParams(vmem_limit_bytes=12 * MIB),
        name="decode",
    )(got, got_scales)


def solution(mesh):
    in_specs = (P("mode", "slab", None, None), P(None, "slab", None, None), P(), P())
    return jax.shard_map(
        on_device,
        mesh=mesh,
        in_specs=in_specs,
        out_specs=P("mode", "slab", None, None),
        check_vma=False,
    )
```

```python
import jax
import jax.numpy as jnp
from jax import lax
from jax.experimental import pallas as pl
from jax.experimental.pallas import tpu as pltpu
from jax.sharding import PartitionSpec as P

MODES = 495
HELD = 512
TERMS = 9
ROWS = 4 * HELD
LANES = 2
UNROLL = 12
CHUNKS = 8
USED = 496
TOP = 32700.0
EARLY = 12
SIDE = 4
MESH = pl.DeviceIdType.MESH
VMEM = pl.BlockSpec(memory_space=pltpu.VMEM)
SMEM = pl.BlockSpec(memory_space=pltpu.SMEM)
HBM = pl.BlockSpec(memory_space=pltpu.HBM)
MIB = 1024 * 1024


def far_first():
    offsets = [(x, y, core) for x in range(SIDE) for y in range(SIDE) for core in range(2)]
    hops = lambda offset: min(offset[0], SIDE - offset[0]) + min(offset[1], SIDE - offset[1])
    return sorted(offsets[1:], key=hops, reverse=True)


OFFSETS = far_first()


def shape_of(shape, dtype):
    return jax.ShapeDtypeStruct(shape, dtype)


def moved(me, offset, sign=1):
    x, y, core = me // (2 * SIDE), (me // 2) % SIDE, me % 2
    x = lax.rem(x + (sign * offset[0]) % SIDE, SIDE)
    y = lax.rem(y + (sign * offset[1]) % SIDE, SIDE)
    return (x * SIDE + y) * 2 + lax.rem(core + offset[2], 2)


def rows_at(start, size):
    return pl.ds(pl.multiple_of(start, size), size)


def plane_neighbours(centre, plane, front):
    return (
        jnp.where(front, plane, pltpu.roll(centre, 2, 0)),
        jnp.where(front, pltpu.roll(centre, 6, 0), plane),
    )


def column_neighbours(centre, second, lane):
    zero = jnp.zeros_like(centre)
    low = pltpu.roll(centre, 1, 1)
    high = pltpu.roll(centre, 127, 1)
    return (
        jnp.where(lane == 0, jnp.where(second, pltpu.roll(low, 1, 0), zero), low),
        jnp.where(lane == 127, jnp.where(second, zero, pltpu.roll(high, 7, 0)), high),
    )


def gather_kernel(
    slabs, count, slot_mode_hbm, field_hbm, coefficient_hbm, couplings_hbm,
    start, image, address, weight,
    slot_mode, field, coefficient, couplings, turned, blocks, raw, wide_raw, wide, wide_planes, found, inverse,
    held, planes, row_low, row_high, plane_low, plane_high, near, coef_low, coef_high,
    faces, plane_rows, column_low, column_high,
    load_sem, own_sem, send_sem, recv_sem, halo_send, halo_recv,
):
    slab, me = lax.axis_index("slab"), lax.axis_index("mode")
    slots = field.shape[0]
    above = (slab, lax.rem(me + 1, count))
    below = (slab, lax.rem(me + count - 1, count))
    right = (lax.rem(slab + 1, slabs), me)
    left = (lax.rem(slab + slabs - 1, slabs), me)
    sub = lax.broadcasted_iota(jnp.int32, (8, 128), 0)
    lane = lax.broadcasted_iota(jnp.int32, (8, 128), 1)
    front = lax.rem(sub, 4) < 2
    second = lax.rem(sub, 2) == 1
    has_left = (slab > 0).astype(jnp.float32)
    has_right = (slab < slabs - 1).astype(jnp.float32)
    mask_plane = jnp.where(front, has_left, has_right)
    mask_low = (me > 0).astype(jnp.float32)
    mask_high = (me < count - 1).astype(jnp.float32)

    piece = slots // 4
    loads = [
        pltpu.make_async_copy(field_hbm.at[pl.ds(piece * part, piece)], field.at[pl.ds(piece * part, piece)], load_sem.at[part])
        for part in range(4)
    ]
    others = [
        pltpu.make_async_copy(source, target, load_sem.at[4 + place])
        for place, (source, target) in enumerate(
            ((coefficient_hbm, coefficient), (slot_mode_hbm, slot_mode), (couplings_hbm, couplings))
        )
    ]
    for load in loads + others:
        load.start()
    barrier = pltpu.get_barrier_semaphore()
    for offset in OFFSETS:
        pl.semaphore_signal(barrier, inc=1, device_id=(slab, moved(me, offset)), device_id_type=MESH)
    for peer in (right, left):
        pl.semaphore_signal(barrier, inc=1, device_id=peer, device_id_type=MESH)

    def turn(slot, carry):
        for part in range(4):
            plane, half = part // 2, part % 2
            value = field[slot, plane, :, 128 * half : 128 * half + 128].astype(jnp.float32)
            turned[pl.ds(4 * slot + part, count, stride=4 * slots), :] = value
        return carry

    for part, load in enumerate(loads):
        load.wait()
        lax.fori_loop(piece * part, piece * (part + 1), turn, 0)

    def narrow_block(row, carry):
        blocks[row] = turned[rows_at(row * 4 * slots, 4 * slots), :].astype(jnp.bfloat16)
        return carry

    lax.fori_loop(0, count, narrow_block, 0)

    pl.semaphore_wait(barrier, len(OFFSETS) + 2)
    copies = []
    for place, offset in enumerate(OFFSETS):
        peer = moved(me, offset)
        copy = pltpu.make_async_remote_copy(
            src_ref=blocks.at[peer],
            dst_ref=raw.at[me],
            send_sem=send_sem.at[place],
            recv_sem=recv_sem.at[place],
            device_id=(slab, peer),
            device_id_type=MESH,
        )
        copy.start()
        copies.append(copy)
    own = pltpu.make_async_copy(blocks.at[me], raw.at[me], own_sem.at[0])
    own.start()
    for load in others:
        load.wait()

    for shift in range(3):
        row = jnp.clip(me + shift - 1, 0, count - 1)
        for term in range(TERMS):
            for part in range(4):
                plane, half = part // 2, part % 2
                tile = coefficient[term, plane, rows_at(row // 8 * 8, 8), 128 * half : 128 * half + 128]
                value = pltpu.roll(tile, lax.rem(8 - row % 8, 8), 0)[0:1]
                near[shift, term, part : part + 1, :] = value
                near[shift, term, part + 4 : part + 5, :] = value

    ids = sub * 128 + lane

    def find(step, place):
        for part in range(8):
            slot = step * 8 + part
            place = jnp.where(ids == slot_mode[slot], slot, place)
        return place

    found[...] = lax.fori_loop(0, slots * count // 8, find, jnp.zeros((8, 128), jnp.int32))
    sent = []

    def send(place, source, target, peer):
        copy = pltpu.make_async_remote_copy(
            src_ref=source,
            dst_ref=target,
            send_sem=halo_send.at[place],
            recv_sem=halo_recv.at[place],
            device_id=peer,
            device_id_type=MESH,
        )
        copy.start()
        sent.append(copy)

    send(4 * CHUNKS, near.at[1], coef_low, right)
    send(4 * CHUNKS + 1, near.at[1], coef_high, left)
    own_coef = near.at[1]
    first = couplings[0:1, :] * 4 + (couplings[2:3, :] - 1) * ROWS
    other = couplings[1:2, :] * 4 + (couplings[2:3, :] - 1) * ROWS
    address[...] = other + first * (1 << 16)
    weight[...] = couplings[3:4, :].astype(jnp.float32) * 0.125

    listed = pltpu.make_async_copy(found, inverse, own_sem.at[1])
    listed.start()
    listed.wait()
    for copy in sent:
        copy.wait()
    sent.clear()

    for term in range(TERMS):
        middle = own_coef[term]
        outer = jnp.where(front, pltpu.roll(coef_low[term], 6, 0), pltpu.roll(coef_high[term], 2, 0)) * mask_plane
        around = plane_neighbours(middle, outer, front) + column_neighbours(middle, second, lane)
        around = around + (near[0, term] * mask_low, near[2, term] * mask_high)
        for place, value in enumerate(around):
            faces[6 * term + place] = 0.5 * (middle + value)

    def widen(source):
        for part in range(4):
            value = raw[source, 32 * part : 32 * part + 32, :].astype(jnp.float32)
            wide_raw[pl.ds(source * slots + 8 * part, 8)] = value.reshape(8, 4, 128)

    own.wait()
    widen(me)
    for copy, offset in zip(copies, OFFSETS):
        copy.wait()
        widen(moved(me, offset, -1))

    ends = [min(chunk * HELD // CHUNKS, USED) for chunk in range(CHUNKS + 1)]

    def pick(step, carry):
        for part in range(8):
            mode = step * 8 + part
            source = inverse[lax.shift_right_logical(step, 4), lax.bitwise_and(step, 15) * 8 + part]
            value = wide_raw[source]
            wide[rows_at(4 * mode, 4), :] = value
            wide_planes[0, rows_at(2 * mode, 2), :] = value[0:2]
            wide_planes[1, rows_at(2 * mode, 2), :] = value[2:4]
        return carry

    def narrow(step, carry):
        at = rows_at(step * 64, 64)
        held[at, :] = wide[at, :].astype(jnp.bfloat16)
        at = rows_at(step * 32, 32)
        planes[0, at, :] = wide_planes[0, at, :].astype(jnp.bfloat16)
        planes[1, at, :] = wide_planes[1, at, :].astype(jnp.bfloat16)
        return carry

    def send_chunk(chunk):
        low, size = ends[chunk], ends[chunk + 1] - ends[chunk]
        at, half = pl.ds(4 * low, 4 * size), pl.ds(2 * low, 2 * size)
        send(4 * chunk, held.at[at], row_low.at[at], above)
        send(4 * chunk + 1, held.at[at], row_high.at[at], below)
        send(4 * chunk + 2, planes.at[1, half], plane_low.at[half], right)
        send(4 * chunk + 3, planes.at[0, half], plane_high.at[half], left)

    def shift_columns(step, carry):
        value = wide[rows_at(step * 64, 64), :]
        around = [column_neighbours(value[8 * part : 8 * part + 8], second, lane) for part in range(8)]
        for part, (low, high) in enumerate(around):
            at = rows_at(step * 64 + 8 * part, 8)
            column_low[at, :] = low
            column_high[at, :] = high
        return carry

    for chunk in range(CHUNKS):
        lax.fori_loop(ends[chunk] // 8, ends[chunk + 1] // 8, pick, 0)
        lax.fori_loop(ends[chunk] // 16, ends[chunk + 1] // 16, narrow, 0)
        if chunk:
            send_chunk(chunk - 1)
    lax.fori_loop(0, 4, shift_columns, 0)
    send_chunk(CHUNKS - 1)
    lax.fori_loop(4, USED // 16, shift_columns, 0)

    def interleave(step, carry):
        at = rows_at(step * 16, 16)
        low = plane_low[at, :].astype(jnp.float32) * has_left
        high = plane_high[at, :].astype(jnp.float32) * has_right
        for part in range(8):
            base = pl.multiple_of(step * 32 + 4 * part, 4)
            plane_rows[pl.ds(base, 2), :] = low[2 * part : 2 * part + 2]
            plane_rows[pl.ds(base + 2, 2), :] = high[2 * part : 2 * part + 2]
        return carry

    def stencil(step, carry):
        at = rows_at(step * 16, 16)
        low = row_low[at, :].astype(jnp.float32)
        high = row_high[at, :].astype(jnp.float32)
        halves = []
        for half in range(2):
            part = slice(8 * half, 8 * half + 8)
            base = pl.multiple_of(step * 16 + 8 * half, 8)
            at = pl.ds(base, 8)
            middle = wide[at, :]
            around = plane_neighbours(middle, plane_rows[at, :], front) + (column_low[at, :], column_high[at, :])
            around = around + (low[part] * mask_low, high[part] * mask_high)
            halves.append((base, [middle - value for value in around]))
        for term in range(TERMS):
            face = [faces[6 * term + place] for place in range(6)]
            for base, drops in halves:
                total = face[0] * drops[0]
                for place in range(1, 6):
                    total = total + face[place] * drops[place]
                if term == 0:
                    start[pl.ds(base, 8), :] = total
                else:
                    image[rows_at((term - 1) * ROWS + base, 8), :] = total
        return carry

    for chunk in range(CHUNKS):
        for copy in sent[4 * chunk : 4 * chunk + 4]:
            copy.wait()
        lax.fori_loop(ends[chunk] // 8, ends[chunk + 1] // 8, interleave, 0)
        lax.fori_loop(ends[chunk] // 4, ends[chunk + 1] // 4, stencil, 0)


def apply_kernel(address, weight, start, image, *sums):
    def clear(step, carry):
        at = rows_at(step * 32, 32)
        for total in sums[1:]:
            total[at, :] = jnp.zeros((32, 128), jnp.float32)
        return carry

    lax.fori_loop(0, ROWS // 32, clear, 0)

    def couple(step, carry):
        for part in range(UNROLL):
            place = 2 * (step * UNROLL + part)
            both = address[0, place]
            low, high = lax.bitwise_and(both, 0xFFFF), lax.shift_right_logical(both, 16)
            at_low = pl.ds(pl.multiple_of(lax.bitwise_and(low, ROWS - 1), 4), 4)
            at_high = pl.ds(pl.multiple_of(lax.bitwise_and(high, ROWS - 1), 4), 4)
            factor = weight[0, place]
            total = sums[part % LANES]
            to_high = total[at_high, :] + factor * image[pl.ds(pl.multiple_of(low, 4), 4), :]
            to_low = total[at_low, :] + factor * image[pl.ds(pl.multiple_of(high, 4), 4), :]
            total[at_high, :] = to_high
            total[at_low, :] = to_low
        return carry

    lax.fori_loop(0, address.shape[1] // (2 * UNROLL), couple, 0)


def return_kernel(count, slot_mode, *refs):
    sums, refs = refs[:LANES], refs[LANES:]
    got, got_scales, image, picked, factors, coded, scales, own_sem, send_sem, recv_sem = refs
    slab, me = lax.axis_index("slab"), lax.axis_index("mode")
    slots = slot_mode.shape[0] // count
    barrier = pltpu.get_barrier_semaphore()
    for offset in OFFSETS:
        pl.semaphore_signal(barrier, inc=1, device_id=(slab, moved(me, offset)), device_id_type=MESH)

    def join(step, carry):
        at = rows_at(step * 32, 32)
        total = sums[0][at, :]
        for other in sums[1:]:
            total = total + other[at, :]
        image[pl.ds(8 * step, 8)] = total.reshape(8, 4, 128)
        return carry

    lax.fori_loop(0, USED // 8, join, 0)
    image[MODES] = jnp.zeros((4, 128), jnp.float32)

    def pick(group, carry):
        tops = [jnp.zeros((4, 128), jnp.float32)] * 4
        for part in range(slots):
            slot = group * slots + part
            value = image[slot_mode[slot]]
            picked[rows_at(4 * slot, 4), :] = value
            tops[part % 4] = jnp.maximum(tops[part % 4], jnp.abs(value))
        factors[group] = jnp.maximum(jnp.maximum(tops[0], tops[1]), jnp.maximum(tops[2], tops[3]))
        return carry

    lax.fori_loop(0, count, pick, 0)

    def measure(step, carry):
        for part in range(8):
            group = step * 8 + part
            top = jnp.max(jnp.max(factors[group], axis=0, keepdims=True), axis=1, keepdims=True)
            top = jnp.broadcast_to(top, (1, 128))
            scales[group] = top * (1.0 / (TOP * TOP))
            factors[group] = jnp.broadcast_to(TOP * lax.rsqrt(jnp.maximum(top, 1e-37)), (4, 128))
        return carry

    lax.fori_loop(0, count // 8, measure, 0)

    def encode(group):
        factor = factors[group][0:1]

        def part_of(part, carry):
            value = picked[rows_at(group * 4 * slots + part * 32, 32), :]
            root = value * lax.rsqrt(jnp.maximum(jnp.abs(value), 1e-37))
            code = jnp.round(root * factor).astype(jnp.int32)
            coded[group, rows_at(part * 32, 32), :] = code.astype(jnp.int16)
            return carry

        lax.fori_loop(0, 4 * slots // 32, part_of, 0)

    copies = []

    def send(place):
        peer = moved(me, OFFSETS[place])
        for kind, (source, target) in enumerate(((coded, got), (scales, got_scales))):
            copy = pltpu.make_async_remote_copy(
                src_ref=source.at[peer],
                dst_ref=target.at[me],
                send_sem=send_sem.at[kind, place],
                recv_sem=recv_sem.at[kind, place],
                device_id=(slab, peer),
                device_id_type=MESH,
            )
            copy.start()
            copies.append(copy)

    for place in range(EARLY):
        encode(moved(me, OFFSETS[place]))
    pl.semaphore_wait(barrier, len(OFFSETS))
    for place in range(EARLY - 1):
        send(place)
    for place in range(EARLY, len(OFFSETS)):
        encode(moved(me, OFFSETS[place]))
        send(place - 1)
    encode(me)
    send(len(OFFSETS) - 1)
    own = [
        pltpu.make_async_copy(coded.at[me], got.at[me], own_sem.at[0]),
        pltpu.make_async_copy(scales.at[me], got_scales.at[me], own_sem.at[1]),
    ]
    for copy in own:
        copy.start()
    for copy in own + copies:
        copy.wait()


def decode_kernel(got, got_scales, out, wide, scale):
    count, rows = got.shape[0], got.shape[1]
    for source in range(count):
        scale[source : source + 1, :] = got_scales[source]

    def widen(source, carry):
        at = rows_at(source * rows, rows)
        wide[at, :] = got[source].astype(jnp.int32).astype(jnp.float32)
        return carry

    lax.fori_loop(0, count, widen, 0)
    factor = scale[...]
    for place in range(rows):
        slot, plane, half = place // 4, (place // 2) % 2, place % 2
        value = wide[pl.ds(place, count, stride=rows), :]
        out[slot, plane, :, 128 * half : 128 * half + 128] = (value * jnp.abs(value)) * factor


def on_device(field, coefficient, slot_mode, couplings):
    slabs, count = lax.axis_size("slab"), lax.axis_size("mode")
    slots, planes_here, rows_all, columns = field.shape
    entries = couplings.shape[0]
    f32, bf16, i16, i32 = jnp.float32, jnp.bfloat16, jnp.int16, jnp.int32
    dma = pltpu.SemaphoreType.DMA
    halo = 4 * CHUNKS + 2

    start, image, address, weight = pl.pallas_call(
        lambda *refs: gather_kernel(slabs, count, *refs),
        out_shape=(
            shape_of((ROWS, 128), f32),
            shape_of(((TERMS - 1) * ROWS, 128), f32),
            shape_of((1, entries), i32),
            shape_of((1, entries), f32),
        ),
        in_specs=[HBM] * 4,
        out_specs=(VMEM,) * 4,
        scratch_shapes=[
            pltpu.SMEM(slot_mode.shape, i32),
            pltpu.VMEM(field.shape, bf16),
            pltpu.VMEM(coefficient.shape, f32),
            pltpu.VMEM((4, entries), i32),
            pltpu.VMEM((count * slots * 4, 128), f32),
            pltpu.VMEM((count, slots * 4, 128), bf16),
            pltpu.VMEM((count, slots * 4, 128), bf16),
            pltpu.VMEM((count * slots, 4, 128), f32),
            pltpu.VMEM((ROWS, 128), f32),
            pltpu.VMEM((2, ROWS // 2, 128), f32),
            pltpu.VMEM((8, 128), i32),
            pltpu.SMEM((8, 128), i32),
            pltpu.VMEM((ROWS, 128), bf16),
            pltpu.VMEM((2, ROWS // 2, 128), bf16),
            pltpu.VMEM((ROWS, 128), bf16),
            pltpu.VMEM((ROWS, 128), bf16),
            pltpu.VMEM((ROWS // 2, 128), bf16),
            pltpu.VMEM((ROWS // 2, 128), bf16),
            pltpu.VMEM((3, TERMS, 8, 128), f32),
            pltpu.VMEM((TERMS, 8, 128), f32),
            pltpu.VMEM((TERMS, 8, 128), f32),
            pltpu.VMEM((6 * TERMS, 8, 128), f32),
            pltpu.VMEM((ROWS, 128), f32),
            pltpu.VMEM((ROWS, 128), f32),
            pltpu.VMEM((ROWS, 128), f32),
            dma((7,)),
            dma((2,)),
            dma((len(OFFSETS),)),
            dma((len(OFFSETS),)),
            dma((halo,)),
            dma((halo,)),
        ],
        compiler_params=pltpu.CompilerParams(collective_id=0, has_side_effects=True, vmem_limit_bytes=30 * MIB),
        name="gather",
    )(*(pltpu.with_memory_space_constraint(value, pltpu.HBM) for value in (slot_mode, field, coefficient, couplings.T)))

    sums = pl.pallas_call(
        apply_kernel,
        out_shape=(shape_of((ROWS, 128), f32),) * LANES,
        in_specs=[SMEM] * 2 + [VMEM] * 2,
        out_specs=(VMEM,) * LANES,
        input_output_aliases={2: 0},
        compiler_params=pltpu.CompilerParams(vmem_limit_bytes=16 * MIB),
        name="apply",
    )(address, weight, start, image)

    got, got_scales = pl.pallas_call(
        lambda *refs: return_kernel(count, *refs),
        out_shape=(shape_of((count, slots * 4, 128), i16), shape_of((count, 1, 128), f32)),
        in_specs=[SMEM] + [VMEM] * LANES,
        out_specs=(VMEM, VMEM),
        scratch_shapes=[
            pltpu.VMEM((HELD, 4, 128), f32),
            pltpu.VMEM((count * slots * 4, 128), f32),
            pltpu.VMEM((count, 4, 128), f32),
            pltpu.VMEM((count, slots * 4, 128), i16),
            pltpu.VMEM((count, 1, 128), f32),
            dma((2,)),
            dma((2, len(OFFSETS))),
            dma((2, len(OFFSETS))),
        ],
        compiler_params=pltpu.CompilerParams(collective_id=2, has_side_effects=True, vmem_limit_bytes=12 * MIB),
        name="give",
    )(slot_mode, *sums)

    step = 8
    return pl.pallas_call(
        decode_kernel,
        out_shape=shape_of((slots, planes_here, rows_all, columns), f32),
        grid=(slots // step,),
        in_specs=[
            pl.BlockSpec((count, 4 * step, 128), lambda i: (0, i, 0)),
            pl.BlockSpec((count, 1, 128), lambda i: (0, 0, 0)),
        ],
        out_specs=pl.BlockSpec((step, planes_here, rows_all, columns), lambda i: (i, 0, 0, 0)),
        scratch_shapes=[pltpu.VMEM((count * 4 * step, 128), f32), pltpu.VMEM((count, 128), f32)],
        compiler_params=pltpu.CompilerParams(vmem_limit_bytes=12 * MIB),
        name="decode",
    )(got, got_scales)


def solution(mesh):
    in_specs = (P("mode", "slab", None, None), P(None, "slab", None, None), P(), P())
    return jax.shard_map(
        on_device,
        mesh=mesh,
        in_specs=in_specs,
        out_specs=P("mode", "slab", None, None),
        check_vma=False,
    )
```

```python
import jax
import jax.numpy as jnp
from jax import lax
from jax.experimental import pallas as pl
from jax.experimental.pallas import tpu as pltpu
from jax.sharding import PartitionSpec as P

MODES = 495
HELD = 512
TERMS = 9
ROWS = 4 * HELD
LANES = 2
UNROLL = 12
CHUNKS = 8
USED = 496
TOP = 32700.0
EARLY = 12
SIDE = 4
MESH = pl.DeviceIdType.MESH
VMEM = pl.BlockSpec(memory_space=pltpu.VMEM)
SMEM = pl.BlockSpec(memory_space=pltpu.SMEM)
HBM = pl.BlockSpec(memory_space=pltpu.HBM)
MIB = 1024 * 1024


def far_first():
    offsets = [(x, y, core) for x in range(SIDE) for y in range(SIDE) for core in range(2)]
    hops = lambda offset: min(offset[0], SIDE - offset[0]) + min(offset[1], SIDE - offset[1])
    return sorted(offsets[1:], key=hops, reverse=True)


OFFSETS = far_first()


def shape_of(shape, dtype):
    return jax.ShapeDtypeStruct(shape, dtype)


def moved(me, offset, sign=1):
    x, y, core = me // (2 * SIDE), (me // 2) % SIDE, me % 2
    x = lax.rem(x + (sign * offset[0]) % SIDE, SIDE)
    y = lax.rem(y + (sign * offset[1]) % SIDE, SIDE)
    return (x * SIDE + y) * 2 + lax.rem(core + offset[2], 2)


def rows_at(start, size):
    return pl.ds(pl.multiple_of(start, size), size)


def plane_neighbours(centre, plane, front):
    return (
        jnp.where(front, plane, pltpu.roll(centre, 2, 0)),
        jnp.where(front, pltpu.roll(centre, 6, 0), plane),
    )


def column_neighbours(centre, second, lane):
    zero = jnp.zeros_like(centre)
    low = pltpu.roll(centre, 1, 1)
    high = pltpu.roll(centre, 127, 1)
    return (
        jnp.where(lane == 0, jnp.where(second, pltpu.roll(low, 1, 0), zero), low),
        jnp.where(lane == 127, jnp.where(second, zero, pltpu.roll(high, 7, 0)), high),
    )


def gather_kernel(
    slabs, count, slot_mode_hbm, field_hbm, coefficient_hbm, couplings_hbm,
    start, image, address, weight,
    slot_mode, field, coefficient, couplings, turned, blocks, raw, wide, wide_planes, found, inverse,
    held, planes, row_low, row_high, plane_low, plane_high, near, coef_low, coef_high,
    faces, plane_rows, column_low, column_high,
    load_sem, own_sem, send_sem, recv_sem, halo_send, halo_recv,
):
    slab, me = lax.axis_index("slab"), lax.axis_index("mode")
    slots = field.shape[0]
    above = (slab, lax.rem(me + 1, count))
    below = (slab, lax.rem(me + count - 1, count))
    right = (lax.rem(slab + 1, slabs), me)
    left = (lax.rem(slab + slabs - 1, slabs), me)
    sub = lax.broadcasted_iota(jnp.int32, (8, 128), 0)
    lane = lax.broadcasted_iota(jnp.int32, (8, 128), 1)
    front = lax.rem(sub, 4) < 2
    second = lax.rem(sub, 2) == 1
    has_left = (slab > 0).astype(jnp.float32)
    has_right = (slab < slabs - 1).astype(jnp.float32)
    mask_plane = jnp.where(front, has_left, has_right)
    mask_low = (me > 0).astype(jnp.float32)
    mask_high = (me < count - 1).astype(jnp.float32)

    piece = slots // 4
    loads = [
        pltpu.make_async_copy(field_hbm.at[pl.ds(piece * part, piece)], field.at[pl.ds(piece * part, piece)], load_sem.at[part])
        for part in range(4)
    ]
    others = [
        pltpu.make_async_copy(source, target, load_sem.at[4 + place])
        for place, (source, target) in enumerate(
            ((coefficient_hbm, coefficient), (slot_mode_hbm, slot_mode), (couplings_hbm, couplings))
        )
    ]
    for load in loads + others:
        load.start()
    barrier = pltpu.get_barrier_semaphore()
    for offset in OFFSETS:
        pl.semaphore_signal(barrier, inc=1, device_id=(slab, moved(me, offset)), device_id_type=MESH)
    for peer in (right, left):
        pl.semaphore_signal(barrier, inc=1, device_id=peer, device_id_type=MESH)

    def turn(slot, carry):
        for part in range(4):
            plane, half = part // 2, part % 2
            value = field[slot, plane, :, 128 * half : 128 * half + 128].astype(jnp.float32)
            turned[pl.ds(4 * slot + part, count, stride=4 * slots), :] = value
        return carry

    for part, load in enumerate(loads):
        load.wait()
        lax.fori_loop(piece * part, piece * (part + 1), turn, 0)

    def narrow_block(row, carry):
        value = turned[rows_at(row * 4 * slots, 4 * slots), :]
        blocks[row] = value.reshape(slots, 4, 128).astype(jnp.bfloat16)
        return carry

    lax.fori_loop(0, count, narrow_block, 0)

    pl.semaphore_wait(barrier, len(OFFSETS) + 2)
    copies = []
    for place, offset in enumerate(OFFSETS):
        peer = moved(me, offset)
        copy = pltpu.make_async_remote_copy(
            src_ref=blocks.at[peer],
            dst_ref=raw.at[pl.ds(me * slots, slots)],
            send_sem=send_sem.at[place],
            recv_sem=recv_sem.at[place],
            device_id=(slab, peer),
            device_id_type=MESH,
        )
        copy.start()
        copies.append(copy)
    own = pltpu.make_async_copy(blocks.at[me], raw.at[pl.ds(me * slots, slots)], own_sem.at[0])
    own.start()
    for load in others:
        load.wait()

    for shift in range(3):
        row = jnp.clip(me + shift - 1, 0, count - 1)
        for term in range(TERMS):
            for part in range(4):
                plane, half = part // 2, part % 2
                tile = coefficient[term, plane, rows_at(row // 8 * 8, 8), 128 * half : 128 * half + 128]
                value = pltpu.roll(tile, lax.rem(8 - row % 8, 8), 0)[0:1]
                near[shift, term, part : part + 1, :] = value
                near[shift, term, part + 4 : part + 5, :] = value

    ids = sub * 128 + lane

    def find(step, place):
        for part in range(8):
            slot = step * 8 + part
            place = jnp.where(ids == slot_mode[slot], slot, place)
        return place

    found[...] = lax.fori_loop(0, slots * count // 8, find, jnp.zeros((8, 128), jnp.int32))
    sent = []

    def send(place, source, target, peer):
        copy = pltpu.make_async_remote_copy(
            src_ref=source,
            dst_ref=target,
            send_sem=halo_send.at[place],
            recv_sem=halo_recv.at[place],
            device_id=peer,
            device_id_type=MESH,
        )
        copy.start()
        sent.append(copy)

    send(4 * CHUNKS, near.at[1], coef_low, right)
    send(4 * CHUNKS + 1, near.at[1], coef_high, left)
    own_coef = near.at[1]
    first = couplings[0:1, :] * 4 + (couplings[2:3, :] - 1) * ROWS
    other = couplings[1:2, :] * 4 + (couplings[2:3, :] - 1) * ROWS
    address[...] = other + first * (1 << 16)
    weight[...] = couplings[3:4, :].astype(jnp.float32) * 0.125

    listed = pltpu.make_async_copy(found, inverse, own_sem.at[1])
    listed.start()
    listed.wait()
    for copy in sent:
        copy.wait()
    sent.clear()

    for term in range(TERMS):
        middle = own_coef[term]
        outer = jnp.where(front, pltpu.roll(coef_low[term], 6, 0), pltpu.roll(coef_high[term], 2, 0)) * mask_plane
        around = plane_neighbours(middle, outer, front) + column_neighbours(middle, second, lane)
        around = around + (near[0, term] * mask_low, near[2, term] * mask_high)
        for place, value in enumerate(around):
            faces[6 * term + place] = 0.5 * (middle + value)

    own.wait()
    for copy in copies:
        copy.wait()

    ends = [min(chunk * HELD // CHUNKS, USED) for chunk in range(CHUNKS + 1)]

    def pick(step, carry):
        for part in range(8):
            mode = step * 8 + part
            source = inverse[lax.shift_right_logical(step, 4), lax.bitwise_and(step, 15) * 8 + part]
            value = raw[source].astype(jnp.float32)
            wide[rows_at(4 * mode, 4), :] = value
            wide_planes[0, rows_at(2 * mode, 2), :] = value[0:2]
            wide_planes[1, rows_at(2 * mode, 2), :] = value[2:4]
        return carry

    def narrow(step, carry):
        at = rows_at(step * 64, 64)
        held[at, :] = wide[at, :].astype(jnp.bfloat16)
        at = rows_at(step * 32, 32)
        planes[0, at, :] = wide_planes[0, at, :].astype(jnp.bfloat16)
        planes[1, at, :] = wide_planes[1, at, :].astype(jnp.bfloat16)
        return carry

    def send_chunk(chunk):
        low, size = ends[chunk], ends[chunk + 1] - ends[chunk]
        at, half = pl.ds(4 * low, 4 * size), pl.ds(2 * low, 2 * size)
        send(4 * chunk, held.at[at], row_low.at[at], above)
        send(4 * chunk + 1, held.at[at], row_high.at[at], below)
        send(4 * chunk + 2, planes.at[1, half], plane_low.at[half], right)
        send(4 * chunk + 3, planes.at[0, half], plane_high.at[half], left)

    def shift_columns(step, carry):
        value = wide[rows_at(step * 64, 64), :]
        around = [column_neighbours(value[8 * part : 8 * part + 8], second, lane) for part in range(8)]
        for part, (low, high) in enumerate(around):
            at = rows_at(step * 64 + 8 * part, 8)
            column_low[at, :] = low
            column_high[at, :] = high
        return carry

    for chunk in range(CHUNKS):
        lax.fori_loop(ends[chunk] // 8, ends[chunk + 1] // 8, pick, 0)
        lax.fori_loop(ends[chunk] // 16, ends[chunk + 1] // 16, narrow, 0)
        if chunk:
            send_chunk(chunk - 1)
    lax.fori_loop(0, 4, shift_columns, 0)
    send_chunk(CHUNKS - 1)
    lax.fori_loop(4, USED // 16, shift_columns, 0)

    def interleave(step, carry):
        at = rows_at(step * 16, 16)
        low = plane_low[at, :].astype(jnp.float32) * has_left
        high = plane_high[at, :].astype(jnp.float32) * has_right
        for part in range(8):
            base = pl.multiple_of(step * 32 + 4 * part, 4)
            plane_rows[pl.ds(base, 2), :] = low[2 * part : 2 * part + 2]
            plane_rows[pl.ds(base + 2, 2), :] = high[2 * part : 2 * part + 2]
        return carry

    def stencil(step, carry):
        at = rows_at(step * 16, 16)
        low = row_low[at, :].astype(jnp.float32)
        high = row_high[at, :].astype(jnp.float32)
        halves = []
        for half in range(2):
            part = slice(8 * half, 8 * half + 8)
            base = pl.multiple_of(step * 16 + 8 * half, 8)
            at = pl.ds(base, 8)
            middle = wide[at, :]
            around = plane_neighbours(middle, plane_rows[at, :], front) + (column_low[at, :], column_high[at, :])
            around = around + (low[part] * mask_low, high[part] * mask_high)
            halves.append((base, [middle - value for value in around]))
        for term in range(TERMS):
            face = [faces[6 * term + place] for place in range(6)]
            for base, drops in halves:
                total = face[0] * drops[0]
                for place in range(1, 6):
                    total = total + face[place] * drops[place]
                if term == 0:
                    start[pl.ds(base, 8), :] = total
                else:
                    image[rows_at((term - 1) * ROWS + base, 8), :] = total
        return carry

    for chunk in range(CHUNKS):
        for copy in sent[4 * chunk : 4 * chunk + 4]:
            copy.wait()
        lax.fori_loop(ends[chunk] // 8, ends[chunk + 1] // 8, interleave, 0)
        lax.fori_loop(ends[chunk] // 4, ends[chunk + 1] // 4, stencil, 0)


def apply_kernel(address, weight, start, image, *sums):
    def clear(step, carry):
        at = rows_at(step * 32, 32)
        for total in sums[1:]:
            total[at, :] = jnp.zeros((32, 128), jnp.float32)
        return carry

    lax.fori_loop(0, ROWS // 32, clear, 0)

    def couple(step, carry):
        for part in range(UNROLL):
            place = 2 * (step * UNROLL + part)
            both = address[0, place]
            low, high = lax.bitwise_and(both, 0xFFFF), lax.shift_right_logical(both, 16)
            at_low = pl.ds(pl.multiple_of(lax.bitwise_and(low, ROWS - 1), 4), 4)
            at_high = pl.ds(pl.multiple_of(lax.bitwise_and(high, ROWS - 1), 4), 4)
            factor = weight[0, place]
            total = sums[part % LANES]
            to_high = total[at_high, :] + factor * image[pl.ds(pl.multiple_of(low, 4), 4), :]
            to_low = total[at_low, :] + factor * image[pl.ds(pl.multiple_of(high, 4), 4), :]
            total[at_high, :] = to_high
            total[at_low, :] = to_low
        return carry

    lax.fori_loop(0, address.shape[1] // (2 * UNROLL), couple, 0)


def return_kernel(count, slot_mode, *refs):
    sums, refs = refs[:LANES], refs[LANES:]
    got, got_scales, image, codes, picked, coded, scale, own_sem, send_sem, recv_sem = refs
    slab, me = lax.axis_index("slab"), lax.axis_index("mode")
    slots = slot_mode.shape[0] // count
    barrier = pltpu.get_barrier_semaphore()
    for offset in OFFSETS:
        pl.semaphore_signal(barrier, inc=1, device_id=(slab, moved(me, offset)), device_id_type=MESH)

    def joined(step):
        at = rows_at(step * 32, 32)
        total = sums[0][at, :]
        for other in sums[1:]:
            total = total + other[at, :]
        return at, total

    def join(step, top):
        at, total = joined(step)
        image[at, :] = total
        size = jnp.abs(total)
        return jnp.maximum(top, jnp.maximum(jnp.maximum(size[0:8], size[8:16]), jnp.maximum(size[16:24], size[24:32])))

    last = USED // 8 - 1
    top = lax.fori_loop(0, last, join, jnp.zeros((8, 128), jnp.float32))
    at, total = joined(last)
    real = lax.broadcasted_iota(jnp.int32, (32, 128), 0) < 4 * (MODES - 8 * last)
    total = jnp.where(real, total, 0.0)
    image[at, :] = total
    size = jnp.max(jnp.abs(total), axis=0, keepdims=True)
    top = jnp.maximum(jnp.max(top, axis=0, keepdims=True), size)
    top = jnp.broadcast_to(jnp.max(top, axis=1, keepdims=True), (1, 128))
    scale[...] = top * (1.0 / (TOP * TOP))
    factor = TOP * lax.rsqrt(jnp.maximum(top, 1e-37))

    def encode(step, carry):
        value = image[rows_at(step * 32, 32), :]
        root = value * lax.rsqrt(jnp.maximum(jnp.abs(value), 1e-37))
        code = jnp.round(root * factor).astype(jnp.int32)
        codes[pl.ds(step * 8, 8)] = code.reshape(8, 4, 128)
        return carry

    lax.fori_loop(0, USED // 8, encode, 0)

    def prepare(group):
        def pick(step, carry):
            for part in range(8):
                slot = group * slots + step * 8 + part
                picked[rows_at(4 * slot, 4), :] = codes[slot_mode[slot]]
            return carry

        lax.fori_loop(0, slots // 8, pick, 0)
        for part in range(4):
            at = rows_at(group * 4 * slots + slots * part, slots)
            coded[group, slots * part : slots * (part + 1), :] = picked[at, :].astype(jnp.int16)

    copies = []

    def send(place):
        peer = moved(me, OFFSETS[place])
        for kind, (source, target) in enumerate(((coded.at[peer], got), (scale, got_scales))):
            copy = pltpu.make_async_remote_copy(
                src_ref=source,
                dst_ref=target.at[me],
                send_sem=send_sem.at[kind, place],
                recv_sem=recv_sem.at[kind, place],
                device_id=(slab, peer),
                device_id_type=MESH,
            )
            copy.start()
            copies.append(copy)

    for place in range(EARLY):
        prepare(moved(me, OFFSETS[place]))
    pl.semaphore_wait(barrier, len(OFFSETS))
    for place in range(EARLY - 1):
        send(place)
    for place in range(EARLY, len(OFFSETS)):
        prepare(moved(me, OFFSETS[place]))
        send(place - 1)
    prepare(me)
    send(len(OFFSETS) - 1)
    own = [
        pltpu.make_async_copy(coded.at[me], got.at[me], own_sem.at[0]),
        pltpu.make_async_copy(scale, got_scales.at[me], own_sem.at[1]),
    ]
    for copy in own:
        copy.start()
    for copy in own + copies:
        copy.wait()


def decode_kernel(got, got_scales, out, wide, scale):
    count, rows = got.shape[0], got.shape[1]
    for source in range(count):
        scale[source : source + 1, :] = got_scales[source]

    def widen(source, carry):
        at = pl.ds(source * (rows + 1), rows)
        wide[at, :] = got[source].astype(jnp.int32).astype(jnp.float32)
        return carry

    lax.fori_loop(0, count, widen, 0)
    factor = scale[...]
    for place in range(rows):
        slot, plane, half = place // 4, (place // 2) % 2, place % 2
        value = wide[pl.ds(place, count, stride=rows + 1), :]
        out[slot, plane, :, 128 * half : 128 * half + 128] = (value * jnp.abs(value)) * factor


def on_device(field, coefficient, slot_mode, couplings):
    slabs, count = lax.axis_size("slab"), lax.axis_size("mode")
    slots, planes_here, rows_all, columns = field.shape
    entries = couplings.shape[0]
    f32, bf16, i16, i32 = jnp.float32, jnp.bfloat16, jnp.int16, jnp.int32
    dma = pltpu.SemaphoreType.DMA
    halo = 4 * CHUNKS + 2

    start, image, address, weight = pl.pallas_call(
        lambda *refs: gather_kernel(slabs, count, *refs),
        out_shape=(
            shape_of((ROWS, 128), f32),
            shape_of(((TERMS - 1) * ROWS, 128), f32),
            shape_of((1, entries), i32),
            shape_of((1, entries), f32),
        ),
        in_specs=[HBM] * 4,
        out_specs=(VMEM,) * 4,
        scratch_shapes=[
            pltpu.SMEM(slot_mode.shape, i32),
            pltpu.VMEM(field.shape, bf16),
            pltpu.VMEM(coefficient.shape, f32),
            pltpu.VMEM((4, entries), i32),
            pltpu.VMEM((count * slots * 4, 128), f32),
            pltpu.VMEM((count, slots, 4, 128), bf16),
            pltpu.VMEM((count * slots, 4, 128), bf16),
            pltpu.VMEM((ROWS, 128), f32),
            pltpu.VMEM((2, ROWS // 2, 128), f32),
            pltpu.VMEM((8, 128), i32),
            pltpu.SMEM((8, 128), i32),
            pltpu.VMEM((ROWS, 128), bf16),
            pltpu.VMEM((2, ROWS // 2, 128), bf16),
            pltpu.VMEM((ROWS, 128), bf16),
            pltpu.VMEM((ROWS, 128), bf16),
            pltpu.VMEM((ROWS // 2, 128), bf16),
            pltpu.VMEM((ROWS // 2, 128), bf16),
            pltpu.VMEM((3, TERMS, 8, 128), f32),
            pltpu.VMEM((TERMS, 8, 128), f32),
            pltpu.VMEM((TERMS, 8, 128), f32),
            pltpu.VMEM((6 * TERMS, 8, 128), f32),
            pltpu.VMEM((ROWS, 128), f32),
            pltpu.VMEM((ROWS, 128), f32),
            pltpu.VMEM((ROWS, 128), f32),
            dma((7,)),
            dma((2,)),
            dma((len(OFFSETS),)),
            dma((len(OFFSETS),)),
            dma((halo,)),
            dma((halo,)),
        ],
        compiler_params=pltpu.CompilerParams(collective_id=0, has_side_effects=True, vmem_limit_bytes=30 * MIB),
        name="gather",
    )(*(pltpu.with_memory_space_constraint(value, pltpu.HBM) for value in (slot_mode, field, coefficient, couplings.T)))

    sums = pl.pallas_call(
        apply_kernel,
        out_shape=(shape_of((ROWS, 128), f32),) * LANES,
        in_specs=[SMEM] * 2 + [VMEM] * 2,
        out_specs=(VMEM,) * LANES,
        input_output_aliases={2: 0},
        compiler_params=pltpu.CompilerParams(vmem_limit_bytes=16 * MIB),
        name="apply",
    )(address, weight, start, image)

    got, got_scales = pl.pallas_call(
        lambda *refs: return_kernel(count, *refs),
        out_shape=(shape_of((count, slots * 4, 128), i16), shape_of((count, 1, 128), f32)),
        in_specs=[SMEM] + [VMEM] * LANES,
        out_specs=(VMEM, VMEM),
        scratch_shapes=[
            pltpu.VMEM((ROWS, 128), f32),
            pltpu.VMEM((HELD, 4, 128), i32),
            pltpu.VMEM((count * slots * 4, 128), i32),
            pltpu.VMEM((count, slots * 4, 128), i16),
            pltpu.VMEM((1, 128), f32),
            dma((2,)),
            dma((2, len(OFFSETS))),
            dma((2, len(OFFSETS))),
        ],
        compiler_params=pltpu.CompilerParams(collective_id=2, has_side_effects=True, vmem_limit_bytes=12 * MIB),
        name="give",
    )(slot_mode, *sums)

    step = 8
    return pl.pallas_call(
        decode_kernel,
        out_shape=shape_of((slots, planes_here, rows_all, columns), f32),
        grid=(slots // step,),
        in_specs=[
            pl.BlockSpec((count, 4 * step, 128), lambda i: (0, i, 0)),
            pl.BlockSpec((count, 1, 128), lambda i: (0, 0, 0)),
        ],
        out_specs=pl.BlockSpec((step, planes_here, rows_all, columns), lambda i: (i, 0, 0, 0)),
        scratch_shapes=[pltpu.VMEM((count * (4 * step + 1), 128), f32), pltpu.VMEM((count, 128), f32)],
        compiler_params=pltpu.CompilerParams(vmem_limit_bytes=12 * MIB),
        name="decode",
    )(got, got_scales)


def solution(mesh):
    in_specs = (P("mode", "slab", None, None), P(None, "slab", None, None), P(), P())
    return jax.shard_map(
        on_device,
        mesh=mesh,
        in_specs=in_specs,
        out_specs=P("mode", "slab", None, None),
        check_vma=False,
    )
```

```python
import jax
import jax.numpy as jnp
from jax import lax
from jax.experimental import pallas as pl
from jax.experimental.pallas import tpu as pltpu
from jax.sharding import PartitionSpec as P

MODES = 495
HELD = 512
TERMS = 9
ROWS = 4 * HELD
CHUNKS = 8
USED = 496
TOP = 32700.0
SIDE = 4
MESH = pl.DeviceIdType.MESH
VMEM = pl.BlockSpec(memory_space=pltpu.VMEM)
SMEM = pl.BlockSpec(memory_space=pltpu.SMEM)
HBM = pl.BlockSpec(memory_space=pltpu.HBM)
MIB = 1024 * 1024


def far_first():
    offsets = [(x, y, core) for x in range(SIDE) for y in range(SIDE) for core in range(2)]
    hops = lambda offset: min(offset[0], SIDE - offset[0]) + min(offset[1], SIDE - offset[1])
    return sorted(offsets[1:], key=hops, reverse=True)


OFFSETS = far_first()


def shape_of(shape, dtype):
    return jax.ShapeDtypeStruct(shape, dtype)


def moved(me, offset, sign=1):
    x, y, core = me // (2 * SIDE), (me // 2) % SIDE, me % 2
    x = lax.rem(x + (sign * offset[0]) % SIDE, SIDE)
    y = lax.rem(y + (sign * offset[1]) % SIDE, SIDE)
    return (x * SIDE + y) * 2 + lax.rem(core + offset[2], 2)


def rows_at(start, size):
    return pl.ds(pl.multiple_of(start, size), size)


def plane_neighbours(centre, plane, front):
    return (
        jnp.where(front, plane, pltpu.roll(centre, 2, 0)),
        jnp.where(front, pltpu.roll(centre, 6, 0), plane),
    )


def column_neighbours(centre, second, lane):
    zero = jnp.zeros_like(centre)
    low = pltpu.roll(centre, 1, 1)
    high = pltpu.roll(centre, 127, 1)
    return (
        jnp.where(lane == 0, jnp.where(second, pltpu.roll(low, 1, 0), zero), low),
        jnp.where(lane == 127, jnp.where(second, zero, pltpu.roll(high, 7, 0)), high),
    )


def gather_kernel(
    slabs, count, slot_mode_hbm, field_hbm, coefficient_hbm, couplings_hbm,
    got, got_scales,
    slot_mode, field, coefficient, couplings, turned, blocks, raw, wide, wide_planes, found, inverse,
    held, planes, row_low, row_high, plane_low, plane_high, near, coef_low, coef_high,
    faces, plane_rows, column_low, column_high, start, image, running,
    targets, words, ranks, order, firsts, target_list, word_list, rank_list, order_list, first_list,
    total, codes, picked, coded, scale,
    load_sem, own_sem, send_sem, recv_sem, halo_send, halo_recv, give_send, give_recv,
):
    slab, me = lax.axis_index("slab"), lax.axis_index("mode")
    slots = field.shape[0]
    above = (slab, lax.rem(me + 1, count))
    below = (slab, lax.rem(me + count - 1, count))
    right = (lax.rem(slab + 1, slabs), me)
    left = (lax.rem(slab + slabs - 1, slabs), me)
    sub = lax.broadcasted_iota(jnp.int32, (8, 128), 0)
    lane = lax.broadcasted_iota(jnp.int32, (8, 128), 1)
    front = lax.rem(sub, 4) < 2
    second = lax.rem(sub, 2) == 1
    has_left = (slab > 0).astype(jnp.float32)
    has_right = (slab < slabs - 1).astype(jnp.float32)
    mask_plane = jnp.where(front, has_left, has_right)
    mask_low = (me > 0).astype(jnp.float32)
    mask_high = (me < count - 1).astype(jnp.float32)

    piece = slots // 4
    loads = [
        pltpu.make_async_copy(field_hbm.at[pl.ds(piece * part, piece)], field.at[pl.ds(piece * part, piece)], load_sem.at[part])
        for part in range(4)
    ]
    others = [
        pltpu.make_async_copy(source, target, load_sem.at[4 + place])
        for place, (source, target) in enumerate(
            ((coefficient_hbm, coefficient), (slot_mode_hbm, slot_mode), (couplings_hbm, couplings))
        )
    ]
    for load in loads + others:
        load.start()
    barrier = pltpu.get_barrier_semaphore()
    for offset in OFFSETS:
        pl.semaphore_signal(barrier, inc=1, device_id=(slab, moved(me, offset)), device_id_type=MESH)
    for peer in (right, left):
        pl.semaphore_signal(barrier, inc=1, device_id=peer, device_id_type=MESH)

    def turn(slot, carry):
        for part in range(4):
            plane, half = part // 2, part % 2
            value = field[slot, plane, :, 128 * half : 128 * half + 128].astype(jnp.float32)
            turned[pl.ds(4 * slot + part, count, stride=4 * slots), :] = value
        return carry

    for part, load in enumerate(loads):
        load.wait()
        lax.fori_loop(piece * part, piece * (part + 1), turn, 0)

    def narrow_block(row, carry):
        value = turned[rows_at(row * 4 * slots, 4 * slots), :]
        blocks[row] = value.reshape(slots, 4, 128).astype(jnp.bfloat16)
        return carry

    lax.fori_loop(0, count, narrow_block, 0)

    for load in others:
        load.wait()
    for shift in range(3):
        row = jnp.clip(me + shift - 1, 0, count - 1)
        for term in range(TERMS):
            for part in range(4):
                plane, half = part // 2, part % 2
                tile = coefficient[term, plane, rows_at(row // 8 * 8, 8), 128 * half : 128 * half + 128]
                value = pltpu.roll(tile, lax.rem(8 - row % 8, 8), 0)[0:1]
                near[shift, term, part : part + 1, :] = value
                near[shift, term, part + 4 : part + 5, :] = value

    pl.semaphore_wait(barrier, len(OFFSETS) + 2)
    copies = []
    for place, offset in enumerate(OFFSETS):
        peer = moved(me, offset)
        copy = pltpu.make_async_remote_copy(
            src_ref=blocks.at[peer],
            dst_ref=raw.at[pl.ds(me * slots, slots)],
            send_sem=send_sem.at[place],
            recv_sem=recv_sem.at[place],
            device_id=(slab, peer),
            device_id_type=MESH,
        )
        copy.start()
        copies.append(copy)
    own = pltpu.make_async_copy(blocks.at[me], raw.at[pl.ds(me * slots, slots)], own_sem.at[0])
    own.start()
    ids = sub * 128 + lane

    def moving(place, source, target):
        copy = pltpu.make_async_copy(source, target, own_sem.at[1 + place])
        copy.start()
        return copy

    entries = couplings.shape[1]
    whole, rest = entries // 128, entries % 128
    tiles = targets.shape[0] // 8
    for row in range(whole + 1):
        size = 128 if row < whole else rest
        if size:
            columns = slice(128 * row, 128 * row + size)
            targets[row : row + 1, 0:size] = couplings[0:1, columns]
            words[row : row + 1, 0:size] = (
                couplings[3:4, columns] * (8 * HELD) + (couplings[2:3, columns] - 1) * HELD + couplings[1:2, columns]
            )
    list_rows = pl.cdiv(entries, 128)
    keys = []
    for tile in range(tiles):
        place = ids + 1024 * tile
        key = targets[8 * tile : 8 * tile + 8, :] * (8 * HELD) + place
        keys.append(jnp.where(place < entries, key, (1 << 30) + place))
        targets[8 * tile : 8 * tile + 8, :] = keys[-1]
        value = words[8 * tile : 8 * tile + 8, :]
        words[8 * tile : 8 * tile + 8, :] = jnp.where(place < entries, value, 0)
    def find(step, place):
        for part in range(8):
            slot = step * 8 + part
            place = jnp.where(ids == slot_mode[slot], slot, place)
        return place

    found[...] = lax.fori_loop(0, slots * count // 8, find, jnp.zeros((8, 128), jnp.int32))
    moves = [moving(0, targets, target_list), moving(1, words, word_list)]
    sent = []

    def send(place, source, target, peer):
        copy = pltpu.make_async_remote_copy(
            src_ref=source,
            dst_ref=target,
            send_sem=halo_send.at[place],
            recv_sem=halo_recv.at[place],
            device_id=peer,
            device_id_type=MESH,
        )
        copy.start()
        sent.append(copy)

    send(4 * CHUNKS, near.at[1], coef_low, right)
    send(4 * CHUNKS + 1, near.at[1], coef_high, left)
    own_coef = near.at[1]
    floors = (sub * (USED // 4) + lane + 1) * (8 * HELD)

    def rank(step, carry):
        for part in range(128):
            key = target_list[step, part]
            carry = tuple(
                jnp.where(value > key, count_of + 1, count_of) for value, count_of in zip(keys + [floors], carry)
            )
        return carry

    none = jnp.zeros((8, 128), jnp.int32)
    for copy in moves:
        copy.wait()
    counted = lax.fori_loop(0, list_rows, rank, (none,) * (tiles + 1))
    for tile in range(tiles):
        ranks[8 * tile : 8 * tile + 8, :] = counted[tile]
    firsts[...] = counted[tiles]
    moves = [moving(2, found, inverse)]
    for copy in sent:
        copy.wait()
    sent.clear()

    for term in range(TERMS):
        middle = own_coef[term]
        outer = jnp.where(front, pltpu.roll(coef_low[term], 6, 0), pltpu.roll(coef_high[term], 2, 0)) * mask_plane
        around = plane_neighbours(middle, outer, front) + column_neighbours(middle, second, lane)
        around = around + (near[0, term] * mask_low, near[2, term] * mask_high)
        for place, value in enumerate(around):
            faces[6 * term + place] = 0.5 * (middle + value)

    moves += [moving(3, ranks, rank_list), moving(4, firsts, first_list)]
    for copy in moves:
        copy.wait()

    def arrange(step, carry):
        for part in range(128):
            place, word = rank_list[step, part], word_list[step, part]
            carry = tuple(
                jnp.where(spot == place, word, value) for spot, value in zip(spots, carry)
            )
        return carry

    spots = [ids + 1024 * tile for tile in range(tiles)]
    arranged = lax.fori_loop(0, list_rows, arrange, (none,) * tiles)
    for tile in range(tiles):
        order[8 * tile : 8 * tile + 8, :] = arranged[tile]
    own.wait()
    for copy in copies:
        copy.wait()

    ends = [min(chunk * HELD // CHUNKS, USED) for chunk in range(CHUNKS + 1)]

    def pick(step, carry):
        for part in range(8):
            mode = step * 8 + part
            source = inverse[lax.shift_right_logical(step, 4), lax.bitwise_and(step, 15) * 8 + part]
            value = raw[source].astype(jnp.float32)
            wide[rows_at(4 * mode, 4), :] = value
            wide_planes[0, rows_at(2 * mode, 2), :] = value[0:2]
            wide_planes[1, rows_at(2 * mode, 2), :] = value[2:4]
        return carry

    def narrow(step, carry):
        at = rows_at(step * 64, 64)
        held[at, :] = wide[at, :].astype(jnp.bfloat16)
        at = rows_at(step * 32, 32)
        planes[0, at, :] = wide_planes[0, at, :].astype(jnp.bfloat16)
        planes[1, at, :] = wide_planes[1, at, :].astype(jnp.bfloat16)
        return carry

    def send_chunk(chunk):
        low, size = ends[chunk], ends[chunk + 1] - ends[chunk]
        at, half = pl.ds(4 * low, 4 * size), pl.ds(2 * low, 2 * size)
        send(4 * chunk, held.at[at], row_low.at[at], above)
        send(4 * chunk + 1, held.at[at], row_high.at[at], below)
        send(4 * chunk + 2, planes.at[1, half], plane_low.at[half], right)
        send(4 * chunk + 3, planes.at[0, half], plane_high.at[half], left)

    def shift_columns(step, carry):
        value = wide[rows_at(step * 64, 64), :]
        around = [column_neighbours(value[8 * part : 8 * part + 8], second, lane) for part in range(8)]
        for part, (low, high) in enumerate(around):
            at = rows_at(step * 64 + 8 * part, 8)
            column_low[at, :] = low
            column_high[at, :] = high
        return carry

    for chunk in range(CHUNKS):
        lax.fori_loop(ends[chunk] // 8, ends[chunk + 1] // 8, pick, 0)
        lax.fori_loop(ends[chunk] // 16, ends[chunk + 1] // 16, narrow, 0)
        if chunk:
            send_chunk(chunk - 1)
    lax.fori_loop(0, 4, shift_columns, 0)
    send_chunk(CHUNKS - 1)
    lax.fori_loop(4, USED // 16, shift_columns, 0)

    ordered = moving(5, order, order_list)

    def interleave(step, carry):
        at = rows_at(step * 16, 16)
        low = plane_low[at, :].astype(jnp.float32) * has_left
        high = plane_high[at, :].astype(jnp.float32) * has_right
        for part in range(8):
            base = pl.multiple_of(step * 32 + 4 * part, 4)
            plane_rows[pl.ds(base, 2), :] = low[2 * part : 2 * part + 2]
            plane_rows[pl.ds(base + 2, 2), :] = high[2 * part : 2 * part + 2]
        return carry

    def stencil(step, carry):
        at = rows_at(step * 16, 16)
        low = row_low[at, :].astype(jnp.float32)
        high = row_high[at, :].astype(jnp.float32)
        halves = []
        for half in range(2):
            part = slice(8 * half, 8 * half + 8)
            base = pl.multiple_of(step * 16 + 8 * half, 8)
            at = pl.ds(base, 8)
            middle = wide[at, :]
            around = plane_neighbours(middle, plane_rows[at, :], front) + (column_low[at, :], column_high[at, :])
            around = around + (low[part] * mask_low, high[part] * mask_high)
            halves.append((base, 2 * half, [middle - value for value in around]))
        for term in range(TERMS):
            face = [faces[6 * term + place] for place in range(6)]
            for base, base_mode, drops in halves:
                total = face[0] * drops[0]
                for place in range(1, 6):
                    total = total + face[place] * drops[place]
                if term == 0:
                    start[pl.ds(base, 8), :] = total
                else:
                    at = (term - 1) * HELD + step * 4 + base_mode
                    image[pl.ds(at, 2)] = total.reshape(2, 4, 128)
        return carry

    for chunk in range(CHUNKS):
        for copy in sent[4 * chunk : 4 * chunk + 4]:
            copy.wait()
        lax.fori_loop(ends[chunk] // 8, ends[chunk + 1] // 8, interleave, 0)
        lax.fori_loop(ends[chunk] // 4, ends[chunk + 1] // 4, stencil, 0)

    def couple(step, carry):
        values = []
        for part in range(128):
            word = order_list[step, part]
            weight = jnp.full((4, 128), lax.shift_right_arithmetic(word, 12), jnp.int32).astype(jnp.float32)
            value = image[lax.bitwise_and(word, 8 * HELD - 1)]
            values.append((weight * 0.125) * value)
        for part in range(0, 128, 4):
            one, two, three, four = values[part : part + 4]
            pair = one + two
            at = step * 128 + part
            running[at] = carry
            running[at + 1] = carry + one
            running[at + 2] = carry + pair
            running[at + 3] = carry + (pair + three)
            carry = carry + (pair + (three + four))
        return carry

    ordered.wait()
    running[128 * list_rows] = lax.fori_loop(0, list_rows, couple, jnp.zeros((4, 128), jnp.float32))

    def spread(step, below_it):
        for part in range(USED // 4):
            mode = step * (USED // 4) + part
            at = first_list[step, part]
            up_to = running[at]
            rows = rows_at(4 * mode, 4)
            total[rows, :] = start[rows, :] + (up_to - below_it)
            below_it = up_to
        return below_it

    lax.fori_loop(0, 4, spread, jnp.zeros((4, 128), jnp.float32))

    def largest(step, top):
        size = jnp.abs(total[rows_at(step * 32, 32), :])
        return jnp.maximum(top, jnp.maximum(jnp.maximum(size[0:8], size[8:16]), jnp.maximum(size[16:24], size[24:32])))

    total[4 * MODES : 4 * MODES + 4, :] = jnp.zeros((4, 128), jnp.float32)
    top = lax.fori_loop(0, USED // 8, largest, jnp.zeros((8, 128), jnp.float32))
    top = jnp.max(jnp.max(top, axis=0, keepdims=True), axis=1, keepdims=True)
    top = jnp.broadcast_to(top, (1, 128))
    scale[...] = top * (1.0 / (TOP * TOP))
    factor = TOP * lax.rsqrt(jnp.maximum(top, 1e-37))

    def encode(step, carry):
        value = total[rows_at(step * 32, 32), :]
        root = value * lax.rsqrt(jnp.maximum(jnp.abs(value), 1e-37))
        code = jnp.round(root * factor).astype(jnp.int32)
        codes[pl.ds(step * 8, 8)] = code.reshape(8, 4, 128)
        return carry

    lax.fori_loop(0, USED // 8, encode, 0)

    def prepare(group):
        def pick_codes(step, carry):
            for part in range(8):
                slot = group * slots + step * 8 + part
                picked[rows_at(4 * slot, 4), :] = codes[slot_mode[slot]]
            return carry

        lax.fori_loop(0, slots // 8, pick_codes, 0)
        for part in range(4):
            at = rows_at(group * 4 * slots + slots * part, slots)
            coded[group, slots * part : slots * (part + 1), :] = picked[at, :].astype(jnp.int16)

    copies = []

    def give(place):
        peer = moved(me, OFFSETS[place])
        for kind, (source, target) in enumerate(((coded.at[peer], got), (scale, got_scales))):
            copy = pltpu.make_async_remote_copy(
                src_ref=source,
                dst_ref=target.at[me],
                send_sem=give_send.at[kind, place],
                recv_sem=give_recv.at[kind, place],
                device_id=(slab, peer),
                device_id_type=MESH,
            )
            copy.start()
            copies.append(copy)

    prepare(moved(me, OFFSETS[0]))
    for place in range(1, len(OFFSETS)):
        prepare(moved(me, OFFSETS[place]))
        give(place - 1)
    prepare(me)
    give(len(OFFSETS) - 1)
    own = [
        pltpu.make_async_copy(coded.at[me], got.at[me], own_sem.at[7]),
        pltpu.make_async_copy(scale, got_scales.at[me], own_sem.at[8]),
    ]
    for copy in own:
        copy.start()
    for copy in own + copies:
        copy.wait()


def decode_kernel(got, got_scales, out, wide, scale):
    count, rows = got.shape[0], got.shape[1]
    for source in range(count):
        scale[source : source + 1, :] = got_scales[source]

    def widen(source, carry):
        at = pl.ds(source * (rows + 1), rows)
        wide[at, :] = got[source].astype(jnp.int32).astype(jnp.float32)
        return carry

    lax.fori_loop(0, count, widen, 0)
    factor = scale[...]
    for place in range(rows):
        slot, plane, half = place // 4, (place // 2) % 2, place % 2
        value = wide[pl.ds(place, count, stride=rows + 1), :]
        out[slot, plane, :, 128 * half : 128 * half + 128] = (value * jnp.abs(value)) * factor


def on_device(field, coefficient, slot_mode, couplings):
    slabs, count = lax.axis_size("slab"), lax.axis_size("mode")
    slots, planes_here, rows_all, columns = field.shape
    entries = couplings.shape[0]
    f32, bf16, i16, i32 = jnp.float32, jnp.bfloat16, jnp.int16, jnp.int32
    dma = pltpu.SemaphoreType.DMA
    halo = 4 * CHUNKS + 2
    places = pl.cdiv(entries, 1024) * 8

    got, got_scales = pl.pallas_call(
        lambda *refs: gather_kernel(slabs, count, *refs),
        out_shape=(shape_of((count, slots * 4, 128), i16), shape_of((count, 1, 128), f32)),
        in_specs=[HBM] * 4,
        out_specs=(VMEM,) * 2,
        scratch_shapes=[
            pltpu.SMEM(slot_mode.shape, i32),
            pltpu.VMEM(field.shape, bf16),
            pltpu.VMEM(coefficient.shape, f32),
            pltpu.VMEM((4, entries), i32),
            pltpu.VMEM((count * slots * 4, 128), f32),
            pltpu.VMEM((count, slots, 4, 128), bf16),
            pltpu.VMEM((count * slots, 4, 128), bf16),
            pltpu.VMEM((ROWS, 128), f32),
            pltpu.VMEM((2, ROWS // 2, 128), f32),
            pltpu.VMEM((8, 128), i32),
            pltpu.SMEM((8, 128), i32),
            pltpu.VMEM((ROWS, 128), bf16),
            pltpu.VMEM((2, ROWS // 2, 128), bf16),
            pltpu.VMEM((ROWS, 128), bf16),
            pltpu.VMEM((ROWS, 128), bf16),
            pltpu.VMEM((ROWS // 2, 128), bf16),
            pltpu.VMEM((ROWS // 2, 128), bf16),
            pltpu.VMEM((3, TERMS, 8, 128), f32),
            pltpu.VMEM((TERMS, 8, 128), f32),
            pltpu.VMEM((TERMS, 8, 128), f32),
            pltpu.VMEM((6 * TERMS, 8, 128), f32),
            pltpu.VMEM((ROWS, 128), f32),
            pltpu.VMEM((ROWS, 128), f32),
            pltpu.VMEM((ROWS, 128), f32),
            pltpu.VMEM((ROWS, 128), f32),
            pltpu.VMEM(((TERMS - 1) * HELD, 4, 128), f32),
            pltpu.VMEM((128 * pl.cdiv(entries, 128) + 8, 4, 128), f32),
        ]
        + [pltpu.VMEM((places, 128), i32)] * 4
        + [pltpu.VMEM((8, 128), i32)]
        + [pltpu.SMEM((places, 128), i32)] * 4
        + [
            pltpu.SMEM((8, 128), i32),
            pltpu.VMEM((ROWS, 128), f32),
            pltpu.VMEM((HELD, 4, 128), i32),
            pltpu.VMEM((count * slots * 4, 128), i32),
            pltpu.VMEM((count, slots * 4, 128), i16),
            pltpu.VMEM((1, 128), f32),
            dma((7,)),
            dma((9,)),
            dma((len(OFFSETS),)),
            dma((len(OFFSETS),)),
            dma((halo,)),
            dma((halo,)),
            dma((2, len(OFFSETS))),
            dma((2, len(OFFSETS))),
        ],
        compiler_params=pltpu.CompilerParams(collective_id=0, has_side_effects=True, vmem_limit_bytes=48 * MIB),
        name="gather",
    )(*(pltpu.with_memory_space_constraint(value, pltpu.HBM) for value in (slot_mode, field, coefficient, couplings.T)))

    step = 8
    return pl.pallas_call(
        decode_kernel,
        out_shape=shape_of((slots, planes_here, rows_all, columns), f32),
        grid=(slots // step,),
        in_specs=[
            pl.BlockSpec((count, 4 * step, 128), lambda i: (0, i, 0)),
            pl.BlockSpec((count, 1, 128), lambda i: (0, 0, 0)),
        ],
        out_specs=pl.BlockSpec((step, planes_here, rows_all, columns), lambda i: (i, 0, 0, 0)),
        scratch_shapes=[pltpu.VMEM((count * (4 * step + 1), 128), f32), pltpu.VMEM((count, 128), f32)],
        compiler_params=pltpu.CompilerParams(vmem_limit_bytes=12 * MIB),
        name="decode",
    )(got, got_scales)


def solution(mesh):
    in_specs = (P("mode", "slab", None, None), P(None, "slab", None, None), P(), P())
    return jax.shard_map(
        on_device,
        mesh=mesh,
        in_specs=in_specs,
        out_specs=P("mode", "slab", None, None),
        check_vma=False,
    )
```

```python
import jax
import jax.numpy as jnp
from jax import lax
from jax.experimental import pallas as pl
from jax.experimental.pallas import tpu as pltpu
from jax.sharding import PartitionSpec as P

MODES = 495
HELD = 512
TERMS = 9
ROWS = 4 * HELD
CHUNKS = 8
USED = 496
LIST_ROWS = 21
SPREAD = 99
TOP = 32700.0
SIDE = 4
MESH = pl.DeviceIdType.MESH
VMEM = pl.BlockSpec(memory_space=pltpu.VMEM)
SMEM = pl.BlockSpec(memory_space=pltpu.SMEM)
HBM = pl.BlockSpec(memory_space=pltpu.HBM)
MIB = 1024 * 1024


def far_first():
    offsets = [(x, y, core) for x in range(SIDE) for y in range(SIDE) for core in range(2)]
    hops = lambda offset: min(offset[0], SIDE - offset[0]) + min(offset[1], SIDE - offset[1])
    return sorted(offsets[1:], key=hops, reverse=True)


OFFSETS = far_first()


def shape_of(shape, dtype):
    return jax.ShapeDtypeStruct(shape, dtype)


def moved(me, offset, sign=1):
    x, y, core = me // (2 * SIDE), (me // 2) % SIDE, me % 2
    x = lax.rem(x + (sign * offset[0]) % SIDE, SIDE)
    y = lax.rem(y + (sign * offset[1]) % SIDE, SIDE)
    return (x * SIDE + y) * 2 + lax.rem(core + offset[2], 2)


def rows_at(start, size):
    return pl.ds(pl.multiple_of(start, size), size)


def plane_neighbours(centre, plane, front):
    return (
        jnp.where(front, plane, pltpu.roll(centre, 2, 0)),
        jnp.where(front, pltpu.roll(centre, 6, 0), plane),
    )


def column_neighbours(centre, second, lane):
    zero = jnp.zeros_like(centre)
    low = pltpu.roll(centre, 1, 1)
    high = pltpu.roll(centre, 127, 1)
    return (
        jnp.where(lane == 0, jnp.where(second, pltpu.roll(low, 1, 0), zero), low),
        jnp.where(lane == 127, jnp.where(second, zero, pltpu.roll(high, 7, 0)), high),
    )


def gather_kernel(
    slabs, count, slot_mode_hbm, field_hbm, coefficient_hbm, couplings_hbm,
    got, got_scales,
    slot_mode, field, coefficient, couplings, turned, blocks, raw, wide, wide_planes, found, inverse,
    held, planes, row_low, row_high, plane_low, plane_high, near, coef_low, coef_high,
    faces, plane_rows, column_low, column_high, start, image, running,
    targets, words, ranks, order, firsts, target_list, word_list, rank_list, first_list,
    total, codes, picked, coded, scale,
    load_sem, own_sem, send_sem, recv_sem, halo_send, halo_recv, give_send, give_recv, *order_lists,
):
    slab, me = lax.axis_index("slab"), lax.axis_index("mode")
    slots = field.shape[0]
    above = (slab, lax.rem(me + 1, count))
    below = (slab, lax.rem(me + count - 1, count))
    right = (lax.rem(slab + 1, slabs), me)
    left = (lax.rem(slab + slabs - 1, slabs), me)
    sub = lax.broadcasted_iota(jnp.int32, (8, 128), 0)
    lane = lax.broadcasted_iota(jnp.int32, (8, 128), 1)
    front = lax.rem(sub, 4) < 2
    second = lax.rem(sub, 2) == 1
    has_left = (slab > 0).astype(jnp.float32)
    has_right = (slab < slabs - 1).astype(jnp.float32)
    mask_plane = jnp.where(front, has_left, has_right)
    mask_low = (me > 0).astype(jnp.float32)
    mask_high = (me < count - 1).astype(jnp.float32)

    piece = slots // 4
    loads = [
        pltpu.make_async_copy(field_hbm.at[pl.ds(piece * part, piece)], field.at[pl.ds(piece * part, piece)], load_sem.at[part])
        for part in range(4)
    ]
    others = [
        pltpu.make_async_copy(source, target, load_sem.at[4 + place])
        for place, (source, target) in enumerate(
            ((coefficient_hbm, coefficient), (slot_mode_hbm, slot_mode), (couplings_hbm, couplings))
        )
    ]
    for load in loads + others:
        load.start()
    barrier = pltpu.get_barrier_semaphore()
    for offset in OFFSETS:
        pl.semaphore_signal(barrier, inc=1, device_id=(slab, moved(me, offset)), device_id_type=MESH)
    for peer in (right, left):
        pl.semaphore_signal(barrier, inc=1, device_id=peer, device_id_type=MESH)

    def turn(slot, carry):
        for part in range(4):
            plane, half = part // 2, part % 2
            value = field[slot, plane, :, 128 * half : 128 * half + 128].astype(jnp.float32)
            turned[pl.ds(4 * slot + part, count, stride=4 * slots), :] = value
        return carry

    for part, load in enumerate(loads):
        load.wait()
        lax.fori_loop(piece * part, piece * (part + 1), turn, 0)

    def narrow_block(row, carry):
        value = turned[rows_at(row * 4 * slots, 4 * slots), :]
        blocks[row] = value.reshape(slots, 4, 128).astype(jnp.bfloat16)
        return carry

    lax.fori_loop(0, count, narrow_block, 0)

    for load in others:
        load.wait()
    for shift in range(3):
        row = jnp.clip(me + shift - 1, 0, count - 1)
        for term in range(TERMS):
            for part in range(4):
                plane, half = part // 2, part % 2
                tile = coefficient[term, plane, rows_at(row // 8 * 8, 8), 128 * half : 128 * half + 128]
                value = pltpu.roll(tile, lax.rem(8 - row % 8, 8), 0)[0:1]
                near[shift, term, part : part + 1, :] = value
                near[shift, term, part + 4 : part + 5, :] = value

    pl.semaphore_wait(barrier, len(OFFSETS) + 2)
    copies = []
    for place, offset in enumerate(OFFSETS):
        peer = moved(me, offset)
        copy = pltpu.make_async_remote_copy(
            src_ref=blocks.at[peer],
            dst_ref=raw.at[pl.ds(me * slots, slots)],
            send_sem=send_sem.at[place],
            recv_sem=recv_sem.at[place],
            device_id=(slab, peer),
            device_id_type=MESH,
        )
        copy.start()
        copies.append(copy)
    own = pltpu.make_async_copy(blocks.at[me], raw.at[pl.ds(me * slots, slots)], own_sem.at[0])
    own.start()
    ids = sub * 128 + lane

    def moving(place, source, target):
        copy = pltpu.make_async_copy(source, target, own_sem.at[1 + place])
        copy.start()
        return copy

    entries = couplings.shape[1]
    whole, rest = entries // 128, entries % 128
    tiles = targets.shape[0] // 8
    for row in range(whole + 1):
        size = 128 if row < whole else rest
        if size:
            columns = slice(128 * row, 128 * row + size)
            targets[row : row + 1, 0:size] = couplings[0:1, columns]
            words[row : row + 1, 0:size] = (
                couplings[3:4, columns] * (8 * HELD) + (couplings[2:3, columns] - 1) * HELD + couplings[1:2, columns]
            )
    keys = []
    for tile in range(tiles):
        place = ids + 1024 * tile
        key = targets[8 * tile : 8 * tile + 8, :] * (8 * HELD) + place
        keys.append(jnp.where(place < entries, key, (1 << 30) + place))
        targets[8 * tile : 8 * tile + 8, :] = keys[-1]
        value = words[8 * tile : 8 * tile + 8, :]
        words[8 * tile : 8 * tile + 8, :] = jnp.where(place < entries, value, 0)
    def find(step, place):
        for part in range(8):
            slot = step * 8 + part
            place = jnp.where(ids == slot_mode[slot], slot, place)
        return place

    found[...] = lax.fori_loop(0, slots * count // 8, find, jnp.zeros((8, 128), jnp.int32))
    moves = [moving(0, targets, target_list), moving(1, words, word_list)]
    sent = []

    def send(place, source, target, peer):
        copy = pltpu.make_async_remote_copy(
            src_ref=source,
            dst_ref=target,
            send_sem=halo_send.at[place],
            recv_sem=halo_recv.at[place],
            device_id=peer,
            device_id_type=MESH,
        )
        copy.start()
        sent.append(copy)

    send(4 * CHUNKS, near.at[1], coef_low, right)
    send(4 * CHUNKS + 1, near.at[1], coef_high, left)
    own_coef = near.at[1]
    floors = (sub * SPREAD + lane + 1) * (8 * HELD)

    def rank(step, carry):
        for part in range(128):
            key = target_list[step, part]
            carry = tuple(
                jnp.where(value > key, count_of + 1, count_of) for value, count_of in zip(keys + [floors], carry)
            )
        return carry

    none = jnp.zeros((8, 128), jnp.int32)
    for copy in moves:
        copy.wait()
    counted = lax.fori_loop(0, LIST_ROWS, rank, (none,) * (tiles + 1))
    for tile in range(tiles):
        ranks[8 * tile : 8 * tile + 8, :] = counted[tile]
    firsts[...] = counted[tiles]
    moves = [moving(2, found, inverse)]
    for copy in sent:
        copy.wait()
    sent.clear()

    for term in range(TERMS):
        middle = own_coef[term]
        outer = jnp.where(front, pltpu.roll(coef_low[term], 6, 0), pltpu.roll(coef_high[term], 2, 0)) * mask_plane
        around = plane_neighbours(middle, outer, front) + column_neighbours(middle, second, lane)
        around = around + (near[0, term] * mask_low, near[2, term] * mask_high)
        for place, value in enumerate(around):
            faces[6 * term + place] = 0.5 * (middle + value)

    moves += [moving(3, ranks, rank_list), moving(4, firsts, first_list)]
    for copy in moves:
        copy.wait()

    def arrange(step, carry):
        for part in range(128):
            place, word = rank_list[step, part], word_list[step, part]
            carry = tuple(
                jnp.where(spot == place, word, value) for spot, value in zip(spots, carry)
            )
        return carry

    spots = []
    for tile in range(tiles):
        row = sub + 8 * tile
        spots.append(jnp.where(row < LIST_ROWS, lane * LIST_ROWS + row, -1))
    arranged = lax.fori_loop(0, LIST_ROWS, arrange, (none,) * tiles)
    for tile in range(tiles):
        order[8 * tile : 8 * tile + 8, :] = arranged[tile]
    own.wait()
    for copy in copies:
        copy.wait()

    ends = [min(chunk * HELD // CHUNKS, USED) for chunk in range(CHUNKS + 1)]

    def pick(step, carry):
        for part in range(8):
            mode = step * 8 + part
            source = inverse[lax.shift_right_logical(step, 4), lax.bitwise_and(step, 15) * 8 + part]
            value = raw[source].astype(jnp.float32)
            wide[rows_at(4 * mode, 4), :] = value
            wide_planes[0, rows_at(2 * mode, 2), :] = value[0:2]
            wide_planes[1, rows_at(2 * mode, 2), :] = value[2:4]
        return carry

    def narrow(step, carry):
        at = rows_at(step * 64, 64)
        held[at, :] = wide[at, :].astype(jnp.bfloat16)
        at = rows_at(step * 32, 32)
        planes[0, at, :] = wide_planes[0, at, :].astype(jnp.bfloat16)
        planes[1, at, :] = wide_planes[1, at, :].astype(jnp.bfloat16)
        return carry

    def send_chunk(chunk):
        low, size = ends[chunk], ends[chunk + 1] - ends[chunk]
        at, half = pl.ds(4 * low, 4 * size), pl.ds(2 * low, 2 * size)
        send(4 * chunk, held.at[at], row_low.at[at], above)
        send(4 * chunk + 1, held.at[at], row_high.at[at], below)
        send(4 * chunk + 2, planes.at[1, half], plane_low.at[half], right)
        send(4 * chunk + 3, planes.at[0, half], plane_high.at[half], left)

    def shift_columns(step, carry):
        value = wide[rows_at(step * 64, 64), :]
        around = [column_neighbours(value[8 * part : 8 * part + 8], second, lane) for part in range(8)]
        for part, (low, high) in enumerate(around):
            at = rows_at(step * 64 + 8 * part, 8)
            column_low[at, :] = low
            column_high[at, :] = high
        return carry

    for chunk in range(CHUNKS):
        lax.fori_loop(ends[chunk] // 8, ends[chunk + 1] // 8, pick, 0)
        lax.fori_loop(ends[chunk] // 16, ends[chunk + 1] // 16, narrow, 0)
        if chunk:
            send_chunk(chunk - 1)
    lax.fori_loop(0, 4, shift_columns, 0)
    send_chunk(CHUNKS - 1)
    lax.fori_loop(4, USED // 16, shift_columns, 0)

    ordered = [moving(5 + row, order.at[row : row + 1], order_lists[row]) for row in range(LIST_ROWS)]

    def interleave(step, carry):
        at = rows_at(step * 16, 16)
        low = plane_low[at, :].astype(jnp.float32) * has_left
        high = plane_high[at, :].astype(jnp.float32) * has_right
        for part in range(8):
            base = pl.multiple_of(step * 32 + 4 * part, 4)
            plane_rows[pl.ds(base, 2), :] = low[2 * part : 2 * part + 2]
            plane_rows[pl.ds(base + 2, 2), :] = high[2 * part : 2 * part + 2]
        return carry

    def stencil(step, carry):
        at = rows_at(step * 16, 16)
        low = row_low[at, :].astype(jnp.float32)
        high = row_high[at, :].astype(jnp.float32)
        halves = []
        for half in range(2):
            part = slice(8 * half, 8 * half + 8)
            base = pl.multiple_of(step * 16 + 8 * half, 8)
            at = pl.ds(base, 8)
            middle = wide[at, :]
            around = plane_neighbours(middle, plane_rows[at, :], front) + (column_low[at, :], column_high[at, :])
            around = around + (low[part] * mask_low, high[part] * mask_high)
            halves.append((base, 2 * half, [middle - value for value in around]))
        for term in range(TERMS):
            face = [faces[6 * term + place] for place in range(6)]
            for base, base_mode, drops in halves:
                total = face[0] * drops[0]
                for place in range(1, 6):
                    total = total + face[place] * drops[place]
                if term == 0:
                    start[pl.ds(base, 8), :] = total
                else:
                    at = (term - 1) * HELD + step * 4 + base_mode
                    image[pl.ds(at, 2)] = total.reshape(2, 4, 128)
        return carry

    for chunk in range(CHUNKS):
        for copy in sent[4 * chunk : 4 * chunk + 4]:
            copy.wait()
        lax.fori_loop(ends[chunk] // 8, ends[chunk + 1] // 8, interleave, 0)
        lax.fori_loop(ends[chunk] // 4, ends[chunk + 1] // 4, stencil, 0)

    def couple(step, carry):
        for lot in range(2):
            column = 2 * step + lot
            values = []
            for part in range(LIST_ROWS):
                word = order_lists[part][0, column]
                weight = lax.shift_right_arithmetic(jnp.full((4, 128), word, jnp.int32), 12).astype(jnp.float32)
                value = image[lax.bitwise_and(word, 8 * HELD - 1)]
                values.append((weight * 0.125) * value)
            for part in range(0, LIST_ROWS, 3):
                one, two, three = values[part : part + 3]
                at = column * LIST_ROWS + part
                running[at] = carry
                running[at + 1] = carry + one
                running[at + 2] = carry + (one + two)
                carry = carry + (one + two + three)
        return carry

    for copy in ordered:
        copy.wait()
    running[128 * LIST_ROWS] = lax.fori_loop(0, 64, couple, jnp.zeros((4, 128), jnp.float32))

    def spread(step, carry):
        below_it, top = carry
        for part in range(SPREAD):
            up_to = running[first_list[step, part]]
            rows = rows_at(4 * (step * SPREAD + part), 4)
            value = start[rows, :] + (up_to - below_it)
            total[rows, :] = value
            below_it = up_to
            top = jnp.maximum(top, jnp.abs(value))
        return below_it, top

    blank = jnp.zeros((4, 128), jnp.float32)
    top = lax.fori_loop(0, MODES // SPREAD, spread, (blank, blank))[1]
    total[4 * MODES : 4 * MODES + 4, :] = blank
    top = jnp.max(jnp.max(top, axis=0, keepdims=True), axis=1, keepdims=True)
    top = jnp.broadcast_to(top, (1, 128))
    scale[...] = top * (1.0 / (TOP * TOP))
    factor = TOP * lax.rsqrt(jnp.maximum(top, 1e-37))

    def encode(step, carry):
        value = total[rows_at(step * 32, 32), :]
        root = value * lax.rsqrt(jnp.maximum(jnp.abs(value), 1e-37))
        code = jnp.round(root * factor).astype(jnp.int32)
        codes[pl.ds(step * 8, 8)] = code.reshape(8, 4, 128)
        return carry

    lax.fori_loop(0, USED // 8, encode, 0)

    def prepare(group):
        def pick_codes(step, carry):
            for part in range(8):
                slot = group * slots + step * 8 + part
                picked[rows_at(4 * slot, 4), :] = codes[slot_mode[slot]]
            return carry

        lax.fori_loop(0, slots // 8, pick_codes, 0)
        for part in range(4):
            at = rows_at(group * 4 * slots + slots * part, slots)
            coded[group, slots * part : slots * (part + 1), :] = picked[at, :].astype(jnp.int16)

    copies = []

    def give(place):
        peer = moved(me, OFFSETS[place])
        for kind, (source, target) in enumerate(((coded.at[peer], got), (scale, got_scales))):
            copy = pltpu.make_async_remote_copy(
                src_ref=source,
                dst_ref=target.at[me],
                send_sem=give_send.at[kind, place],
                recv_sem=give_recv.at[kind, place],
                device_id=(slab, peer),
                device_id_type=MESH,
            )
            copy.start()
            copies.append(copy)

    prepare(moved(me, OFFSETS[0]))
    for place in range(1, len(OFFSETS)):
        prepare(moved(me, OFFSETS[place]))
        give(place - 1)
    prepare(me)
    give(len(OFFSETS) - 1)
    own = [
        pltpu.make_async_copy(coded.at[me], got.at[me], own_sem.at[6 + LIST_ROWS]),
        pltpu.make_async_copy(scale, got_scales.at[me], own_sem.at[7 + LIST_ROWS]),
    ]
    for copy in own:
        copy.start()
    for copy in own + copies:
        copy.wait()


def decode_kernel(got, got_scales, out, wide, scale):
    count, rows = got.shape[0], got.shape[1]
    for source in range(count):
        scale[source : source + 1, :] = got_scales[source]

    def widen(source, carry):
        at = pl.ds(source * (rows + 1), rows)
        wide[at, :] = got[source].astype(jnp.int32).astype(jnp.float32)
        return carry

    lax.fori_loop(0, count, widen, 0)
    factor = scale[...]
    for place in range(rows):
        slot, plane, half = place // 4, (place // 2) % 2, place % 2
        value = wide[pl.ds(place, count, stride=rows + 1), :]
        out[slot, plane, :, 128 * half : 128 * half + 128] = (value * jnp.abs(value)) * factor


def on_device(field, coefficient, slot_mode, couplings):
    slabs, count = lax.axis_size("slab"), lax.axis_size("mode")
    slots, planes_here, rows_all, columns = field.shape
    entries = couplings.shape[0]
    f32, bf16, i16, i32 = jnp.float32, jnp.bfloat16, jnp.int16, jnp.int32
    dma = pltpu.SemaphoreType.DMA
    halo = 4 * CHUNKS + 2
    places = pl.cdiv(entries, 1024) * 8

    got, got_scales = pl.pallas_call(
        lambda *refs: gather_kernel(slabs, count, *refs),
        out_shape=(shape_of((count, slots * 4, 128), i16), shape_of((count, 1, 128), f32)),
        in_specs=[HBM] * 4,
        out_specs=(VMEM,) * 2,
        scratch_shapes=[
            pltpu.SMEM(slot_mode.shape, i32),
            pltpu.VMEM(field.shape, bf16),
            pltpu.VMEM(coefficient.shape, f32),
            pltpu.VMEM((4, entries), i32),
            pltpu.VMEM((count * slots * 4, 128), f32),
            pltpu.VMEM((count, slots, 4, 128), bf16),
            pltpu.VMEM((count * slots, 4, 128), bf16),
            pltpu.VMEM((ROWS, 128), f32),
            pltpu.VMEM((2, ROWS // 2, 128), f32),
            pltpu.VMEM((8, 128), i32),
            pltpu.SMEM((8, 128), i32),
            pltpu.VMEM((ROWS, 128), bf16),
            pltpu.VMEM((2, ROWS // 2, 128), bf16),
            pltpu.VMEM((ROWS, 128), bf16),
            pltpu.VMEM((ROWS, 128), bf16),
            pltpu.VMEM((ROWS // 2, 128), bf16),
            pltpu.VMEM((ROWS // 2, 128), bf16),
            pltpu.VMEM((3, TERMS, 8, 128), f32),
            pltpu.VMEM((TERMS, 8, 128), f32),
            pltpu.VMEM((TERMS, 8, 128), f32),
            pltpu.VMEM((6 * TERMS, 8, 128), f32),
            pltpu.VMEM((ROWS, 128), f32),
            pltpu.VMEM((ROWS, 128), f32),
            pltpu.VMEM((ROWS, 128), f32),
            pltpu.VMEM((ROWS, 128), f32),
            pltpu.VMEM(((TERMS - 1) * HELD, 4, 128), f32),
            pltpu.VMEM((128 * LIST_ROWS + 8, 4, 128), f32),
        ]
        + [pltpu.VMEM((places, 128), i32)] * 4
        + [pltpu.VMEM((8, 128), i32)]
        + [pltpu.SMEM((places, 128), i32)] * 3
        + [
            pltpu.SMEM((8, 128), i32),
            pltpu.VMEM((ROWS, 128), f32),
            pltpu.VMEM((HELD, 4, 128), i32),
            pltpu.VMEM((count * slots * 4, 128), i32),
            pltpu.VMEM((count, slots * 4, 128), i16),
            pltpu.VMEM((1, 128), f32),
            dma((7,)),
            dma((8 + LIST_ROWS,)),
            dma((len(OFFSETS),)),
            dma((len(OFFSETS),)),
            dma((halo,)),
            dma((halo,)),
            dma((2, len(OFFSETS))),
            dma((2, len(OFFSETS))),
        ]
        + [pltpu.SMEM((1, 128), i32)] * LIST_ROWS,
        compiler_params=pltpu.CompilerParams(collective_id=0, has_side_effects=True, vmem_limit_bytes=48 * MIB),
        name="gather",
    )(*(pltpu.with_memory_space_constraint(value, pltpu.HBM) for value in (slot_mode, field, coefficient, couplings.T)))

    step = 8
    return pl.pallas_call(
        decode_kernel,
        out_shape=shape_of((slots, planes_here, rows_all, columns), f32),
        grid=(slots // step,),
        in_specs=[
            pl.BlockSpec((count, 4 * step, 128), lambda i: (0, i, 0)),
            pl.BlockSpec((count, 1, 128), lambda i: (0, 0, 0)),
        ],
        out_specs=pl.BlockSpec((step, planes_here, rows_all, columns), lambda i: (i, 0, 0, 0)),
        scratch_shapes=[pltpu.VMEM((count * (4 * step + 1), 128), f32), pltpu.VMEM((count, 128), f32)],
        compiler_params=pltpu.CompilerParams(vmem_limit_bytes=12 * MIB),
        name="decode",
    )(got, got_scales)


def solution(mesh):
    in_specs = (P("mode", "slab", None, None), P(None, "slab", None, None), P(), P())
    return jax.shard_map(
        on_device,
        mesh=mesh,
        in_specs=in_specs,
        out_specs=P("mode", "slab", None, None),
        check_vma=False,
    )
```

```python
import jax
import jax.numpy as jnp
from jax import lax
from jax.experimental import pallas as pl
from jax.experimental.pallas import tpu as pltpu
from jax.sharding import PartitionSpec as P

MODES = 495
HELD = 512
TERMS = 9
ROWS = 4 * HELD
STRIDE = 33
CHUNKS = 4
USED = 496
LIST_ROWS = 21
SPREAD = 99
TOP = 32700.0
SIDE = 4
MESH = pl.DeviceIdType.MESH
VMEM = pl.BlockSpec(memory_space=pltpu.VMEM)
SMEM = pl.BlockSpec(memory_space=pltpu.SMEM)
HBM = pl.BlockSpec(memory_space=pltpu.HBM)
MIB = 1024 * 1024


def far_first():
    offsets = [(x, y, core) for x in range(SIDE) for y in range(SIDE) for core in range(2)]
    hops = lambda offset: min(offset[0], SIDE - offset[0]) + min(offset[1], SIDE - offset[1])
    return sorted(offsets[1:], key=hops, reverse=True)


OFFSETS = far_first()


def shape_of(shape, dtype):
    return jax.ShapeDtypeStruct(shape, dtype)


def moved(me, offset, sign=1):
    x, y, core = me // (2 * SIDE), (me // 2) % SIDE, me % 2
    x = lax.rem(x + (sign * offset[0]) % SIDE, SIDE)
    y = lax.rem(y + (sign * offset[1]) % SIDE, SIDE)
    return (x * SIDE + y) * 2 + lax.rem(core + offset[2], 2)


def rows_at(start, size):
    return pl.ds(pl.multiple_of(start, size), size)


def column_neighbours(centre, second, lane):
    zero = jnp.zeros_like(centre)
    low = pltpu.roll(centre, 1, 1)
    high = pltpu.roll(centre, 127, 1)
    return (
        jnp.where(lane == 0, jnp.where(second, pltpu.roll(low, 1, 0), zero), low),
        jnp.where(lane == 127, jnp.where(second, zero, pltpu.roll(high, 7, 0)), high),
    )


def gather_kernel(
    slabs, count, slot_mode_hbm, field_hbm, coefficient_hbm, couplings_hbm,
    got, got_scales,
    slot_mode, field, coefficient, couplings, turned, blocks, raw, wide, found, inverse,
    planes, row_low, row_high, outer, near, coef_outer, faces, column_low, column_high, start, image, running,
    targets, words, ranks, order, firsts, target_list, word_list, rank_list, first_list,
    total, codes, picked, coded, scale,
    load_sem, own_sem, send_sem, recv_sem, halo_send, halo_recv, give_send, give_recv, *order_lists,
):
    slab, me = lax.axis_index("slab"), lax.axis_index("mode")
    core = lax.rem(me, 2)
    slots = field.shape[0]
    above = (slab, lax.rem(me + 1, count))
    below = (slab, lax.rem(me + count - 1, count))
    right = (lax.rem(slab + 1, slabs), me)
    left = (lax.rem(slab + slabs - 1, slabs), me)
    sub = lax.broadcasted_iota(jnp.int32, (8, 128), 0)
    lane = lax.broadcasted_iota(jnp.int32, (8, 128), 1)
    second = lax.rem(sub, 2) == 1
    mask_outer = [(slab > 0).astype(jnp.float32), (slab < slabs - 1).astype(jnp.float32)]
    mask_low = (me > 0).astype(jnp.float32)
    mask_high = (me < count - 1).astype(jnp.float32)

    piece = slots // 4
    loads = [
        pltpu.make_async_copy(field_hbm.at[pl.ds(piece * part, piece)], field.at[pl.ds(piece * part, piece)], load_sem.at[part])
        for part in range(4)
    ]
    others = [
        pltpu.make_async_copy(source, target, load_sem.at[4 + place])
        for place, (source, target) in enumerate(
            ((coefficient_hbm, coefficient), (slot_mode_hbm, slot_mode), (couplings_hbm, couplings))
        )
    ]
    for load in loads + others:
        load.start()
    barrier = pltpu.get_barrier_semaphore()
    for offset in OFFSETS:
        pl.semaphore_signal(barrier, inc=1, device_id=(slab, moved(me, offset)), device_id_type=MESH)
    for peer in (right, left):
        pl.semaphore_signal(barrier, inc=1, device_id=peer, device_id_type=MESH)

    def turn(slot, carry):
        for part in range(4):
            plane, half = part // 2, part % 2
            value = field[slot, plane, :, 128 * half : 128 * half + 128].astype(jnp.float32)
            turned[pl.ds(4 * slot + part, count, stride=4 * slots), :] = value
        return carry

    for part, load in enumerate(loads):
        load.wait()
        lax.fori_loop(piece * part, piece * (part + 1), turn, 0)

    def narrow_block(row, carry):
        value = turned[rows_at(row * 4 * slots, 4 * slots), :]
        blocks[row] = value.reshape(slots, 4, 128).astype(jnp.bfloat16)
        return carry

    lax.fori_loop(0, count, narrow_block, 0)

    for load in others:
        load.wait()
    for shift in range(3):
        row = jnp.clip(me + shift - 1, 0, count - 1)
        for term in range(TERMS):
            for part in range(4):
                plane, half = part // 2, part % 2
                tile = coefficient[term, plane, rows_at(row // 8 * 8, 8), 128 * half : 128 * half + 128]
                value = pltpu.roll(tile, lax.rem(8 - row % 8, 8), 0)[0:1]
                for again in range(4):
                    near[shift, plane, term, 2 * again + half : 2 * again + half + 1, :] = value

    pl.semaphore_wait(barrier, len(OFFSETS) + 2)
    copies = []
    for place, offset in enumerate(OFFSETS):
        peer = moved(me, offset)
        copy = pltpu.make_async_remote_copy(
            src_ref=blocks.at[peer],
            dst_ref=raw.at[pl.ds(me * slots, slots)],
            send_sem=send_sem.at[place],
            recv_sem=recv_sem.at[place],
            device_id=(slab, peer),
            device_id_type=MESH,
        )
        copy.start()
        copies.append(copy)
    own = pltpu.make_async_copy(blocks.at[me], raw.at[pl.ds(me * slots, slots)], own_sem.at[0])
    own.start()
    ids = sub * 128 + lane

    def moving(place, source, target):
        copy = pltpu.make_async_copy(source, target, own_sem.at[1 + place])
        copy.start()
        return copy

    entries = couplings.shape[1]
    whole, rest = entries // 128, entries % 128
    tiles = targets.shape[0] // 8
    for row in range(whole + 1):
        size = 128 if row < whole else rest
        if size:
            columns = slice(128 * row, 128 * row + size)
            targets[row : row + 1, 0:size] = couplings[0:1, columns]
            words[row : row + 1, 0:size] = (
                couplings[3:4, columns] * (8 * HELD) + (couplings[2:3, columns] - 1) * HELD + couplings[1:2, columns]
            )
    keys = []
    for tile in range(tiles):
        place = ids + 1024 * tile
        key = targets[8 * tile : 8 * tile + 8, :] * (8 * HELD) + place
        keys.append(jnp.where(place < entries, key, (1 << 30) + place))
        targets[8 * tile : 8 * tile + 8, :] = keys[-1]
        value = words[8 * tile : 8 * tile + 8, :]
        words[8 * tile : 8 * tile + 8, :] = jnp.where(place < entries, value, 0)
    def find(step, place):
        for part in range(8):
            slot = step * 8 + part
            place = jnp.where(ids == slot_mode[slot], slot, place)
        return place

    found[...] = lax.fori_loop(0, slots * count // 8, find, jnp.zeros((8, 128), jnp.int32))
    moves = [moving(0, targets, target_list), moving(1, words, word_list)]
    sent = []

    def send(place, source, target, peer):
        copy = pltpu.make_async_remote_copy(
            src_ref=source,
            dst_ref=target,
            send_sem=halo_send.at[place],
            recv_sem=halo_recv.at[place],
            device_id=peer,
            device_id_type=MESH,
        )
        copy.start()
        sent.append(copy)

    send(6 * CHUNKS, near.at[1, 1], coef_outer.at[0], right)
    send(6 * CHUNKS + 1, near.at[1, 0], coef_outer.at[1], left)
    floors = (sub * SPREAD + lane + 1) * (8 * HELD)

    def rank(step, carry):
        for part in range(128):
            key = target_list[step, part]
            carry = tuple(
                jnp.where(value > key, count_of + 1, count_of) for value, count_of in zip(keys + [floors], carry)
            )
        return carry

    none = jnp.zeros((8, 128), jnp.int32)
    for copy in moves:
        copy.wait()
    counted = lax.fori_loop(0, LIST_ROWS, rank, (none,) * (tiles + 1))
    for tile in range(tiles):
        ranks[8 * tile : 8 * tile + 8, :] = counted[tile]
    firsts[...] = counted[tiles]
    moves = [moving(2, found, inverse)]
    for copy in sent:
        copy.wait()
    sent.clear()

    for plane in range(2):
        for term in range(TERMS):
            middle = near[1, plane, term]
            around = (coef_outer[plane, term] * mask_outer[plane], near[1, 1 - plane, term])
            around = around + column_neighbours(middle, second, lane)
            around = around + (near[0, plane, term] * mask_low, near[2, plane, term] * mask_high)
            for place, value in enumerate(around):
                faces[plane, 6 * term + place] = 0.5 * (middle + value)

    moves += [moving(3, ranks, rank_list), moving(4, firsts, first_list)]
    for copy in moves:
        copy.wait()

    def arrange(step, carry):
        for part in range(128):
            place, word = rank_list[step, part], word_list[step, part]
            carry = tuple(
                jnp.where(spot == place, word, value) for spot, value in zip(spots, carry)
            )
        return carry

    spots = []
    for tile in range(tiles):
        row = sub + 8 * tile
        spots.append(jnp.where(row < LIST_ROWS, lane * LIST_ROWS + row, -1))
    arranged = lax.fori_loop(0, LIST_ROWS, arrange, (none,) * tiles)
    for tile in range(tiles):
        order[8 * tile : 8 * tile + 8, :] = arranged[tile]
    own.wait()
    for copy in copies:
        copy.wait()

    ends = [min(chunk * HELD // CHUNKS, USED) for chunk in range(CHUNKS + 1)]

    def pick(step, carry):
        for part in range(8):
            mode = step * 8 + part
            source = inverse[lax.shift_right_logical(step, 4), lax.bitwise_and(step, 15) * 8 + part]
            value = raw[source].astype(jnp.float32)
            wide[0, rows_at(2 * mode, 2), :] = value[0:2]
            wide[1, rows_at(2 * mode, 2), :] = value[2:4]
        return carry

    def narrow(step, carry):
        at = rows_at(step * 32, 32)
        planes[0, at, :] = wide[0, at, :].astype(jnp.bfloat16)
        planes[1, at, :] = wide[1, at, :].astype(jnp.bfloat16)
        return carry

    def send_chunk(phase, chunk):
        mine = core if phase == 0 else 1 - core
        beside = 1 - mine
        low, size = ends[chunk], ends[chunk + 1] - ends[chunk]
        at = pl.ds(2 * low, 2 * size)
        place = 3 * (CHUNKS * phase + chunk)
        send(place, planes.at[beside, at], row_low.at[beside, at], above)
        send(place + 1, planes.at[beside, at], row_high.at[beside, at], below)
        onward = lax.rem(slab + slabs + 1 - 2 * mine, slabs)
        send(place + 2, planes.at[beside, at], outer.at[mine, at], (onward, me))

    def shift_columns(step, carry):
        at = rows_at(step * 32, 32)
        around = []
        for plane in range(2):
            value = wide[plane, at, :]
            around += [column_neighbours(value[8 * part : 8 * part + 8], second, lane) for part in range(4)]
        for part, (low, high) in enumerate(around):
            at = rows_at(step * 32 + 8 * (part % 4), 8)
            column_low[part // 4, at, :] = low
            column_high[part // 4, at, :] = high
        return carry

    for chunk in range(CHUNKS):
        lax.fori_loop(ends[chunk] // 8, ends[chunk + 1] // 8, pick, 0)
        lax.fori_loop(ends[chunk] // 16, ends[chunk + 1] // 16, narrow, 0)
        if chunk:
            send_chunk(0, chunk - 1)
    lax.fori_loop(0, 4, shift_columns, 0)
    send_chunk(0, CHUNKS - 1)
    for chunk in range(CHUNKS):
        send_chunk(1, chunk)
    lax.fori_loop(4, USED // 16, shift_columns, 0)
    ordered = [moving(5 + row, order.at[row : row + 1], order_lists[row]) for row in range(LIST_ROWS)]

    def stencil_of(mine):
        edge = jnp.where(mine == 0, mask_outer[0], mask_outer[1])

        def stencil(step, carry):
            at = rows_at(step * 16, 16)
            low = row_low[mine, at, :].astype(jnp.float32)
            high = row_high[mine, at, :].astype(jnp.float32)
            far = outer[mine, at, :].astype(jnp.float32)
            halves = []
            for half in range(2):
                part = slice(8 * half, 8 * half + 8)
                base = pl.multiple_of(step * 16 + 8 * half, 8)
                at = pl.ds(base, 8)
                middle = wide[mine, at, :]
                around = (far[part] * edge, wide[1 - mine, at, :], column_low[mine, at, :], column_high[mine, at, :])
                around = around + (low[part] * mask_low, high[part] * mask_high)
                halves.append((base, 4 * half, [middle - value for value in around]))
            for term in range(TERMS):
                face = [faces[mine, 6 * term + place] for place in range(6)]
                for base, base_mode, drops in halves:
                    value = face[0] * drops[0]
                    for place in range(1, 6):
                        value = value + face[place] * drops[place]
                    if term == 0:
                        start[pl.ds(base, 8), :] = value
                    else:
                        image[pl.ds((term - 1) * HELD + step * 8 + base_mode, 4)] = value.reshape(4, 2, 128)
            return carry

        return stencil

    def couple(step, carry):
        for lot in range(2):
            column = 2 * step + lot
            values = []
            for part in range(LIST_ROWS):
                word = order_lists[part][0, column]
                weight = lax.shift_right_arithmetic(jnp.full((2, 128), word, jnp.int32), 12).astype(jnp.float32)
                value = image[lax.bitwise_and(word, 8 * HELD - 1)]
                values.append((weight * 0.125) * value)
            for part in range(0, LIST_ROWS, 3):
                one, two, three = values[part : part + 3]
                at = column * LIST_ROWS + part
                running[at] = carry
                running[at + 1] = carry + one
                running[at + 2] = carry + (one + two)
                carry = carry + (one + two + three)
        return carry

    def spread(step, carry):
        below_it, top = carry
        for part in range(SPREAD):
            up_to = running[first_list[step, part]]
            rows = rows_at(2 * (step * SPREAD + part), 2)
            value = start[rows, :] + (up_to - below_it)
            total[rows, :] = value
            below_it = up_to
            top = jnp.maximum(top, jnp.abs(value))
        return below_it, top

    blank = jnp.zeros((2, 128), jnp.float32)
    copies = []

    def give(phase, mine, place):
        peer = moved(me, OFFSETS[place])
        for kind, (source, target) in enumerate(((coded.at[phase, peer], got), (scale.at[phase], got_scales))):
            copy = pltpu.make_async_remote_copy(
                src_ref=source,
                dst_ref=target.at[mine, me],
                send_sem=give_send.at[kind, phase * len(OFFSETS) + place],
                recv_sem=give_recv.at[kind, phase * len(OFFSETS) + place],
                device_id=(slab, peer),
                device_id_type=MESH,
            )
            copy.start()
            copies.append(copy)

    for phase in range(2):
        mine = core if phase == 0 else 1 - core
        stencil = stencil_of(mine)
        for chunk in range(CHUNKS):
            place = 3 * (CHUNKS * phase + chunk)
            for copy in sent[place : place + 3]:
                copy.wait()
            lax.fori_loop(ends[chunk] // 8, ends[chunk + 1] // 8, stencil, 0)
        if phase == 0:
            for copy in ordered:
                copy.wait()
        running[128 * LIST_ROWS] = lax.fori_loop(0, 64, couple, blank)
        top = lax.fori_loop(0, MODES // SPREAD, spread, (blank, blank))[1]
        total[2 * MODES : 2 * MODES + 2, :] = blank
        top = jnp.max(jnp.max(top, axis=0, keepdims=True), axis=1, keepdims=True)
        top = jnp.broadcast_to(top, (1, 128))
        scale[phase] = top * (1.0 / (TOP * TOP))
        factor = TOP * lax.rsqrt(jnp.maximum(top, 1e-37))

        def encode(step, carry):
            value = total[rows_at(step * 32, 32), :]
            root = value * lax.rsqrt(jnp.maximum(jnp.abs(value), 1e-37))
            code = jnp.round(root * factor).astype(jnp.int32)
            codes[pl.ds(step * 16, 16)] = code.reshape(16, 2, 128)
            return carry

        lax.fori_loop(0, USED // 16, encode, 0)

        def prepare(group):
            def pick_codes(step, carry):
                for part in range(8):
                    slot = group * slots + step * 8 + part
                    picked[rows_at(2 * slot, 2), :] = codes[slot_mode[slot]]
                return carry

            lax.fori_loop(0, slots // 8, pick_codes, 0)
            for part in range(2):
                at = rows_at(group * 2 * slots + slots * part, slots)
                coded[phase, group, slots * part : slots * (part + 1), :] = picked[at, :].astype(jnp.int16)

        prepare(moved(me, OFFSETS[0]))
        for place in range(1, len(OFFSETS)):
            prepare(moved(me, OFFSETS[place]))
            give(phase, mine, place - 1)
        prepare(me)
        give(phase, mine, len(OFFSETS) - 1)

    own = []
    for phase in range(2):
        mine = core if phase == 0 else 1 - core
        at = 5 + LIST_ROWS + 2 * phase
        own.append(pltpu.make_async_copy(coded.at[phase, me], got.at[mine, me], own_sem.at[1 + at]))
        own.append(pltpu.make_async_copy(scale.at[phase], got_scales.at[mine, me], own_sem.at[2 + at]))
    for copy in own:
        copy.start()
    for copy in own + copies:
        copy.wait()


def decode_kernel(got, got_scales, out, wide, scale):
    planes, count, rows = got.shape[:3]
    for plane in range(planes):
        for source in range(count):
            at = plane * count + source
            scale[at : at + 1, :] = got_scales[plane, source]

    def widen(source, carry):
        for plane in range(planes):
            at = pl.ds((plane * count + source) * STRIDE, rows)
            wide[at, :] = got[plane, source].astype(jnp.int32).astype(jnp.float32)
        return carry

    lax.fori_loop(0, count, widen, 0)
    for plane in range(planes):
        factor = scale[plane * count : (plane + 1) * count, :]
        for place in range(rows):
            slot, half = place // 2, place % 2
            value = wide[pl.ds(plane * count * STRIDE + place, count, stride=STRIDE), :]
            out[slot, plane, :, 128 * half : 128 * half + 128] = (value * jnp.abs(value)) * factor


def on_device(field, coefficient, slot_mode, couplings):
    slabs, count = lax.axis_size("slab"), lax.axis_size("mode")
    slots, planes_here, rows_all, columns = field.shape
    entries = couplings.shape[0]
    f32, bf16, i16, i32 = jnp.float32, jnp.bfloat16, jnp.int16, jnp.int32
    dma = pltpu.SemaphoreType.DMA
    halo = 6 * CHUNKS + 2
    places = pl.cdiv(entries, 1024) * 8

    got, got_scales = pl.pallas_call(
        lambda *refs: gather_kernel(slabs, count, *refs),
        out_shape=(shape_of((2, count, slots * 2, 128), i16), shape_of((2, count, 1, 128), f32)),
        in_specs=[HBM] * 4,
        out_specs=(VMEM,) * 2,
        scratch_shapes=[
            pltpu.SMEM(slot_mode.shape, i32),
            pltpu.VMEM(field.shape, bf16),
            pltpu.VMEM(coefficient.shape, f32),
            pltpu.VMEM((4, entries), i32),
            pltpu.VMEM((count * slots * 4, 128), f32),
            pltpu.VMEM((count, slots, 4, 128), bf16),
            pltpu.VMEM((count * slots, 4, 128), bf16),
            pltpu.VMEM((2, ROWS // 2, 128), f32),
            pltpu.VMEM((8, 128), i32),
            pltpu.SMEM((8, 128), i32),
        ]
        + [pltpu.VMEM((2, ROWS // 2, 128), bf16)] * 4
        + [
            pltpu.VMEM((3, 2, TERMS, 8, 128), f32),
            pltpu.VMEM((2, TERMS, 8, 128), f32),
            pltpu.VMEM((2, 6 * TERMS, 8, 128), f32),
            pltpu.VMEM((2, ROWS // 2, 128), f32),
            pltpu.VMEM((2, ROWS // 2, 128), f32),
            pltpu.VMEM((ROWS // 2, 128), f32),
            pltpu.VMEM(((TERMS - 1) * HELD, 2, 128), f32),
            pltpu.VMEM((128 * LIST_ROWS + 8, 2, 128), f32),
        ]
        + [pltpu.VMEM((places, 128), i32)] * 4
        + [pltpu.VMEM((8, 128), i32)]
        + [pltpu.SMEM((places, 128), i32)] * 3
        + [
            pltpu.SMEM((8, 128), i32),
            pltpu.VMEM((ROWS // 2, 128), f32),
            pltpu.VMEM((HELD, 2, 128), i32),
            pltpu.VMEM((count * slots * 2, 128), i32),
            pltpu.VMEM((2, count, slots * 2, 128), i16),
            pltpu.VMEM((2, 1, 128), f32),
            dma((7,)),
            dma((10 + LIST_ROWS,)),
            dma((len(OFFSETS),)),
            dma((len(OFFSETS),)),
            dma((halo,)),
            dma((halo,)),
            dma((2, 2 * len(OFFSETS))),
            dma((2, 2 * len(OFFSETS))),
        ]
        + [pltpu.SMEM((1, 128), i32)] * LIST_ROWS,
        compiler_params=pltpu.CompilerParams(collective_id=0, has_side_effects=True, vmem_limit_bytes=48 * MIB),
        name="gather",
    )(*(pltpu.with_memory_space_constraint(value, pltpu.HBM) for value in (slot_mode, field, coefficient, couplings.T)))

    step = 8
    return pl.pallas_call(
        decode_kernel,
        out_shape=shape_of((slots, planes_here, rows_all, columns), f32),
        grid=(slots // step,),
        in_specs=[
            pl.BlockSpec((2, count, 2 * step, 128), lambda i: (0, 0, i, 0)),
            pl.BlockSpec((2, count, 1, 128), lambda i: (0, 0, 0, 0)),
        ],
        out_specs=pl.BlockSpec((step, planes_here, rows_all, columns), lambda i: (i, 0, 0, 0)),
        scratch_shapes=[pltpu.VMEM((2 * count * STRIDE, 128), f32), pltpu.VMEM((2 * count, 128), f32)],
        compiler_params=pltpu.CompilerParams(vmem_limit_bytes=12 * MIB),
        name="decode",
    )(got, got_scales)


def solution(mesh):
    in_specs = (P("mode", "slab", None, None), P(None, "slab", None, None), P(), P())
    return jax.shard_map(
        on_device,
        mesh=mesh,
        in_specs=in_specs,
        out_specs=P("mode", "slab", None, None),
        check_vma=False,
    )
```

```python
import jax
import jax.numpy as jnp
from jax import lax
from jax.experimental import pallas as pl
from jax.experimental.pallas import tpu as pltpu
from jax.sharding import PartitionSpec as P

MODES = 495
HELD = 512
TERMS = 9
ROWS = 4 * HELD
CHUNKS = 8
USED = 496
LIST_ROWS = 21
SPREAD = 99
TOP = 32700.0
SIDE = 4
MESH = pl.DeviceIdType.MESH
VMEM = pl.BlockSpec(memory_space=pltpu.VMEM)
SMEM = pl.BlockSpec(memory_space=pltpu.SMEM)
HBM = pl.BlockSpec(memory_space=pltpu.HBM)
MIB = 1024 * 1024


def far_first():
    offsets = [(x, y, core) for x in range(SIDE) for y in range(SIDE) for core in range(2)]
    hops = lambda offset: min(offset[0], SIDE - offset[0]) + min(offset[1], SIDE - offset[1])
    return sorted(offsets[1:], key=hops, reverse=True)


OFFSETS = far_first()


def shape_of(shape, dtype):
    return jax.ShapeDtypeStruct(shape, dtype)


def moved(me, offset, sign=1):
    x, y, core = me // (2 * SIDE), (me // 2) % SIDE, me % 2
    x = lax.rem(x + (sign * offset[0]) % SIDE, SIDE)
    y = lax.rem(y + (sign * offset[1]) % SIDE, SIDE)
    return (x * SIDE + y) * 2 + lax.rem(core + offset[2], 2)


def rows_at(start, size):
    return pl.ds(pl.multiple_of(start, size), size)


def plane_neighbours(centre, plane, front):
    return (
        jnp.where(front, plane, pltpu.roll(centre, 2, 0)),
        jnp.where(front, pltpu.roll(centre, 6, 0), plane),
    )


def column_neighbours(centre, second, lane):
    zero = jnp.zeros_like(centre)
    low = pltpu.roll(centre, 1, 1)
    high = pltpu.roll(centre, 127, 1)
    return (
        jnp.where(lane == 0, jnp.where(second, pltpu.roll(low, 1, 0), zero), low),
        jnp.where(lane == 127, jnp.where(second, zero, pltpu.roll(high, 7, 0)), high),
    )


def gather_kernel(
    slabs, count, slot_mode_hbm, field_hbm, coefficient_hbm, couplings_hbm,
    got, got_scales,
    slot_mode, field, coefficient, couplings, turned, blocks, raw, wide, wide_planes, found, inverse,
    held, planes, row_low, row_high, plane_low, plane_high, near, coef_low, coef_high,
    faces, plane_rows, column_low, column_high, start, image, running,
    targets, words, ranks, order, firsts, target_list, word_list, rank_list, first_list,
    total, codes, picked, coded, scale,
    load_sem, own_sem, send_sem, recv_sem, halo_send, halo_recv, give_send, give_recv, *order_lists,
):
    slab, me = lax.axis_index("slab"), lax.axis_index("mode")
    slots = field.shape[0]
    above = (slab, lax.rem(me + 1, count))
    below = (slab, lax.rem(me + count - 1, count))
    right = (lax.rem(slab + 1, slabs), me)
    left = (lax.rem(slab + slabs - 1, slabs), me)
    sub = lax.broadcasted_iota(jnp.int32, (8, 128), 0)
    lane = lax.broadcasted_iota(jnp.int32, (8, 128), 1)
    front = lax.rem(sub, 4) < 2
    second = lax.rem(sub, 2) == 1
    has_left = (slab > 0).astype(jnp.float32)
    has_right = (slab < slabs - 1).astype(jnp.float32)
    mask_plane = jnp.where(front, has_left, has_right)
    mask_low = (me > 0).astype(jnp.float32)
    mask_high = (me < count - 1).astype(jnp.float32)

    piece = slots // 4
    loads = [
        pltpu.make_async_copy(field_hbm.at[pl.ds(piece * part, piece)], field.at[pl.ds(piece * part, piece)], load_sem.at[part])
        for part in range(4)
    ]
    others = [
        pltpu.make_async_copy(source, target, load_sem.at[4 + place])
        for place, (source, target) in enumerate(
            ((coefficient_hbm, coefficient), (slot_mode_hbm, slot_mode), (couplings_hbm, couplings))
        )
    ]
    for load in loads + others:
        load.start()
    barrier = pltpu.get_barrier_semaphore()
    for offset in OFFSETS:
        pl.semaphore_signal(barrier, inc=1, device_id=(slab, moved(me, offset)), device_id_type=MESH)
    for peer in (right, left):
        pl.semaphore_signal(barrier, inc=1, device_id=peer, device_id_type=MESH)

    def turn(slot, carry):
        for part in range(4):
            plane, half = part // 2, part % 2
            value = field[slot, plane, :, 128 * half : 128 * half + 128].astype(jnp.float32)
            turned[pl.ds(4 * slot + part, count, stride=4 * slots), :] = value
        return carry

    for part, load in enumerate(loads):
        load.wait()
        lax.fori_loop(piece * part, piece * (part + 1), turn, 0)

    def narrow_block(row, carry):
        value = turned[rows_at(row * 4 * slots, 4 * slots), :]
        blocks[row] = value.reshape(slots, 4, 128).astype(jnp.bfloat16)
        return carry

    lax.fori_loop(0, count, narrow_block, 0)

    for load in others:
        load.wait()
    for shift in range(3):
        row = jnp.clip(me + shift - 1, 0, count - 1)
        for term in range(TERMS):
            for part in range(4):
                plane, half = part // 2, part % 2
                tile = coefficient[term, plane, rows_at(row // 8 * 8, 8), 128 * half : 128 * half + 128]
                value = pltpu.roll(tile, lax.rem(8 - row % 8, 8), 0)[0:1]
                near[shift, term, part : part + 1, :] = value
                near[shift, term, part + 4 : part + 5, :] = value

    pl.semaphore_wait(barrier, len(OFFSETS) + 2)
    copies = []
    for place, offset in enumerate(OFFSETS):
        peer = moved(me, offset)
        copy = pltpu.make_async_remote_copy(
            src_ref=blocks.at[peer],
            dst_ref=raw.at[pl.ds(me * slots, slots)],
            send_sem=send_sem.at[place],
            recv_sem=recv_sem.at[place],
            device_id=(slab, peer),
            device_id_type=MESH,
        )
        copy.start()
        copies.append(copy)
    own = pltpu.make_async_copy(blocks.at[me], raw.at[pl.ds(me * slots, slots)], own_sem.at[0])
    own.start()
    ids = sub * 128 + lane

    def moving(place, source, target):
        copy = pltpu.make_async_copy(source, target, own_sem.at[1 + place])
        copy.start()
        return copy

    entries = couplings.shape[1]
    whole, rest = entries // 128, entries % 128
    tiles = targets.shape[0] // 8
    for row in range(whole + 1):
        size = 128 if row < whole else rest
        if size:
            columns = slice(128 * row, 128 * row + size)
            targets[row : row + 1, 0:size] = couplings[0:1, columns]
            words[row : row + 1, 0:size] = (
                couplings[3:4, columns] * (8 * HELD) + (couplings[2:3, columns] - 1) * HELD + couplings[1:2, columns]
            )
    keys = []
    for tile in range(tiles):
        place = ids + 1024 * tile
        key = targets[8 * tile : 8 * tile + 8, :] * (8 * HELD) + place
        keys.append(jnp.where(place < entries, key, (1 << 30) + place))
        targets[8 * tile : 8 * tile + 8, :] = keys[-1]
        value = words[8 * tile : 8 * tile + 8, :]
        words[8 * tile : 8 * tile + 8, :] = jnp.where(place < entries, value, 0)
    def find(step, place):
        for part in range(8):
            slot = step * 8 + part
            place = jnp.where(ids == slot_mode[slot], slot, place)
        return place

    found[...] = lax.fori_loop(0, slots * count // 8, find, jnp.zeros((8, 128), jnp.int32))
    moves = [moving(0, targets, target_list), moving(1, words, word_list)]
    sent = []

    def send(place, source, target, peer):
        copy = pltpu.make_async_remote_copy(
            src_ref=source,
            dst_ref=target,
            send_sem=halo_send.at[place],
            recv_sem=halo_recv.at[place],
            device_id=peer,
            device_id_type=MESH,
        )
        copy.start()
        sent.append(copy)

    send(4 * CHUNKS, near.at[1], coef_low, right)
    send(4 * CHUNKS + 1, near.at[1], coef_high, left)
    own_coef = near.at[1]
    floors = (sub * SPREAD + lane + 1) * (8 * HELD)

    def rank(step, carry):
        for part in range(128):
            key = target_list[step, part]
            carry = tuple(
                jnp.where(value > key, count_of + 1, count_of) for value, count_of in zip(keys + [floors], carry)
            )
        return carry

    none = jnp.zeros((8, 128), jnp.int32)
    for copy in moves:
        copy.wait()
    counted = lax.fori_loop(0, LIST_ROWS, rank, (none,) * (tiles + 1))
    for tile in range(tiles):
        ranks[8 * tile : 8 * tile + 8, :] = counted[tile]
    firsts[...] = counted[tiles]
    moves = [moving(2, found, inverse)]
    for copy in sent:
        copy.wait()
    sent.clear()

    for term in range(TERMS):
        middle = own_coef[term]
        outer = jnp.where(front, pltpu.roll(coef_low[term], 6, 0), pltpu.roll(coef_high[term], 2, 0)) * mask_plane
        around = plane_neighbours(middle, outer, front) + column_neighbours(middle, second, lane)
        around = around + (near[0, term] * mask_low, near[2, term] * mask_high)
        for place, value in enumerate(around):
            faces[6 * term + place] = 0.5 * (middle + value)

    moves += [moving(3, ranks, rank_list), moving(4, firsts, first_list)]
    for copy in moves:
        copy.wait()

    def arrange(step, carry):
        for part in range(128):
            place, word = rank_list[step, part], word_list[step, part]
            carry = tuple(
                jnp.where(spot == place, word, value) for spot, value in zip(spots, carry)
            )
        return carry

    spots = []
    for tile in range(tiles):
        row = sub + 8 * tile
        spots.append(jnp.where(row < LIST_ROWS, lane * LIST_ROWS + row, -1))
    arranged = lax.fori_loop(0, LIST_ROWS, arrange, (none,) * tiles)
    for tile in range(tiles):
        order[8 * tile : 8 * tile + 8, :] = arranged[tile]
    own.wait()
    for copy in copies:
        copy.wait()

    ends = [min(chunk * HELD // CHUNKS, USED) for chunk in range(CHUNKS + 1)]

    def pick(low, high):
        for mode in range(low, high):
            value = raw[inverse[mode // 128, mode % 128]].astype(jnp.float32)
            wide[4 * mode : 4 * mode + 4, :] = value
            wide_planes[0, 2 * mode : 2 * mode + 2, :] = value[0:2]
            wide_planes[1, 2 * mode : 2 * mode + 2, :] = value[2:4]

    def narrow(step, carry):
        at = rows_at(step * 64, 64)
        held[at, :] = wide[at, :].astype(jnp.bfloat16)
        at = rows_at(step * 32, 32)
        planes[0, at, :] = wide_planes[0, at, :].astype(jnp.bfloat16)
        planes[1, at, :] = wide_planes[1, at, :].astype(jnp.bfloat16)
        return carry

    def send_chunk(chunk):
        low, size = ends[chunk], ends[chunk + 1] - ends[chunk]
        at, half = pl.ds(4 * low, 4 * size), pl.ds(2 * low, 2 * size)
        send(4 * chunk, held.at[at], row_low.at[at], above)
        send(4 * chunk + 1, held.at[at], row_high.at[at], below)
        send(4 * chunk + 2, planes.at[1, half], plane_low.at[half], right)
        send(4 * chunk + 3, planes.at[0, half], plane_high.at[half], left)

    def shift_columns(step, carry):
        value = wide[rows_at(step * 64, 64), :]
        around = [column_neighbours(value[8 * part : 8 * part + 8], second, lane) for part in range(8)]
        for part, (low, high) in enumerate(around):
            at = rows_at(step * 64 + 8 * part, 8)
            column_low[at, :] = low
            column_high[at, :] = high
        return carry

    for chunk in range(CHUNKS):
        pick(ends[chunk], ends[chunk + 1])
        lax.fori_loop(ends[chunk] // 16, ends[chunk + 1] // 16, narrow, 0)
        if chunk:
            send_chunk(chunk - 1)
    lax.fori_loop(0, 4, shift_columns, 0)
    send_chunk(CHUNKS - 1)
    lax.fori_loop(4, USED // 16, shift_columns, 0)

    ordered = [moving(5 + row, order.at[row : row + 1], order_lists[row]) for row in range(LIST_ROWS)]

    def interleave(step, carry):
        at = rows_at(step * 16, 16)
        low = plane_low[at, :].astype(jnp.float32) * has_left
        high = plane_high[at, :].astype(jnp.float32) * has_right
        for part in range(8):
            base = pl.multiple_of(step * 32 + 4 * part, 4)
            plane_rows[pl.ds(base, 2), :] = low[2 * part : 2 * part + 2]
            plane_rows[pl.ds(base + 2, 2), :] = high[2 * part : 2 * part + 2]
        return carry

    def stencil(step, carry):
        at = rows_at(step * 16, 16)
        low = row_low[at, :].astype(jnp.float32)
        high = row_high[at, :].astype(jnp.float32)
        halves = []
        for half in range(2):
            part = slice(8 * half, 8 * half + 8)
            base = pl.multiple_of(step * 16 + 8 * half, 8)
            at = pl.ds(base, 8)
            middle = wide[at, :]
            around = plane_neighbours(middle, plane_rows[at, :], front) + (column_low[at, :], column_high[at, :])
            around = around + (low[part] * mask_low, high[part] * mask_high)
            halves.append((base, 2 * half, [middle - value for value in around]))
        for term in range(TERMS):
            face = [faces[6 * term + place] for place in range(6)]
            for base, base_mode, drops in halves:
                total = face[0] * drops[0]
                for place in range(1, 6):
                    total = total + face[place] * drops[place]
                if term == 0:
                    start[pl.ds(base, 8), :] = total
                else:
                    at = (term - 1) * HELD + step * 4 + base_mode
                    image[pl.ds(at, 2)] = total.reshape(2, 4, 128)
        return carry

    for chunk in range(CHUNKS):
        for copy in sent[4 * chunk : 4 * chunk + 4]:
            copy.wait()
        lax.fori_loop(ends[chunk] // 8, ends[chunk + 1] // 8, interleave, 0)
        lax.fori_loop(ends[chunk] // 4, ends[chunk + 1] // 4, stencil, 0)

    def couple(step, carry):
        for lot in range(2):
            column = 2 * step + lot
            values = []
            for part in range(LIST_ROWS):
                word = order_lists[part][0, column]
                weight = lax.shift_right_arithmetic(jnp.full((4, 128), word, jnp.int32), 12).astype(jnp.float32)
                value = image[lax.bitwise_and(word, 8 * HELD - 1)]
                values.append((weight * 0.125) * value)
            for part in range(0, LIST_ROWS, 3):
                one, two, three = values[part : part + 3]
                at = column * LIST_ROWS + part
                running[at] = carry
                running[at + 1] = carry + one
                running[at + 2] = carry + (one + two)
                carry = carry + (one + two + three)
        return carry

    for copy in ordered:
        copy.wait()
    running[128 * LIST_ROWS] = lax.fori_loop(0, 64, couple, jnp.zeros((4, 128), jnp.float32))

    def spread(step, carry):
        below_it, top = carry
        for part in range(SPREAD):
            up_to = running[first_list[step, part]]
            rows = rows_at(4 * (step * SPREAD + part), 4)
            value = start[rows, :] + (up_to - below_it)
            total[rows, :] = value
            below_it = up_to
            top = jnp.maximum(top, jnp.abs(value))
        return below_it, top

    blank = jnp.zeros((4, 128), jnp.float32)
    top = lax.fori_loop(0, MODES // SPREAD, spread, (blank, blank))[1]
    total[4 * MODES : 4 * MODES + 4, :] = blank
    top = jnp.max(jnp.max(top, axis=0, keepdims=True), axis=1, keepdims=True)
    top = jnp.broadcast_to(top, (1, 128))
    scale[...] = top * (1.0 / (TOP * TOP))
    factor = TOP * lax.rsqrt(jnp.maximum(top, 1e-37))

    def encode(step, carry):
        value = total[rows_at(step * 64, 64), :]
        root = value * lax.rsqrt(jnp.maximum(jnp.abs(value), 1e-37))
        code = jnp.round(root * factor).astype(jnp.int32)
        codes[pl.ds(step * 16, 16)] = code.reshape(16, 4, 128)
        return carry

    lax.fori_loop(0, USED // 16, encode, 0)

    def prepare(group):
        for part in range(slots):
            slot = group * slots + part
            picked[rows_at(4 * slot, 4), :] = codes[slot_mode[slot]]
        for part in range(4):
            at = rows_at(group * 4 * slots + slots * part, slots)
            coded[group, slots * part : slots * (part + 1), :] = picked[at, :].astype(jnp.int16)

    copies = []

    def give(place):
        peer = moved(me, OFFSETS[place])
        for kind, (source, target) in enumerate(((coded.at[peer], got), (scale, got_scales))):
            copy = pltpu.make_async_remote_copy(
                src_ref=source,
                dst_ref=target.at[me],
                send_sem=give_send.at[kind, place],
                recv_sem=give_recv.at[kind, place],
                device_id=(slab, peer),
                device_id_type=MESH,
            )
            copy.start()
            copies.append(copy)

    prepare(moved(me, OFFSETS[0]))
    for place in range(1, len(OFFSETS)):
        prepare(moved(me, OFFSETS[place]))
        give(place - 1)
    prepare(me)
    give(len(OFFSETS) - 1)
    own = [
        pltpu.make_async_copy(coded.at[me], got.at[me], own_sem.at[6 + LIST_ROWS]),
        pltpu.make_async_copy(scale, got_scales.at[me], own_sem.at[7 + LIST_ROWS]),
    ]
    for copy in own:
        copy.start()
    for copy in own + copies:
        copy.wait()


def decode_kernel(got, got_scales, out, wide, scale):
    count, rows = got.shape[0], got.shape[1]
    for source in range(count):
        scale[source : source + 1, :] = got_scales[source]

    def widen(source, carry):
        at = pl.ds(source * (rows + 1), rows)
        wide[at, :] = got[source].astype(jnp.int32).astype(jnp.float32)
        return carry

    lax.fori_loop(0, count, widen, 0)
    factor = scale[...]
    for place in range(rows):
        slot, plane, half = place // 4, (place // 2) % 2, place % 2
        value = wide[pl.ds(place, count, stride=rows + 1), :]
        out[slot, plane, :, 128 * half : 128 * half + 128] = (value * jnp.abs(value)) * factor


def on_device(field, coefficient, slot_mode, couplings):
    slabs, count = lax.axis_size("slab"), lax.axis_size("mode")
    slots, planes_here, rows_all, columns = field.shape
    entries = couplings.shape[0]
    f32, bf16, i16, i32 = jnp.float32, jnp.bfloat16, jnp.int16, jnp.int32
    dma = pltpu.SemaphoreType.DMA
    halo = 4 * CHUNKS + 2
    places = pl.cdiv(entries, 1024) * 8

    got, got_scales = pl.pallas_call(
        lambda *refs: gather_kernel(slabs, count, *refs),
        out_shape=(shape_of((count, slots * 4, 128), i16), shape_of((count, 1, 128), f32)),
        in_specs=[HBM] * 4,
        out_specs=(VMEM,) * 2,
        scratch_shapes=[
            pltpu.SMEM(slot_mode.shape, i32),
            pltpu.VMEM(field.shape, bf16),
            pltpu.VMEM(coefficient.shape, f32),
            pltpu.VMEM((4, entries), i32),
            pltpu.VMEM((count * slots * 4, 128), f32),
            pltpu.VMEM((count, slots, 4, 128), bf16),
            pltpu.VMEM((count * slots, 4, 128), bf16),
            pltpu.VMEM((ROWS, 128), f32),
            pltpu.VMEM((2, ROWS // 2, 128), f32),
            pltpu.VMEM((8, 128), i32),
            pltpu.SMEM((8, 128), i32),
            pltpu.VMEM((ROWS, 128), bf16),
            pltpu.VMEM((2, ROWS // 2, 128), bf16),
            pltpu.VMEM((ROWS, 128), bf16),
            pltpu.VMEM((ROWS, 128), bf16),
            pltpu.VMEM((ROWS // 2, 128), bf16),
            pltpu.VMEM((ROWS // 2, 128), bf16),
            pltpu.VMEM((3, TERMS, 8, 128), f32),
            pltpu.VMEM((TERMS, 8, 128), f32),
            pltpu.VMEM((TERMS, 8, 128), f32),
            pltpu.VMEM((6 * TERMS, 8, 128), f32),
            pltpu.VMEM((ROWS, 128), f32),
            pltpu.VMEM((ROWS, 128), f32),
            pltpu.VMEM((ROWS, 128), f32),
            pltpu.VMEM((ROWS, 128), f32),
            pltpu.VMEM(((TERMS - 1) * HELD, 4, 128), f32),
            pltpu.VMEM((128 * LIST_ROWS + 8, 4, 128), f32),
        ]
        + [pltpu.VMEM((places, 128), i32)] * 4
        + [pltpu.VMEM((8, 128), i32)]
        + [pltpu.SMEM((places, 128), i32)] * 3
        + [
            pltpu.SMEM((8, 128), i32),
            pltpu.VMEM((ROWS, 128), f32),
            pltpu.VMEM((HELD, 4, 128), i32),
            pltpu.VMEM((count * slots * 4, 128), i32),
            pltpu.VMEM((count, slots * 4, 128), i16),
            pltpu.VMEM((1, 128), f32),
            dma((7,)),
            dma((8 + LIST_ROWS,)),
            dma((len(OFFSETS),)),
            dma((len(OFFSETS),)),
            dma((halo,)),
            dma((halo,)),
            dma((2, len(OFFSETS))),
            dma((2, len(OFFSETS))),
        ]
        + [pltpu.SMEM((1, 128), i32)] * LIST_ROWS,
        compiler_params=pltpu.CompilerParams(collective_id=0, has_side_effects=True, vmem_limit_bytes=48 * MIB),
        name="gather",
    )(*(pltpu.with_memory_space_constraint(value, pltpu.HBM) for value in (slot_mode, field, coefficient, couplings.T)))

    step = 8
    return pl.pallas_call(
        decode_kernel,
        out_shape=shape_of((slots, planes_here, rows_all, columns), f32),
        grid=(slots // step,),
        in_specs=[
            pl.BlockSpec((count, 4 * step, 128), lambda i: (0, i, 0)),
            pl.BlockSpec((count, 1, 128), lambda i: (0, 0, 0)),
        ],
        out_specs=pl.BlockSpec((step, planes_here, rows_all, columns), lambda i: (i, 0, 0, 0)),
        scratch_shapes=[pltpu.VMEM((count * (4 * step + 1), 128), f32), pltpu.VMEM((count, 128), f32)],
        compiler_params=pltpu.CompilerParams(vmem_limit_bytes=12 * MIB),
        name="decode",
    )(got, got_scales)


def solution(mesh):
    in_specs = (P("mode", "slab", None, None), P(None, "slab", None, None), P(), P())
    return jax.shard_map(
        on_device,
        mesh=mesh,
        in_specs=in_specs,
        out_specs=P("mode", "slab", None, None),
        check_vma=False,
    )
```

```python
import jax
import jax.numpy as jnp
from jax import lax
from jax.experimental import pallas as pl
from jax.experimental.pallas import tpu as pltpu
from jax.sharding import PartitionSpec as P

MODES = 495
HELD = 512
TERMS = 9
ROWS = 4 * HELD
CHUNKS = 9
USED = 496
LIST_ROWS = 21
SPREAD = 99
TOP = 32700.0
SIDE = 4
MESH = pl.DeviceIdType.MESH
VMEM = pl.BlockSpec(memory_space=pltpu.VMEM)
SMEM = pl.BlockSpec(memory_space=pltpu.SMEM)
HBM = pl.BlockSpec(memory_space=pltpu.HBM)
MIB = 1024 * 1024


def far_first():
    offsets = [(x, y, core) for x in range(SIDE) for y in range(SIDE) for core in range(2)]
    hops = lambda offset: min(offset[0], SIDE - offset[0]) + min(offset[1], SIDE - offset[1])
    return sorted(offsets[1:], key=hops, reverse=True)


OFFSETS = far_first()


def shape_of(shape, dtype):
    return jax.ShapeDtypeStruct(shape, dtype)


def moved(me, offset, sign=1):
    x, y, core = me // (2 * SIDE), (me // 2) % SIDE, me % 2
    x = lax.rem(x + (sign * offset[0]) % SIDE, SIDE)
    y = lax.rem(y + (sign * offset[1]) % SIDE, SIDE)
    return (x * SIDE + y) * 2 + lax.rem(core + offset[2], 2)


def rows_at(start, size):
    return pl.ds(pl.multiple_of(start, size), size)


def plane_neighbours(centre, plane, front):
    return (
        jnp.where(front, plane, pltpu.roll(centre, 2, 0)),
        jnp.where(front, pltpu.roll(centre, 6, 0), plane),
    )


def column_neighbours(centre, second, lane):
    zero = jnp.zeros_like(centre)
    low = pltpu.roll(centre, 1, 1)
    high = pltpu.roll(centre, 127, 1)
    return (
        jnp.where(lane == 0, jnp.where(second, pltpu.roll(low, 1, 0), zero), low),
        jnp.where(lane == 127, jnp.where(second, zero, pltpu.roll(high, 7, 0)), high),
    )


def gather_kernel(
    slabs, count, slot_mode_hbm, field_hbm, coefficient_hbm, couplings_hbm,
    got, got_scales,
    slot_mode, field, coefficient, couplings, turned, blocks, raw, wide, wide_planes, found, inverse,
    held, planes, row_low, row_high, plane_low, plane_high, near, coef_low, coef_high,
    faces, plane_rows, column_low, column_high, start, image, running,
    targets, words, ranks, order, firsts, target_list, word_list, rank_list, first_list,
    total, codes, picked, coded, scale,
    load_sem, own_sem, send_sem, recv_sem, halo_send, halo_recv, give_send, give_recv, *order_lists,
):
    slab, me = lax.axis_index("slab"), lax.axis_index("mode")
    slots = field.shape[0]
    above = (slab, lax.rem(me + 1, count))
    below = (slab, lax.rem(me + count - 1, count))
    right = (lax.rem(slab + 1, slabs), me)
    left = (lax.rem(slab + slabs - 1, slabs), me)
    sub = lax.broadcasted_iota(jnp.int32, (8, 128), 0)
    lane = lax.broadcasted_iota(jnp.int32, (8, 128), 1)
    front = lax.rem(sub, 4) < 2
    second = lax.rem(sub, 2) == 1
    has_left = (slab > 0).astype(jnp.float32)
    has_right = (slab < slabs - 1).astype(jnp.float32)
    mask_plane = jnp.where(front, has_left, has_right)
    mask_low = (me > 0).astype(jnp.float32)
    mask_high = (me < count - 1).astype(jnp.float32)

    piece = slots // 4
    loads = [
        pltpu.make_async_copy(field_hbm.at[pl.ds(piece * part, piece)], field.at[pl.ds(piece * part, piece)], load_sem.at[part])
        for part in range(4)
    ]
    others = [
        pltpu.make_async_copy(source, target, load_sem.at[4 + place])
        for place, (source, target) in enumerate(
            ((coefficient_hbm, coefficient), (slot_mode_hbm, slot_mode), (couplings_hbm, couplings))
        )
    ]
    for load in loads + others:
        load.start()
    barrier = pltpu.get_barrier_semaphore()
    for offset in OFFSETS:
        pl.semaphore_signal(barrier, inc=1, device_id=(slab, moved(me, offset)), device_id_type=MESH)
    for peer in (right, left):
        pl.semaphore_signal(barrier, inc=1, device_id=peer, device_id_type=MESH)

    def turn(slot, carry):
        for part in range(4):
            plane, half = part // 2, part % 2
            value = field[slot, plane, :, 128 * half : 128 * half + 128].astype(jnp.float32)
            turned[pl.ds(4 * slot + part, count, stride=4 * slots), :] = value
        return carry

    for part, load in enumerate(loads):
        load.wait()
        lax.fori_loop(piece * part, piece * (part + 1), turn, 0)

    def narrow_block(row, carry):
        value = turned[rows_at(row * 4 * slots, 4 * slots), :]
        blocks[row] = value.reshape(slots, 4, 128).astype(jnp.bfloat16)
        return carry

    lax.fori_loop(0, count, narrow_block, 0)

    for load in others:
        load.wait()
    for shift in range(3):
        row = jnp.clip(me + shift - 1, 0, count - 1)
        for term in range(TERMS):
            for part in range(4):
                plane, half = part // 2, part % 2
                tile = coefficient[term, plane, rows_at(row // 8 * 8, 8), 128 * half : 128 * half + 128]
                value = pltpu.roll(tile, lax.rem(8 - row % 8, 8), 0)[0:1]
                near[shift, term, part : part + 1, :] = value
                near[shift, term, part + 4 : part + 5, :] = value

    pl.semaphore_wait(barrier, len(OFFSETS) + 2)
    copies = []
    for place, offset in enumerate(OFFSETS):
        peer = moved(me, offset)
        copy = pltpu.make_async_remote_copy(
            src_ref=blocks.at[peer],
            dst_ref=raw.at[pl.ds(me * slots, slots)],
            send_sem=send_sem.at[place],
            recv_sem=recv_sem.at[place],
            device_id=(slab, peer),
            device_id_type=MESH,
        )
        copy.start()
        copies.append(copy)
    own = pltpu.make_async_copy(blocks.at[me], raw.at[pl.ds(me * slots, slots)], own_sem.at[0])
    own.start()
    ids = sub * 128 + lane

    def moving(place, source, target):
        copy = pltpu.make_async_copy(source, target, own_sem.at[1 + place])
        copy.start()
        return copy

    entries = couplings.shape[1]
    whole, rest = entries // 128, entries % 128
    tiles = targets.shape[0] // 8
    for row in range(whole + 1):
        size = 128 if row < whole else rest
        if size:
            columns = slice(128 * row, 128 * row + size)
            targets[row : row + 1, 0:size] = couplings[0:1, columns]
            words[row : row + 1, 0:size] = (
                couplings[3:4, columns] * (8 * HELD) + (couplings[2:3, columns] - 1) * HELD + couplings[1:2, columns]
            )
    keys = []
    for tile in range(tiles):
        place = ids + 1024 * tile
        key = targets[8 * tile : 8 * tile + 8, :] * (8 * HELD) + place
        keys.append(jnp.where(place < entries, key, (1 << 30) + place))
        targets[8 * tile : 8 * tile + 8, :] = keys[-1]
        value = words[8 * tile : 8 * tile + 8, :]
        words[8 * tile : 8 * tile + 8, :] = jnp.where(place < entries, value, 0)
    def find(step, place):
        for part in range(8):
            slot = step * 8 + part
            place = jnp.where(ids == slot_mode[slot], slot, place)
        return place

    found[...] = lax.fori_loop(0, slots * count // 8, find, jnp.zeros((8, 128), jnp.int32))
    moves = [moving(0, targets, target_list), moving(1, words, word_list)]
    sent = []

    def send(place, source, target, peer):
        copy = pltpu.make_async_remote_copy(
            src_ref=source,
            dst_ref=target,
            send_sem=halo_send.at[place],
            recv_sem=halo_recv.at[place],
            device_id=peer,
            device_id_type=MESH,
        )
        copy.start()
        sent.append(copy)

    send(4 * CHUNKS, near.at[1], coef_low, right)
    send(4 * CHUNKS + 1, near.at[1], coef_high, left)
    own_coef = near.at[1]
    floors = (sub * SPREAD + lane + 1) * (8 * HELD)

    def rank(step, carry):
        for part in range(128):
            key = target_list[step, part]
            carry = tuple(
                jnp.where(value > key, count_of + 1, count_of) for value, count_of in zip(keys + [floors], carry)
            )
        return carry

    none = jnp.zeros((8, 128), jnp.int32)
    for copy in moves:
        copy.wait()
    counted = lax.fori_loop(0, LIST_ROWS, rank, (none,) * (tiles + 1))
    for tile in range(tiles):
        ranks[8 * tile : 8 * tile + 8, :] = counted[tile]
    firsts[...] = counted[tiles]
    moves = [moving(2, found, inverse)]
    for copy in sent:
        copy.wait()
    sent.clear()

    for term in range(TERMS):
        middle = own_coef[term]
        outer = jnp.where(front, pltpu.roll(coef_low[term], 6, 0), pltpu.roll(coef_high[term], 2, 0)) * mask_plane
        around = plane_neighbours(middle, outer, front) + column_neighbours(middle, second, lane)
        around = around + (near[0, term] * mask_low, near[2, term] * mask_high)
        for place, value in enumerate(around):
            faces[6 * term + place] = 0.5 * (middle + value)

    moves += [moving(3, ranks, rank_list), moving(4, firsts, first_list)]
    for copy in moves:
        copy.wait()

    def arrange(step, carry):
        for part in range(128):
            place, word = rank_list[step, part], word_list[step, part]
            carry = tuple(
                jnp.where(spot == place, word, value) for spot, value in zip(spots, carry)
            )
        return carry

    spots = []
    for tile in range(tiles):
        row = sub + 8 * tile
        spots.append(jnp.where(row < LIST_ROWS, lane * LIST_ROWS + row, -1))
    arranged = lax.fori_loop(0, LIST_ROWS, arrange, (none,) * tiles)
    for tile in range(tiles):
        order[8 * tile : 8 * tile + 8, :] = arranged[tile]
    own.wait()
    for copy in copies:
        copy.wait()

    ends = [0, 32] + [64 * chunk for chunk in range(1, CHUNKS - 1)] + [USED]

    def pick(low, high):
        for mode in range(low, high):
            value = raw[inverse[mode // 128, mode % 128]].astype(jnp.float32)
            wide[4 * mode : 4 * mode + 4, :] = value
            wide_planes[0, 2 * mode : 2 * mode + 2, :] = value[0:2]
            wide_planes[1, 2 * mode : 2 * mode + 2, :] = value[2:4]

    def narrow(step, carry):
        at = rows_at(step * 64, 64)
        held[at, :] = wide[at, :].astype(jnp.bfloat16)
        at = rows_at(step * 32, 32)
        planes[0, at, :] = wide_planes[0, at, :].astype(jnp.bfloat16)
        planes[1, at, :] = wide_planes[1, at, :].astype(jnp.bfloat16)
        return carry

    def send_chunk(chunk):
        low, size = ends[chunk], ends[chunk + 1] - ends[chunk]
        at, half = pl.ds(4 * low, 4 * size), pl.ds(2 * low, 2 * size)
        send(4 * chunk, held.at[at], row_low.at[at], above)
        send(4 * chunk + 1, held.at[at], row_high.at[at], below)
        send(4 * chunk + 2, planes.at[1, half], plane_low.at[half], right)
        send(4 * chunk + 3, planes.at[0, half], plane_high.at[half], left)

    def shift_columns(step, carry):
        value = wide[rows_at(step * 64, 64), :]
        around = [column_neighbours(value[8 * part : 8 * part + 8], second, lane) for part in range(8)]
        for part, (low, high) in enumerate(around):
            at = rows_at(step * 64 + 8 * part, 8)
            column_low[at, :] = low
            column_high[at, :] = high
        return carry

    for chunk in range(CHUNKS):
        pick(ends[chunk], ends[chunk + 1])
        lax.fori_loop(ends[chunk] // 16, ends[chunk + 1] // 16, narrow, 0)
        if chunk:
            send_chunk(chunk - 1)
    lax.fori_loop(0, 4, shift_columns, 0)
    send_chunk(CHUNKS - 1)
    lax.fori_loop(4, USED // 16, shift_columns, 0)

    ordered = [moving(5 + row, order.at[row : row + 1], order_lists[row]) for row in range(LIST_ROWS)]

    def interleave(step, carry):
        at = rows_at(step * 16, 16)
        low = plane_low[at, :].astype(jnp.float32) * has_left
        high = plane_high[at, :].astype(jnp.float32) * has_right
        for part in range(8):
            base = pl.multiple_of(step * 32 + 4 * part, 4)
            plane_rows[pl.ds(base, 2), :] = low[2 * part : 2 * part + 2]
            plane_rows[pl.ds(base + 2, 2), :] = high[2 * part : 2 * part + 2]
        return carry

    def stencil(step, carry):
        at = rows_at(step * 16, 16)
        low = row_low[at, :].astype(jnp.float32)
        high = row_high[at, :].astype(jnp.float32)
        halves = []
        for half in range(2):
            part = slice(8 * half, 8 * half + 8)
            base = pl.multiple_of(step * 16 + 8 * half, 8)
            at = pl.ds(base, 8)
            middle = wide[at, :]
            around = plane_neighbours(middle, plane_rows[at, :], front) + (column_low[at, :], column_high[at, :])
            around = around + (low[part] * mask_low, high[part] * mask_high)
            halves.append((base, 2 * half, [middle - value for value in around]))
        for term in range(TERMS):
            face = [faces[6 * term + place] for place in range(6)]
            for base, base_mode, drops in halves:
                total = face[0] * drops[0]
                for place in range(1, 6):
                    total = total + face[place] * drops[place]
                if term == 0:
                    start[pl.ds(base, 8), :] = total
                else:
                    at = (term - 1) * HELD + step * 4 + base_mode
                    image[pl.ds(at, 2)] = total.reshape(2, 4, 128)
        return carry

    for chunk in range(CHUNKS):
        for copy in sent[4 * chunk : 4 * chunk + 4]:
            copy.wait()
        lax.fori_loop(ends[chunk] // 8, ends[chunk + 1] // 8, interleave, 0)
        lax.fori_loop(ends[chunk] // 4, ends[chunk + 1] // 4, stencil, 0)

    def couple(step, carry):
        for lot in range(2):
            column = 2 * step + lot
            values = []
            for part in range(LIST_ROWS):
                word = order_lists[part][0, column]
                weight = lax.shift_right_arithmetic(jnp.full((4, 128), word, jnp.int32), 12).astype(jnp.float32)
                value = image[lax.bitwise_and(word, 8 * HELD - 1)]
                values.append((weight * 0.125) * value)
            for part in range(0, LIST_ROWS, 3):
                one, two, three = values[part : part + 3]
                at = column * LIST_ROWS + part
                running[at] = carry
                running[at + 1] = carry + one
                running[at + 2] = carry + (one + two)
                carry = carry + (one + two + three)
        return carry

    for copy in ordered:
        copy.wait()
    running[128 * LIST_ROWS] = lax.fori_loop(0, 64, couple, jnp.zeros((4, 128), jnp.float32))

    blank = jnp.zeros((4, 128), jnp.float32)
    below_it, top = blank, blank
    for mode in range(MODES):
        up_to = running[first_list[mode // SPREAD, mode % SPREAD]]
        value = start[4 * mode : 4 * mode + 4, :] + (up_to - below_it)
        total[4 * mode : 4 * mode + 4, :] = value
        below_it = up_to
        top = jnp.maximum(top, jnp.abs(value))
    total[4 * MODES : 4 * MODES + 4, :] = blank
    top = jnp.max(jnp.max(top, axis=0, keepdims=True), axis=1, keepdims=True)
    top = jnp.broadcast_to(top, (1, 128))
    scale[...] = top * (1.0 / (TOP * TOP))
    factor = TOP * lax.rsqrt(jnp.maximum(top, 1e-37))

    def encode(step, carry):
        value = total[rows_at(step * 64, 64), :]
        root = value * lax.rsqrt(jnp.maximum(jnp.abs(value), 1e-37))
        code = jnp.round(root * factor).astype(jnp.int32)
        codes[pl.ds(step * 16, 16)] = code.reshape(16, 4, 128)
        return carry

    lax.fori_loop(0, USED // 16, encode, 0)

    def prepare(group):
        for part in range(slots):
            slot = group * slots + part
            picked[rows_at(4 * slot, 4), :] = codes[slot_mode[slot]]
        for part in range(4):
            at = rows_at(group * 4 * slots + slots * part, slots)
            coded[group, slots * part : slots * (part + 1), :] = picked[at, :].astype(jnp.int16)

    copies = []

    def give(place, kind):
        peer = moved(me, OFFSETS[place])
        source, target = ((coded.at[peer], got), (scale, got_scales))[kind]
        copy = pltpu.make_async_remote_copy(
            src_ref=source,
            dst_ref=target.at[me],
            send_sem=give_send.at[kind, place],
            recv_sem=give_recv.at[kind, place],
            device_id=(slab, peer),
            device_id_type=MESH,
        )
        copy.start()
        copies.append(copy)

    prepare(moved(me, OFFSETS[0]))
    for place in range(1, len(OFFSETS)):
        prepare(moved(me, OFFSETS[place]))
        give(place - 1, 1)
        give(place - 1, 0)
    prepare(me)
    give(len(OFFSETS) - 1, 1)
    give(len(OFFSETS) - 1, 0)
    own = [
        pltpu.make_async_copy(coded.at[me], got.at[me], own_sem.at[6 + LIST_ROWS]),
        pltpu.make_async_copy(scale, got_scales.at[me], own_sem.at[7 + LIST_ROWS]),
    ]
    for copy in own:
        copy.start()
    for copy in own + copies:
        copy.wait()


def decode_kernel(got, got_scales, out, wide, scale):
    count, rows = got.shape[0], got.shape[1]
    for source in range(count):
        scale[source : source + 1, :] = got_scales[source]

    def widen(source, carry):
        at = pl.ds(source * (rows + 1), rows)
        wide[at, :] = got[source].astype(jnp.int32).astype(jnp.float32)
        return carry

    lax.fori_loop(0, count, widen, 0)
    factor = scale[...]
    for place in range(rows):
        slot, plane, half = place // 4, (place // 2) % 2, place % 2
        value = wide[pl.ds(place, count, stride=rows + 1), :]
        out[slot, plane, :, 128 * half : 128 * half + 128] = (value * jnp.abs(value)) * factor


def on_device(field, coefficient, slot_mode, couplings):
    slabs, count = lax.axis_size("slab"), lax.axis_size("mode")
    slots, planes_here, rows_all, columns = field.shape
    entries = couplings.shape[0]
    f32, bf16, i16, i32 = jnp.float32, jnp.bfloat16, jnp.int16, jnp.int32
    dma = pltpu.SemaphoreType.DMA
    halo = 4 * CHUNKS + 2
    places = pl.cdiv(entries, 1024) * 8

    got, got_scales = pl.pallas_call(
        lambda *refs: gather_kernel(slabs, count, *refs),
        out_shape=(shape_of((count, slots * 4, 128), i16), shape_of((count, 1, 128), f32)),
        in_specs=[HBM] * 4,
        out_specs=(VMEM,) * 2,
        scratch_shapes=[
            pltpu.SMEM(slot_mode.shape, i32),
            pltpu.VMEM(field.shape, bf16),
            pltpu.VMEM(coefficient.shape, f32),
            pltpu.VMEM((4, entries), i32),
            pltpu.VMEM((count * slots * 4, 128), f32),
            pltpu.VMEM((count, slots, 4, 128), bf16),
            pltpu.VMEM((count * slots, 4, 128), bf16),
            pltpu.VMEM((ROWS, 128), f32),
            pltpu.VMEM((2, ROWS // 2, 128), f32),
            pltpu.VMEM((8, 128), i32),
            pltpu.SMEM((8, 128), i32),
            pltpu.VMEM((ROWS, 128), bf16),
            pltpu.VMEM((2, ROWS // 2, 128), bf16),
            pltpu.VMEM((ROWS, 128), bf16),
            pltpu.VMEM((ROWS, 128), bf16),
            pltpu.VMEM((ROWS // 2, 128), bf16),
            pltpu.VMEM((ROWS // 2, 128), bf16),
            pltpu.VMEM((3, TERMS, 8, 128), f32),
            pltpu.VMEM((TERMS, 8, 128), f32),
            pltpu.VMEM((TERMS, 8, 128), f32),
            pltpu.VMEM((6 * TERMS, 8, 128), f32),
            pltpu.VMEM((ROWS, 128), f32),
            pltpu.VMEM((ROWS, 128), f32),
            pltpu.VMEM((ROWS, 128), f32),
            pltpu.VMEM((ROWS, 128), f32),
            pltpu.VMEM(((TERMS - 1) * HELD, 4, 128), f32),
            pltpu.VMEM((128 * LIST_ROWS + 8, 4, 128), f32),
        ]
        + [pltpu.VMEM((places, 128), i32)] * 4
        + [pltpu.VMEM((8, 128), i32)]
        + [pltpu.SMEM((places, 128), i32)] * 3
        + [
            pltpu.SMEM((8, 128), i32),
            pltpu.VMEM((ROWS, 128), f32),
            pltpu.VMEM((HELD, 4, 128), i32),
            pltpu.VMEM((count * slots * 4, 128), i32),
            pltpu.VMEM((count, slots * 4, 128), i16),
            pltpu.VMEM((1, 128), f32),
            dma((7,)),
            dma((8 + LIST_ROWS,)),
            dma((len(OFFSETS),)),
            dma((len(OFFSETS),)),
            dma((halo,)),
            dma((halo,)),
            dma((2, len(OFFSETS))),
            dma((2, len(OFFSETS))),
        ]
        + [pltpu.SMEM((1, 128), i32)] * LIST_ROWS,
        compiler_params=pltpu.CompilerParams(collective_id=0, has_side_effects=True, vmem_limit_bytes=48 * MIB),
        name="gather",
    )(*(pltpu.with_memory_space_constraint(value, pltpu.HBM) for value in (slot_mode, field, coefficient, couplings.T)))

    step = 16
    return pl.pallas_call(
        decode_kernel,
        out_shape=shape_of((slots, planes_here, rows_all, columns), f32),
        grid=(slots // step,),
        in_specs=[
            pl.BlockSpec((count, 4 * step, 128), lambda i: (0, i, 0)),
            pl.BlockSpec((count, 1, 128), lambda i: (0, 0, 0)),
        ],
        out_specs=pl.BlockSpec((step, planes_here, rows_all, columns), lambda i: (i, 0, 0, 0)),
        scratch_shapes=[pltpu.VMEM((count * (4 * step + 1), 128), f32), pltpu.VMEM((count, 128), f32)],
        compiler_params=pltpu.CompilerParams(vmem_limit_bytes=12 * MIB),
        name="decode",
    )(got, got_scales)


def solution(mesh):
    in_specs = (P("mode", "slab", None, None), P(None, "slab", None, None), P(), P())
    return jax.shard_map(
        on_device,
        mesh=mesh,
        in_specs=in_specs,
        out_specs=P("mode", "slab", None, None),
        check_vma=False,
    )
```

```python
import jax
import jax.numpy as jnp
from jax import lax
from jax.experimental import pallas as pl
from jax.experimental.pallas import tpu as pltpu
from jax.sharding import PartitionSpec as P

MODES = 495
HELD = 512
TERMS = 9
ROWS = 4 * HELD
CHUNKS = 9
USED = 496
LIST_ROWS = 21
SPREAD = 99
TOP = 32700.0
SIDE = 4
MESH = pl.DeviceIdType.MESH
VMEM = pl.BlockSpec(memory_space=pltpu.VMEM)
SMEM = pl.BlockSpec(memory_space=pltpu.SMEM)
HBM = pl.BlockSpec(memory_space=pltpu.HBM)
MIB = 1024 * 1024


def far_first():
    offsets = [(x, y, core) for x in range(SIDE) for y in range(SIDE) for core in range(2)]
    hops = lambda offset: min(offset[0], SIDE - offset[0]) + min(offset[1], SIDE - offset[1])
    return sorted(offsets[1:], key=hops, reverse=True)


OFFSETS = far_first()


def shape_of(shape, dtype):
    return jax.ShapeDtypeStruct(shape, dtype)


def moved(me, offset, sign=1):
    x, y, core = me // (2 * SIDE), (me // 2) % SIDE, me % 2
    x = lax.rem(x + (sign * offset[0]) % SIDE, SIDE)
    y = lax.rem(y + (sign * offset[1]) % SIDE, SIDE)
    return (x * SIDE + y) * 2 + lax.rem(core + offset[2], 2)


def rows_at(start, size):
    return pl.ds(pl.multiple_of(start, size), size)


def plane_neighbours(centre, plane, front):
    return (
        jnp.where(front, plane, pltpu.roll(centre, 2, 0)),
        jnp.where(front, pltpu.roll(centre, 6, 0), plane),
    )


def column_neighbours(centre, second, lane):
    zero = jnp.zeros_like(centre)
    low = pltpu.roll(centre, 1, 1)
    high = pltpu.roll(centre, 127, 1)
    return (
        jnp.where(lane == 0, jnp.where(second, pltpu.roll(low, 1, 0), zero), low),
        jnp.where(lane == 127, jnp.where(second, zero, pltpu.roll(high, 7, 0)), high),
    )


def gather_kernel(
    slabs, count, slot_mode_hbm, field_hbm, coefficient_hbm, couplings_hbm,
    got, got_scales,
    slot_mode, field, coefficient, couplings, turned, blocks, raw, wide, wide_planes, found, inverse,
    held, planes, row_low, row_high, plane_low, plane_high, near, coef_low, coef_high,
    faces, plane_rows, column_low, column_high, start, image, running,
    targets, words, ranks, order, firsts, target_list, word_list, rank_list, first_list,
    total, codes, picked, coded, scale,
    load_sem, own_sem, send_sem, recv_sem, halo_send, halo_recv, give_send, give_recv, *order_lists,
):
    slab, me = lax.axis_index("slab"), lax.axis_index("mode")
    slots = field.shape[0]
    above = (slab, lax.rem(me + 1, count))
    below = (slab, lax.rem(me + count - 1, count))
    right = (lax.rem(slab + 1, slabs), me)
    left = (lax.rem(slab + slabs - 1, slabs), me)
    sub = lax.broadcasted_iota(jnp.int32, (8, 128), 0)
    lane = lax.broadcasted_iota(jnp.int32, (8, 128), 1)
    front = lax.rem(sub, 4) < 2
    second = lax.rem(sub, 2) == 1
    has_left = (slab > 0).astype(jnp.float32)
    has_right = (slab < slabs - 1).astype(jnp.float32)
    mask_plane = jnp.where(front, has_left, has_right)
    mask_low = (me > 0).astype(jnp.float32)
    mask_high = (me < count - 1).astype(jnp.float32)

    piece = slots // 4
    loads = [
        pltpu.make_async_copy(field_hbm.at[pl.ds(piece * part, piece)], field.at[pl.ds(piece * part, piece)], load_sem.at[part])
        for part in range(4)
    ]
    others = [
        pltpu.make_async_copy(source, target, load_sem.at[4 + place])
        for place, (source, target) in enumerate(
            ((coefficient_hbm, coefficient), (slot_mode_hbm, slot_mode), (couplings_hbm, couplings))
        )
    ]
    for load in loads + others:
        load.start()
    barrier = pltpu.get_barrier_semaphore()
    for offset in OFFSETS:
        pl.semaphore_signal(barrier, inc=1, device_id=(slab, moved(me, offset)), device_id_type=MESH)
    for peer in (right, left):
        pl.semaphore_signal(barrier, inc=1, device_id=peer, device_id_type=MESH)

    def turn(slot, carry):
        for part in range(4):
            plane, half = part // 2, part % 2
            value = field[slot, plane, :, 128 * half : 128 * half + 128].astype(jnp.float32)
            turned[pl.ds(4 * slot + part, count, stride=4 * slots + 1), :] = value
        return carry

    for part, load in enumerate(loads):
        load.wait()
        lax.fori_loop(piece * part, piece * (part + 1), turn, 0)

    def narrow_block(row, carry):
        value = turned[pl.ds(row * (4 * slots + 1), 4 * slots), :]
        blocks[row] = value.reshape(slots, 4, 128).astype(jnp.bfloat16)
        return carry

    lax.fori_loop(0, count, narrow_block, 0)

    pl.semaphore_wait(barrier, len(OFFSETS) + 2)
    copies = []
    for place, offset in enumerate(OFFSETS):
        peer = moved(me, offset)
        copy = pltpu.make_async_remote_copy(
            src_ref=blocks.at[peer],
            dst_ref=raw.at[pl.ds(me * slots, slots)],
            send_sem=send_sem.at[place],
            recv_sem=recv_sem.at[place],
            device_id=(slab, peer),
            device_id_type=MESH,
        )
        copy.start()
        copies.append(copy)
    own = pltpu.make_async_copy(blocks.at[me], raw.at[pl.ds(me * slots, slots)], own_sem.at[0])
    own.start()
    for load in others:
        load.wait()
    for shift in range(3):
        row = jnp.clip(me + shift - 1, 0, count - 1)
        for term in range(TERMS):
            for part in range(4):
                plane, half = part // 2, part % 2
                tile = coefficient[term, plane, rows_at(row // 8 * 8, 8), 128 * half : 128 * half + 128]
                value = pltpu.roll(tile, lax.rem(8 - row % 8, 8), 0)[0:1]
                near[shift, term, part : part + 1, :] = value
                near[shift, term, part + 4 : part + 5, :] = value

    ids = sub * 128 + lane

    def moving(place, source, target):
        copy = pltpu.make_async_copy(source, target, own_sem.at[1 + place])
        copy.start()
        return copy

    entries = couplings.shape[1]
    whole, rest = entries // 128, entries % 128
    tiles = targets.shape[0] // 8
    for row in range(whole + 1):
        size = 128 if row < whole else rest
        if size:
            columns = slice(128 * row, 128 * row + size)
            targets[row : row + 1, 0:size] = couplings[0:1, columns]
            words[row : row + 1, 0:size] = (
                couplings[3:4, columns] * (8 * HELD) + (couplings[2:3, columns] - 1) * HELD + couplings[1:2, columns]
            )
    keys = []
    for tile in range(tiles):
        place = ids + 1024 * tile
        key = targets[8 * tile : 8 * tile + 8, :] * (8 * HELD) + place
        keys.append(jnp.where(place < entries, key, (1 << 30) + place))
        targets[8 * tile : 8 * tile + 8, :] = keys[-1]
        value = words[8 * tile : 8 * tile + 8, :]
        words[8 * tile : 8 * tile + 8, :] = jnp.where(place < entries, value, 0)
    def find(step, place):
        for part in range(8):
            slot = step * 8 + part
            place = jnp.where(ids == slot_mode[slot], slot, place)
        return place

    found[...] = lax.fori_loop(0, slots * count // 8, find, jnp.zeros((8, 128), jnp.int32))
    moves = [moving(0, targets, target_list), moving(1, words, word_list)]
    sent = []

    def send(place, source, target, peer):
        copy = pltpu.make_async_remote_copy(
            src_ref=source,
            dst_ref=target,
            send_sem=halo_send.at[place],
            recv_sem=halo_recv.at[place],
            device_id=peer,
            device_id_type=MESH,
        )
        copy.start()
        sent.append(copy)

    send(4 * CHUNKS, near.at[1], coef_low, right)
    send(4 * CHUNKS + 1, near.at[1], coef_high, left)
    own_coef = near.at[1]
    floors = (sub * SPREAD + lane + 1) * (8 * HELD)

    def rank(step, carry):
        for part in range(128):
            key = target_list[step, part]
            carry = tuple(
                jnp.where(value > key, count_of + 1, count_of) for value, count_of in zip(keys + [floors], carry)
            )
        return carry

    none = jnp.zeros((8, 128), jnp.int32)
    for copy in moves:
        copy.wait()
    counted = lax.fori_loop(0, LIST_ROWS, rank, (none,) * (tiles + 1))
    for tile in range(tiles):
        ranks[8 * tile : 8 * tile + 8, :] = counted[tile]
    firsts[...] = counted[tiles]
    moves = [moving(2, found, inverse)]
    for copy in sent:
        copy.wait()
    sent.clear()

    for term in range(TERMS):
        middle = own_coef[term]
        outer = jnp.where(front, pltpu.roll(coef_low[term], 6, 0), pltpu.roll(coef_high[term], 2, 0)) * mask_plane
        around = plane_neighbours(middle, outer, front) + column_neighbours(middle, second, lane)
        around = around + (near[0, term] * mask_low, near[2, term] * mask_high)
        for place, value in enumerate(around):
            faces[6 * term + place] = 0.5 * (middle + value)

    moves += [moving(3, ranks, rank_list), moving(4, firsts, first_list)]
    for copy in moves:
        copy.wait()

    def arrange(step, carry):
        for part in range(128):
            place, word = rank_list[step, part], word_list[step, part]
            carry = tuple(
                jnp.where(spot == place, word, value) for spot, value in zip(spots, carry)
            )
        return carry

    spots = []
    for tile in range(tiles):
        row = sub + 8 * tile
        spots.append(jnp.where(row < LIST_ROWS, lane * LIST_ROWS + row, -1))
    arranged = lax.fori_loop(0, LIST_ROWS, arrange, (none,) * tiles)
    for tile in range(tiles):
        order[8 * tile : 8 * tile + 8, :] = arranged[tile]
    own.wait()
    for copy in copies:
        copy.wait()

    ends = [0, 32] + [64 * chunk for chunk in range(1, CHUNKS - 1)] + [USED]

    def pick(low, high):
        for mode in range(low, high):
            value = raw[inverse[mode // 128, mode % 128]].astype(jnp.float32)
            wide[4 * mode : 4 * mode + 4, :] = value
            wide_planes[0, 2 * mode : 2 * mode + 2, :] = value[0:2]
            wide_planes[1, 2 * mode : 2 * mode + 2, :] = value[2:4]

    def narrow(step, carry):
        at = rows_at(step * 64, 64)
        held[at, :] = wide[at, :].astype(jnp.bfloat16)
        at = rows_at(step * 32, 32)
        planes[0, at, :] = wide_planes[0, at, :].astype(jnp.bfloat16)
        planes[1, at, :] = wide_planes[1, at, :].astype(jnp.bfloat16)
        return carry

    def send_chunk(chunk):
        low, size = ends[chunk], ends[chunk + 1] - ends[chunk]
        at, half = pl.ds(4 * low, 4 * size), pl.ds(2 * low, 2 * size)
        send(4 * chunk, held.at[at], row_low.at[at], above)
        send(4 * chunk + 1, held.at[at], row_high.at[at], below)
        send(4 * chunk + 2, planes.at[1, half], plane_low.at[half], right)
        send(4 * chunk + 3, planes.at[0, half], plane_high.at[half], left)

    def shift_columns(step, carry):
        value = wide[rows_at(step * 64, 64), :]
        around = [column_neighbours(value[8 * part : 8 * part + 8], second, lane) for part in range(8)]
        for part, (low, high) in enumerate(around):
            at = rows_at(step * 64 + 8 * part, 8)
            column_low[at, :] = low
            column_high[at, :] = high
        return carry

    for chunk in range(CHUNKS):
        pick(ends[chunk], ends[chunk + 1])
        lax.fori_loop(ends[chunk] // 16, ends[chunk + 1] // 16, narrow, 0)
        if chunk:
            send_chunk(chunk - 1)
    lax.fori_loop(0, 4, shift_columns, 0)
    send_chunk(CHUNKS - 1)
    lax.fori_loop(4, USED // 16, shift_columns, 0)

    ordered = [moving(5 + row, order.at[row : row + 1], order_lists[row]) for row in range(LIST_ROWS)]

    def interleave(step, carry):
        at = rows_at(step * 16, 16)
        low = plane_low[at, :].astype(jnp.float32) * has_left
        high = plane_high[at, :].astype(jnp.float32) * has_right
        for part in range(8):
            base = pl.multiple_of(step * 32 + 4 * part, 4)
            plane_rows[pl.ds(base, 2), :] = low[2 * part : 2 * part + 2]
            plane_rows[pl.ds(base + 2, 2), :] = high[2 * part : 2 * part + 2]
        return carry

    def stencil(step, carry):
        at = rows_at(step * 16, 16)
        low = row_low[at, :].astype(jnp.float32)
        high = row_high[at, :].astype(jnp.float32)
        halves = []
        for half in range(2):
            part = slice(8 * half, 8 * half + 8)
            base = pl.multiple_of(step * 16 + 8 * half, 8)
            at = pl.ds(base, 8)
            middle = wide[at, :]
            around = plane_neighbours(middle, plane_rows[at, :], front) + (column_low[at, :], column_high[at, :])
            around = around + (low[part] * mask_low, high[part] * mask_high)
            halves.append((base, 2 * half, [middle - value for value in around]))
        for term in range(TERMS):
            face = [faces[6 * term + place] for place in range(6)]
            for base, base_mode, drops in halves:
                total = face[0] * drops[0]
                for place in range(1, 6):
                    total = total + face[place] * drops[place]
                if term == 0:
                    start[pl.ds(base, 8), :] = total
                else:
                    at = (term - 1) * HELD + step * 4 + base_mode
                    image[pl.ds(at, 2)] = total.reshape(2, 4, 128)
        return carry

    for chunk in range(CHUNKS):
        for copy in sent[4 * chunk : 4 * chunk + 4]:
            copy.wait()
        lax.fori_loop(ends[chunk] // 8, ends[chunk + 1] // 8, interleave, 0)
        lax.fori_loop(ends[chunk] // 4, ends[chunk + 1] // 4, stencil, 0)

    def couple(step, carry):
        for lot in range(4):
            column = 4 * step + lot
            values = []
            for part in range(LIST_ROWS):
                word = order_lists[part][0, column]
                weight = lax.shift_right_arithmetic(jnp.full((4, 128), word, jnp.int32), 12).astype(jnp.float32)
                value = image[lax.bitwise_and(word, 8 * HELD - 1)]
                values.append((weight * 0.125) * value)
            for part in range(0, LIST_ROWS, 3):
                one, two, three = values[part : part + 3]
                at = column * LIST_ROWS + part
                running[at] = carry
                running[at + 1] = carry + one
                running[at + 2] = carry + (one + two)
                carry = carry + (one + two + three)
        return carry

    for copy in ordered:
        copy.wait()
    running[128 * LIST_ROWS] = lax.fori_loop(0, 32, couple, jnp.zeros((4, 128), jnp.float32))

    blank = jnp.zeros((4, 128), jnp.float32)
    below_it, top = blank, blank
    for mode in range(MODES):
        up_to = running[first_list[mode // SPREAD, mode % SPREAD]]
        value = start[4 * mode : 4 * mode + 4, :] + (up_to - below_it)
        total[4 * mode : 4 * mode + 4, :] = value
        below_it = up_to
        top = jnp.maximum(top, jnp.abs(value))
    total[4 * MODES : 4 * MODES + 4, :] = blank
    top = jnp.max(jnp.max(top, axis=0, keepdims=True), axis=1, keepdims=True)
    top = jnp.broadcast_to(top, (1, 128))
    scale[...] = top * (1.0 / (TOP * TOP))
    factor = TOP * lax.rsqrt(jnp.maximum(top, 1e-37))

    def encode(step, carry):
        value = total[rows_at(step * 64, 64), :]
        root = value * lax.rsqrt(jnp.maximum(jnp.abs(value), 1e-37))
        code = jnp.round(root * factor).astype(jnp.int32)
        codes[pl.ds(step * 16, 16)] = code.reshape(16, 4, 128)
        return carry

    lax.fori_loop(0, USED // 16, encode, 0)

    def prepare(group):
        for part in range(slots):
            slot = group * slots + part
            picked[rows_at(4 * slot, 4), :] = codes[slot_mode[slot]]
        for part in range(4):
            at = rows_at(group * 4 * slots + slots * part, slots)
            coded[group, slots * part : slots * (part + 1), :] = picked[at, :].astype(jnp.int16)

    copies = []

    def give(place, kind):
        peer = moved(me, OFFSETS[place])
        source, target = ((coded.at[peer], got), (scale, got_scales))[kind]
        copy = pltpu.make_async_remote_copy(
            src_ref=source,
            dst_ref=target.at[me],
            send_sem=give_send.at[kind, place],
            recv_sem=give_recv.at[kind, place],
            device_id=(slab, peer),
            device_id_type=MESH,
        )
        copy.start()
        copies.append(copy)

    prepare(moved(me, OFFSETS[0]))
    for place in range(1, len(OFFSETS)):
        prepare(moved(me, OFFSETS[place]))
        give(place - 1, 1)
        give(place - 1, 0)
    prepare(me)
    give(len(OFFSETS) - 1, 1)
    give(len(OFFSETS) - 1, 0)
    own = [
        pltpu.make_async_copy(coded.at[me], got.at[me], own_sem.at[6 + LIST_ROWS]),
        pltpu.make_async_copy(scale, got_scales.at[me], own_sem.at[7 + LIST_ROWS]),
    ]
    for copy in own:
        copy.start()
    for copy in own + copies:
        copy.wait()


def decode_kernel(got, got_scales, out, wide, scale):
    count, rows = got.shape[0], got.shape[1]
    for source in range(count):
        scale[source : source + 1, :] = got_scales[source]

    def widen(source, carry):
        at = pl.ds(source * (rows + 1), rows)
        wide[at, :] = got[source].astype(jnp.int32).astype(jnp.float32)
        return carry

    lax.fori_loop(0, count, widen, 0)
    factor = scale[...]
    for place in range(rows):
        slot, plane, half = place // 4, (place // 2) % 2, place % 2
        value = wide[pl.ds(place, count, stride=rows + 1), :]
        out[slot, plane, :, 128 * half : 128 * half + 128] = (value * jnp.abs(value)) * factor


def on_device(field, coefficient, slot_mode, couplings):
    slabs, count = lax.axis_size("slab"), lax.axis_size("mode")
    slots, planes_here, rows_all, columns = field.shape
    entries = couplings.shape[0]
    f32, bf16, i16, i32 = jnp.float32, jnp.bfloat16, jnp.int16, jnp.int32
    dma = pltpu.SemaphoreType.DMA
    halo = 4 * CHUNKS + 2
    places = pl.cdiv(entries, 1024) * 8

    got, got_scales = pl.pallas_call(
        lambda *refs: gather_kernel(slabs, count, *refs),
        out_shape=(shape_of((count, slots * 4, 128), i16), shape_of((count, 1, 128), f32)),
        in_specs=[HBM] * 4,
        out_specs=(VMEM,) * 2,
        scratch_shapes=[
            pltpu.SMEM(slot_mode.shape, i32),
            pltpu.VMEM(field.shape, bf16),
            pltpu.VMEM(coefficient.shape, f32),
            pltpu.VMEM((4, entries), i32),
            pltpu.VMEM((count * (slots * 4 + 1), 128), f32),
            pltpu.VMEM((count, slots, 4, 128), bf16),
            pltpu.VMEM((count * slots, 4, 128), bf16),
            pltpu.VMEM((ROWS, 128), f32),
            pltpu.VMEM((2, ROWS // 2, 128), f32),
            pltpu.VMEM((8, 128), i32),
            pltpu.SMEM((8, 128), i32),
            pltpu.VMEM((ROWS, 128), bf16),
            pltpu.VMEM((2, ROWS // 2, 128), bf16),
            pltpu.VMEM((ROWS, 128), bf16),
            pltpu.VMEM((ROWS, 128), bf16),
            pltpu.VMEM((ROWS // 2, 128), bf16),
            pltpu.VMEM((ROWS // 2, 128), bf16),
            pltpu.VMEM((3, TERMS, 8, 128), f32),
            pltpu.VMEM((TERMS, 8, 128), f32),
            pltpu.VMEM((TERMS, 8, 128), f32),
            pltpu.VMEM((6 * TERMS, 8, 128), f32),
            pltpu.VMEM((ROWS, 128), f32),
            pltpu.VMEM((ROWS, 128), f32),
            pltpu.VMEM((ROWS, 128), f32),
            pltpu.VMEM((ROWS, 128), f32),
            pltpu.VMEM(((TERMS - 1) * HELD, 4, 128), f32),
            pltpu.VMEM((128 * LIST_ROWS + 8, 4, 128), f32),
        ]
        + [pltpu.VMEM((places, 128), i32)] * 4
        + [pltpu.VMEM((8, 128), i32)]
        + [pltpu.SMEM((places, 128), i32)] * 3
        + [
            pltpu.SMEM((8, 128), i32),
            pltpu.VMEM((ROWS, 128), f32),
            pltpu.VMEM((HELD, 4, 128), i32),
            pltpu.VMEM((count * slots * 4, 128), i32),
            pltpu.VMEM((count, slots * 4, 128), i16),
            pltpu.VMEM((1, 128), f32),
            dma((7,)),
            dma((8 + LIST_ROWS,)),
            dma((len(OFFSETS),)),
            dma((len(OFFSETS),)),
            dma((halo,)),
            dma((halo,)),
            dma((2, len(OFFSETS))),
            dma((2, len(OFFSETS))),
        ]
        + [pltpu.SMEM((1, 128), i32)] * LIST_ROWS,
        compiler_params=pltpu.CompilerParams(collective_id=0, has_side_effects=True, vmem_limit_bytes=48 * MIB),
        name="gather",
    )(*(pltpu.with_memory_space_constraint(value, pltpu.HBM) for value in (slot_mode, field, coefficient, couplings.T)))

    step = 16
    return pl.pallas_call(
        decode_kernel,
        out_shape=shape_of((slots, planes_here, rows_all, columns), f32),
        grid=(slots // step,),
        in_specs=[
            pl.BlockSpec((count, 4 * step, 128), lambda i: (0, i, 0)),
            pl.BlockSpec((count, 1, 128), lambda i: (0, 0, 0)),
        ],
        out_specs=pl.BlockSpec((step, planes_here, rows_all, columns), lambda i: (i, 0, 0, 0)),
        scratch_shapes=[pltpu.VMEM((count * (4 * step + 1), 128), f32), pltpu.VMEM((count, 128), f32)],
        compiler_params=pltpu.CompilerParams(vmem_limit_bytes=12 * MIB),
        name="decode",
    )(got, got_scales)


def solution(mesh):
    in_specs = (P("mode", "slab", None, None), P(None, "slab", None, None), P(), P())
    return jax.shard_map(
        on_device,
        mesh=mesh,
        in_specs=in_specs,
        out_specs=P("mode", "slab", None, None),
        check_vma=False,
    )
```

```python
import jax
import jax.numpy as jnp
from jax import lax
from jax.experimental import pallas as pl
from jax.experimental.pallas import tpu as pltpu
from jax.sharding import PartitionSpec as P

MODES = 495
HELD = 512
TERMS = 9
ROWS = 4 * HELD
CHUNKS = 9
USED = 496
LIST_ROWS = 21
SPREAD = 99
TOP = 32700.0
SIDE = 4
MESH = pl.DeviceIdType.MESH
VMEM = pl.BlockSpec(memory_space=pltpu.VMEM)
SMEM = pl.BlockSpec(memory_space=pltpu.SMEM)
HBM = pl.BlockSpec(memory_space=pltpu.HBM)
MIB = 1024 * 1024


def far_first():
    offsets = [(x, y, core) for x in range(SIDE) for y in range(SIDE) for core in range(2)]
    hops = lambda offset: min(offset[0], SIDE - offset[0]) + min(offset[1], SIDE - offset[1])
    return sorted(offsets[1:], key=hops, reverse=True)


OFFSETS = far_first()


def shape_of(shape, dtype):
    return jax.ShapeDtypeStruct(shape, dtype)


def moved(me, offset, sign=1):
    x, y, core = me // (2 * SIDE), (me // 2) % SIDE, me % 2
    x = lax.rem(x + (sign * offset[0]) % SIDE, SIDE)
    y = lax.rem(y + (sign * offset[1]) % SIDE, SIDE)
    return (x * SIDE + y) * 2 + lax.rem(core + offset[2], 2)


def rows_at(start, size):
    return pl.ds(pl.multiple_of(start, size), size)


def plane_neighbours(centre, plane, front):
    return (
        jnp.where(front, plane, pltpu.roll(centre, 2, 0)),
        jnp.where(front, pltpu.roll(centre, 6, 0), plane),
    )


def column_neighbours(centre, second, lane):
    zero = jnp.zeros_like(centre)
    low = pltpu.roll(centre, 1, 1)
    high = pltpu.roll(centre, 127, 1)
    return (
        jnp.where(lane == 0, jnp.where(second, pltpu.roll(low, 1, 0), zero), low),
        jnp.where(lane == 127, jnp.where(second, zero, pltpu.roll(high, 7, 0)), high),
    )


def gather_kernel(
    slabs, count, slot_mode_hbm, field_hbm, coefficient_hbm, couplings_hbm,
    got, got_scales,
    slot_mode, field, coefficient, couplings, turned, blocks, raw, wide, wide_planes, found, inverse,
    held, planes, row_low, row_high, plane_low, plane_high, near, coef_low, coef_high,
    faces, plane_rows, column_low, column_high, start, image, running,
    targets, words, ranks, order, firsts, target_list, word_list, rank_list, first_list,
    total, codes, picked, coded, scale,
    load_sem, own_sem, send_sem, recv_sem, halo_send, halo_recv, give_send, give_recv, *order_lists,
):
    slab, me = lax.axis_index("slab"), lax.axis_index("mode")
    slots = field.shape[0]
    above = (slab, lax.rem(me + 1, count))
    below = (slab, lax.rem(me + count - 1, count))
    right = (lax.rem(slab + 1, slabs), me)
    left = (lax.rem(slab + slabs - 1, slabs), me)
    sub = lax.broadcasted_iota(jnp.int32, (8, 128), 0)
    lane = lax.broadcasted_iota(jnp.int32, (8, 128), 1)
    front = lax.rem(sub, 4) < 2
    second = lax.rem(sub, 2) == 1
    has_left = (slab > 0).astype(jnp.float32)
    has_right = (slab < slabs - 1).astype(jnp.float32)
    mask_plane = jnp.where(front, has_left, has_right)
    mask_low = (me > 0).astype(jnp.float32)
    mask_high = (me < count - 1).astype(jnp.float32)

    piece = slots // 4
    loads = [
        pltpu.make_async_copy(field_hbm.at[pl.ds(piece * part, piece)], field.at[pl.ds(piece * part, piece)], load_sem.at[part])
        for part in range(4)
    ]
    others = [
        pltpu.make_async_copy(source, target, load_sem.at[4 + place])
        for place, (source, target) in enumerate(
            ((coefficient_hbm, coefficient), (slot_mode_hbm, slot_mode), (couplings_hbm, couplings))
        )
    ]
    for load in loads + others:
        load.start()
    barrier = pltpu.get_barrier_semaphore()
    for offset in OFFSETS:
        pl.semaphore_signal(barrier, inc=1, device_id=(slab, moved(me, offset)), device_id_type=MESH)
    for peer in (right, left):
        pl.semaphore_signal(barrier, inc=1, device_id=peer, device_id_type=MESH)

    def turn(slot, carry):
        for part in range(4):
            plane, half = part // 2, part % 2
            value = field[slot, plane, :, 128 * half : 128 * half + 128].astype(jnp.float32)
            turned[pl.ds(4 * slot + part, count, stride=4 * slots + 1), :] = value
        return carry

    for part, load in enumerate(loads):
        load.wait()
        lax.fori_loop(piece * part, piece * (part + 1), turn, 0)

    def narrow_block(row, carry):
        value = turned[pl.ds(row * (4 * slots + 1), 4 * slots), :]
        blocks[row] = value.reshape(slots, 4, 128).astype(jnp.bfloat16)
        return carry

    lax.fori_loop(0, count, narrow_block, 0)

    pl.semaphore_wait(barrier, len(OFFSETS) + 2)
    copies = []
    for place, offset in enumerate(OFFSETS):
        peer = moved(me, offset)
        copy = pltpu.make_async_remote_copy(
            src_ref=blocks.at[peer],
            dst_ref=raw.at[pl.ds(me * slots, slots)],
            send_sem=send_sem.at[place],
            recv_sem=recv_sem.at[place],
            device_id=(slab, peer),
            device_id_type=MESH,
        )
        copy.start()
        copies.append(copy)
    own = pltpu.make_async_copy(blocks.at[me], raw.at[pl.ds(me * slots, slots)], own_sem.at[0])
    own.start()
    for load in others:
        load.wait()
    for shift in range(3):
        row = jnp.clip(me + shift - 1, 0, count - 1)
        for term in range(TERMS):
            for part in range(4):
                plane, half = part // 2, part % 2
                tile = coefficient[term, plane, rows_at(row // 8 * 8, 8), 128 * half : 128 * half + 128]
                value = pltpu.roll(tile, lax.rem(8 - row % 8, 8), 0)[0:1]
                near[shift, term, part : part + 1, :] = value
                near[shift, term, part + 4 : part + 5, :] = value

    ids = sub * 128 + lane

    def moving(place, source, target):
        copy = pltpu.make_async_copy(source, target, own_sem.at[1 + place])
        copy.start()
        return copy

    entries = couplings.shape[1]
    whole, rest = entries // 128, entries % 128
    tiles = targets.shape[0] // 8
    for row in range(whole + 1):
        size = 128 if row < whole else rest
        if size:
            columns = slice(128 * row, 128 * row + size)
            targets[row : row + 1, 0:size] = couplings[0:1, columns]
            words[row : row + 1, 0:size] = (
                couplings[3:4, columns] * (8 * HELD) + (couplings[2:3, columns] - 1) * HELD + couplings[1:2, columns]
            )
    keys = []
    for tile in range(tiles):
        place = ids + 1024 * tile
        key = targets[8 * tile : 8 * tile + 8, :] * (8 * HELD) + place
        keys.append(jnp.where(place < entries, key, (1 << 30) + place))
        targets[8 * tile : 8 * tile + 8, :] = keys[-1]
        value = words[8 * tile : 8 * tile + 8, :]
        words[8 * tile : 8 * tile + 8, :] = jnp.where(place < entries, value, 0)
    def find(step, place):
        for part in range(8):
            slot = step * 8 + part
            place = jnp.where(ids == slot_mode[slot], slot, place)
        return place

    found[...] = lax.fori_loop(0, slots * count // 8, find, jnp.zeros((8, 128), jnp.int32))
    moves = [moving(0, targets, target_list), moving(1, words, word_list)]
    sent = []

    def send(place, source, target, peer):
        copy = pltpu.make_async_remote_copy(
            src_ref=source,
            dst_ref=target,
            send_sem=halo_send.at[place],
            recv_sem=halo_recv.at[place],
            device_id=peer,
            device_id_type=MESH,
        )
        copy.start()
        sent.append(copy)

    send(4 * CHUNKS, near.at[1], coef_low, right)
    send(4 * CHUNKS + 1, near.at[1], coef_high, left)
    own_coef = near.at[1]
    floors = (sub * SPREAD + lane + 1) * (8 * HELD)

    def rank(step, carry):
        for part in range(128):
            key = target_list[step, part]
            carry = tuple(
                jnp.where(value > key, count_of + 1, count_of) for value, count_of in zip(keys + [floors], carry)
            )
        return carry

    none = jnp.zeros((8, 128), jnp.int32)
    for copy in moves:
        copy.wait()
    counted = lax.fori_loop(0, LIST_ROWS, rank, (none,) * (tiles + 1))
    for tile in range(tiles):
        ranks[8 * tile : 8 * tile + 8, :] = counted[tile]
    firsts[...] = counted[tiles]
    moves = [moving(2, found, inverse)]
    for copy in sent:
        copy.wait()
    sent.clear()

    for term in range(TERMS):
        middle = own_coef[term]
        outer = jnp.where(front, pltpu.roll(coef_low[term], 6, 0), pltpu.roll(coef_high[term], 2, 0)) * mask_plane
        around = plane_neighbours(middle, outer, front) + column_neighbours(middle, second, lane)
        around = around + (near[0, term] * mask_low, near[2, term] * mask_high)
        for place, value in enumerate(around):
            faces[6 * term + place] = 0.5 * (middle + value)

    moves += [moving(3, ranks, rank_list), moving(4, firsts, first_list)]
    for copy in moves:
        copy.wait()

    def arrange(step, carry):
        for part in range(128):
            place, word = rank_list[step, part], word_list[step, part]
            carry = tuple(
                jnp.where(spot == place, word, value) for spot, value in zip(spots, carry)
            )
        return carry

    spots = []
    for tile in range(tiles):
        row = sub + 8 * tile
        spots.append(jnp.where(row < LIST_ROWS, lane * LIST_ROWS + row, -1))
    arranged = lax.fori_loop(0, LIST_ROWS, arrange, (none,) * tiles)
    for tile in range(tiles):
        order[8 * tile : 8 * tile + 8, :] = arranged[tile]
    own.wait()
    for copy in copies:
        copy.wait()

    ends = [0, 32] + [64 * chunk for chunk in range(1, CHUNKS - 1)] + [USED]

    def pick(low, high):
        for mode in range(low, high):
            value = raw[inverse[mode // 128, mode % 128]].astype(jnp.float32)
            wide[4 * mode : 4 * mode + 4, :] = value
            wide_planes[0, 2 * mode : 2 * mode + 2, :] = value[0:2]
            wide_planes[1, 2 * mode : 2 * mode + 2, :] = value[2:4]

    def narrow(step, carry):
        at = rows_at(step * 64, 64)
        held[at, :] = wide[at, :].astype(jnp.bfloat16)
        at = rows_at(step * 32, 32)
        planes[0, at, :] = wide_planes[0, at, :].astype(jnp.bfloat16)
        planes[1, at, :] = wide_planes[1, at, :].astype(jnp.bfloat16)
        return carry

    def send_chunk(chunk):
        low, size = ends[chunk], ends[chunk + 1] - ends[chunk]
        at, half = pl.ds(4 * low, 4 * size), pl.ds(2 * low, 2 * size)
        send(4 * chunk, held.at[at], row_low.at[at], above)
        send(4 * chunk + 1, held.at[at], row_high.at[at], below)
        send(4 * chunk + 2, planes.at[1, half], plane_low.at[half], right)
        send(4 * chunk + 3, planes.at[0, half], plane_high.at[half], left)

    def shift_columns(step, carry):
        value = wide[rows_at(step * 64, 64), :]
        around = [column_neighbours(value[8 * part : 8 * part + 8], second, lane) for part in range(8)]
        for part, (low, high) in enumerate(around):
            at = rows_at(step * 64 + 8 * part, 8)
            column_low[at, :] = low
            column_high[at, :] = high
        return carry

    for chunk in range(CHUNKS):
        pick(ends[chunk], ends[chunk + 1])
        lax.fori_loop(ends[chunk] // 16, ends[chunk + 1] // 16, narrow, 0)
        if chunk:
            send_chunk(chunk - 1)
    lax.fori_loop(0, 4, shift_columns, 0)
    send_chunk(CHUNKS - 1)
    lax.fori_loop(4, USED // 16, shift_columns, 0)

    ordered = [moving(5 + row, order.at[row : row + 1], order_lists[row]) for row in range(LIST_ROWS)]

    def interleave(step, carry):
        at = rows_at(step * 16, 16)
        low = plane_low[at, :].astype(jnp.float32) * has_left
        high = plane_high[at, :].astype(jnp.float32) * has_right
        for part in range(8):
            base = pl.multiple_of(step * 32 + 4 * part, 4)
            plane_rows[pl.ds(base, 2), :] = low[2 * part : 2 * part + 2]
            plane_rows[pl.ds(base + 2, 2), :] = high[2 * part : 2 * part + 2]
        return carry

    def stencil(step, carry):
        at = rows_at(step * 16, 16)
        low = row_low[at, :].astype(jnp.float32)
        high = row_high[at, :].astype(jnp.float32)
        halves = []
        for half in range(2):
            part = slice(8 * half, 8 * half + 8)
            base = pl.multiple_of(step * 16 + 8 * half, 8)
            at = pl.ds(base, 8)
            middle = wide[at, :]
            around = plane_neighbours(middle, plane_rows[at, :], front) + (column_low[at, :], column_high[at, :])
            around = around + (low[part] * mask_low, high[part] * mask_high)
            halves.append((base, 2 * half, [middle - value for value in around]))
        for term in range(TERMS):
            face = [faces[6 * term + place] for place in range(6)]
            for base, base_mode, drops in halves:
                total = face[0] * drops[0]
                for place in range(1, 6):
                    total = total + face[place] * drops[place]
                if term == 0:
                    start[pl.ds(base, 8), :] = total
                else:
                    at = (term - 1) * HELD + step * 4 + base_mode
                    image[pl.ds(at, 2)] = total.reshape(2, 4, 128)
        return carry

    for chunk in range(CHUNKS):
        for copy in sent[4 * chunk : 4 * chunk + 4]:
            copy.wait()
        lax.fori_loop(ends[chunk] // 8, ends[chunk + 1] // 8, interleave, 0)
        lax.fori_loop(ends[chunk] // 4, ends[chunk + 1] // 4, stencil, 0)

    def couple(step, carry):
        for lot in range(4):
            column = 4 * step + lot
            values = []
            for part in range(LIST_ROWS):
                word = order_lists[part][0, column]
                weight = lax.shift_right_arithmetic(jnp.full((4, 128), word, jnp.int32), 12).astype(jnp.float32)
                value = image[lax.bitwise_and(word, 8 * HELD - 1)]
                values.append(weight * value)
            for part in range(0, LIST_ROWS, 3):
                one, two, three = values[part : part + 3]
                at = column * LIST_ROWS + part
                running[at] = carry
                running[at + 1] = carry + one
                running[at + 2] = carry + (one + two)
                carry = carry + (one + two + three)
        return carry

    for copy in ordered:
        copy.wait()
    running[128 * LIST_ROWS] = lax.fori_loop(0, 32, couple, jnp.zeros((4, 128), jnp.float32))

    blank = jnp.zeros((4, 128), jnp.float32)
    below_it, top = blank, blank
    for mode in range(MODES):
        up_to = running[first_list[mode // SPREAD, mode % SPREAD]]
        value = start[4 * mode : 4 * mode + 4, :] + 0.125 * (up_to - below_it)
        total[4 * mode : 4 * mode + 4, :] = value
        below_it = up_to
        top = jnp.maximum(top, jnp.abs(value))
    total[4 * MODES : 4 * MODES + 4, :] = blank
    top = jnp.max(jnp.max(top, axis=0, keepdims=True), axis=1, keepdims=True)
    top = jnp.broadcast_to(top, (1, 128))
    scale[...] = top * (1.0 / (TOP * TOP))
    factor = TOP * lax.rsqrt(jnp.maximum(top, 1e-37))

    def encode(step, carry):
        value = total[rows_at(step * 64, 64), :]
        root = value * lax.rsqrt(jnp.maximum(jnp.abs(value), 1e-37))
        code = jnp.round(root * factor).astype(jnp.int32)
        codes[pl.ds(step * 16, 16)] = code.reshape(16, 4, 128)
        return carry

    lax.fori_loop(0, USED // 16, encode, 0)

    def prepare(group):
        for part in range(slots):
            slot = group * slots + part
            picked[rows_at(4 * slot, 4), :] = codes[slot_mode[slot]]
        for part in range(4):
            at = rows_at(group * 4 * slots + slots * part, slots)
            coded[group, slots * part : slots * (part + 1), :] = picked[at, :].astype(jnp.int16)

    copies = []

    def give(place, kind):
        peer = moved(me, OFFSETS[place])
        source, target = ((coded.at[peer], got), (scale, got_scales))[kind]
        copy = pltpu.make_async_remote_copy(
            src_ref=source,
            dst_ref=target.at[me],
            send_sem=give_send.at[kind, place],
            recv_sem=give_recv.at[kind, place],
            device_id=(slab, peer),
            device_id_type=MESH,
        )
        copy.start()
        copies.append(copy)

    prepare(moved(me, OFFSETS[0]))
    for place in range(1, len(OFFSETS)):
        prepare(moved(me, OFFSETS[place]))
        give(place - 1, 1)
        give(place - 1, 0)
    prepare(me)
    give(len(OFFSETS) - 1, 1)
    give(len(OFFSETS) - 1, 0)
    own = [
        pltpu.make_async_copy(coded.at[me], got.at[me], own_sem.at[6 + LIST_ROWS]),
        pltpu.make_async_copy(scale, got_scales.at[me], own_sem.at[7 + LIST_ROWS]),
    ]
    for copy in own:
        copy.start()
    for copy in own + copies:
        copy.wait()


def decode_kernel(got, got_scales, out, wide, scale):
    count, rows = got.shape[0], got.shape[1]
    for source in range(count):
        scale[source : source + 1, :] = got_scales[source]

    def widen(source, carry):
        at = pl.ds(source * (rows + 1), rows)
        wide[at, :] = got[source].astype(jnp.int32).astype(jnp.float32)
        return carry

    lax.fori_loop(0, count, widen, 0)
    factor = scale[...]
    for place in range(rows):
        slot, plane, half = place // 4, (place // 2) % 2, place % 2
        value = wide[pl.ds(place, count, stride=rows + 1), :]
        out[slot, plane, :, 128 * half : 128 * half + 128] = (value * jnp.abs(value)) * factor


def on_device(field, coefficient, slot_mode, couplings):
    slabs, count = lax.axis_size("slab"), lax.axis_size("mode")
    slots, planes_here, rows_all, columns = field.shape
    entries = couplings.shape[0]
    f32, bf16, i16, i32 = jnp.float32, jnp.bfloat16, jnp.int16, jnp.int32
    dma = pltpu.SemaphoreType.DMA
    halo = 4 * CHUNKS + 2
    places = pl.cdiv(entries, 1024) * 8

    got, got_scales = pl.pallas_call(
        lambda *refs: gather_kernel(slabs, count, *refs),
        out_shape=(shape_of((count, slots * 4, 128), i16), shape_of((count, 1, 128), f32)),
        in_specs=[HBM] * 4,
        out_specs=(VMEM,) * 2,
        scratch_shapes=[
            pltpu.SMEM(slot_mode.shape, i32),
            pltpu.VMEM(field.shape, bf16),
            pltpu.VMEM(coefficient.shape, f32),
            pltpu.VMEM((4, entries), i32),
            pltpu.VMEM((count * (slots * 4 + 1), 128), f32),
            pltpu.VMEM((count, slots, 4, 128), bf16),
            pltpu.VMEM((count * slots, 4, 128), bf16),
            pltpu.VMEM((ROWS, 128), f32),
            pltpu.VMEM((2, ROWS // 2, 128), f32),
            pltpu.VMEM((8, 128), i32),
            pltpu.SMEM((8, 128), i32),
            pltpu.VMEM((ROWS, 128), bf16),
            pltpu.VMEM((2, ROWS // 2, 128), bf16),
            pltpu.VMEM((ROWS, 128), bf16),
            pltpu.VMEM((ROWS, 128), bf16),
            pltpu.VMEM((ROWS // 2, 128), bf16),
            pltpu.VMEM((ROWS // 2, 128), bf16),
            pltpu.VMEM((3, TERMS, 8, 128), f32),
            pltpu.VMEM((TERMS, 8, 128), f32),
            pltpu.VMEM((TERMS, 8, 128), f32),
            pltpu.VMEM((6 * TERMS, 8, 128), f32),
            pltpu.VMEM((ROWS, 128), f32),
            pltpu.VMEM((ROWS, 128), f32),
            pltpu.VMEM((ROWS, 128), f32),
            pltpu.VMEM((ROWS, 128), f32),
            pltpu.VMEM(((TERMS - 1) * HELD, 4, 128), f32),
            pltpu.VMEM((128 * LIST_ROWS + 8, 4, 128), f32),
        ]
        + [pltpu.VMEM((places, 128), i32)] * 4
        + [pltpu.VMEM((8, 128), i32)]
        + [pltpu.SMEM((places, 128), i32)] * 3
        + [
            pltpu.SMEM((8, 128), i32),
            pltpu.VMEM((ROWS, 128), f32),
            pltpu.VMEM((HELD, 4, 128), i32),
            pltpu.VMEM((count * slots * 4, 128), i32),
            pltpu.VMEM((count, slots * 4, 128), i16),
            pltpu.VMEM((1, 128), f32),
            dma((7,)),
            dma((8 + LIST_ROWS,)),
            dma((len(OFFSETS),)),
            dma((len(OFFSETS),)),
            dma((halo,)),
            dma((halo,)),
            dma((2, len(OFFSETS))),
            dma((2, len(OFFSETS))),
        ]
        + [pltpu.SMEM((1, 128), i32)] * LIST_ROWS,
        compiler_params=pltpu.CompilerParams(collective_id=0, has_side_effects=True, vmem_limit_bytes=48 * MIB),
        name="gather",
    )(*(pltpu.with_memory_space_constraint(value, pltpu.HBM) for value in (slot_mode, field, coefficient, couplings.T)))

    step = 16
    return pl.pallas_call(
        decode_kernel,
        out_shape=shape_of((slots, planes_here, rows_all, columns), f32),
        grid=(slots // step,),
        in_specs=[
            pl.BlockSpec((count, 4 * step, 128), lambda i: (0, i, 0)),
            pl.BlockSpec((count, 1, 128), lambda i: (0, 0, 0)),
        ],
        out_specs=pl.BlockSpec((step, planes_here, rows_all, columns), lambda i: (i, 0, 0, 0)),
        scratch_shapes=[pltpu.VMEM((count * (4 * step + 1), 128), f32), pltpu.VMEM((count, 128), f32)],
        compiler_params=pltpu.CompilerParams(vmem_limit_bytes=12 * MIB),
        name="decode",
    )(got, got_scales)


def solution(mesh):
    in_specs = (P("mode", "slab", None, None), P(None, "slab", None, None), P(), P())
    return jax.shard_map(
        on_device,
        mesh=mesh,
        in_specs=in_specs,
        out_specs=P("mode", "slab", None, None),
        check_vma=False,
    )
```
